256 devices in a mesh: xy: 64 (over z, y_hi, x), gz: 4 (over y_lo, core).
Axes of the slice: x: 4, y: 4 (y_hi: 2, y_lo: 2; y = y_hi * 2 + y_lo), z: 8, core: 2. Of those that a mesh axis runs over, the one named last changes fastest.
Arguments:
- gauge_links: float32 [4, 2, 3, 3, 6, 128, 1024], P(None, None, None, None, None, 'xy', 'gz'), may hold values from -2.4 to 2.4
- pattern: int32 [4, 4], replicated, may hold values from 0 to 1
- link_parity: int32 [4], replicated, may hold values from 0 to 1
- conv_weight: bfloat16 [81, 48, 64], replicated, may hold values from -0.09375 to 0.09375
- conv_bias: float32 [64], replicated, may hold values from -3 to 3
- head_weight: float32 [64, 4], replicated, may hold values from -0.75 to 0.75
- cotangent: float32 [4, 2, 128, 1024], P(None, None, 'xy', 'gz'), may hold values from -6 to 6
Outputs:
- coefficients: float32 [4, 2, 128, 1024], P(None, None, 'xy', 'gz')
- grad_conv_weight: float32 [81, 48, 64], replicated
- grad_conv_bias: float32 [64], replicated
- grad_head_weight: float32 [64, 4], replicated
The draws below stay inside these ranges and needn't reach their ends.
All inputs are finite; a program needn't handle non-finite values.
Results may differ from the reference program's by a relative error of at most 0.0059.
Values may be sent and summed in bfloat16 or wider, within the bound.
No kernel may reach another device: no remote copies, remote signals or barrier semaphores. Data moves between devices by JAX's collectives and lax.ppermute only.
A program may use at most 128 MiB of HBM per device.

```python
import math
import jax
import jax.numpy as jnp
from jax import lax

FEAT = 48
HID = 64
OFFS = 81
LY = 64
TS = 2
TL = 6
NX = 128
NZ = 16
ROWS = 1024


def with_ends(entries, key, least, top_value):
    longest = entries.shape.index(max(entries.shape))
    spots = []
    for shift in (0, 1):
        where = [jax.random.randint(jax.random.fold_in(key, axis), (), 0, length) for axis, length in enumerate(entries.shape)]
        where[longest] = (where[longest] + shift) % entries.shape[longest]
        spots.append(tuple(where))
    return entries.at[spots[0]].set(least).at[spots[1]].set(top_value)


def block_scale(stream_key, dims, shards, low, top_value):
    def one(dim, parts):
        heights = jax.random.uniform(jax.random.fold_in(jax.random.fold_in(stream_key, 6), dim), (parts,), jnp.float32, low / len(shards), top_value / len(shards))
        return jnp.repeat(jnp.exp(heights), dims[dim] // parts).reshape((-1,) + (1,) * (len(dims) - dim - 1))

    gain = one(*shards[0])
    for cut in shards[1:]:
        gain = gain * one(*cut)
    return gain


def scatter_about(key, extent, width, bound, cuts=(), kind=jnp.bfloat16):
    result = jax.random.normal(key, extent, jnp.float32) * width
    if len(cuts) > 0:
        result = block_scale(key, extent, cuts, -0.22, 0.18) * result
    return jnp.clip(result, min=-bound, max=bound).astype(kind)


def setup_inputs(seed: int = 0) -> dict:
    seeds = jax.random.split(jax.random.key(seed), 8)
    return {
        "gauge_links": scatter_about(seeds[0], (4, 2, 3, 3, TL, NX, NZ * LY), 0.4, 2.4, ((5, 64), (6, 4)), jnp.float32),
        "pattern": with_ends(jax.random.randint(seeds[1], (4, 4), 0, 2), jax.random.fold_in(seeds[1], 1), 0, 1).astype(jnp.int32),
        "link_parity": with_ends(jax.random.randint(seeds[2], (4,), 0, 2), jax.random.fold_in(seeds[2], 1), 0, 1).astype(jnp.int32),
        "conv_weight": scatter_about(seeds[3], (OFFS, FEAT, HID), (OFFS * FEAT) ** -0.5, 0.09375),
        "conv_bias": scatter_about(seeds[4], (HID,), 0.5, 3.0, (), jnp.float32),
        "head_weight": scatter_about(seeds[5], (HID, 4), HID ** -0.5, 0.75, (), jnp.float32),
        "cotangent": scatter_about(seeds[6], (4, TS, NX, NZ * LY), 1.0, 6.0, ((2, 64), (3, 4)), jnp.float32),
    }


plane_pairs = ((0, 1), (0, 2), (0, 3), (1, 2), (1, 3), (2, 3))

def complex_product(left_side, right_side):
    real_part = lax.optimization_barrier(jnp.sum(left_side[0][:, :, None] * right_side[0][None], axis=1)) - lax.optimization_barrier(jnp.sum(left_side[1][:, :, None] * right_side[1][None], axis=1))
    imag_part = lax.optimization_barrier(jnp.sum(left_side[0][:, :, None] * right_side[1][None], axis=1)) + lax.optimization_barrier(jnp.sum(left_side[1][:, :, None] * right_side[0][None], axis=1))
    return jnp.stack([real_part, imag_part])

def plaquettes(extended):
    time_span = extended.shape[4] - 1
    width_x = extended.shape[5] - 1
    width_z = extended.shape[6] - 1

    def at_site(direction):
        return extended[direction, :, :, :, :time_span, :width_x, :width_z, :]

    def one_ahead(direction, step_dir):
        if step_dir == 0:
            return extended[direction, :, :, :, :time_span, 1:, :width_z, :]
        if step_dir == 1:
            return jnp.roll(at_site(direction), -1, axis=6)
        if step_dir == 2:
            return extended[direction, :, :, :, :time_span, :width_x, 1:, :]
        return extended[direction, :, :, :, 1:, :width_x, :width_z, :]
    wilson_loops = []
    for dir_one, dir_two in plane_pairs:
        first_pair = complex_product(at_site(dir_one), one_ahead(dir_two, dir_one))
        second = complex_product(at_site(dir_two), one_ahead(dir_one, dir_two))
        real_part = lax.optimization_barrier(jnp.sum(first_pair[0] * second[0] + first_pair[1] * second[1], axis=(0, 1)))
        imag_part = lax.optimization_barrier(jnp.sum(first_pair[1] * second[0] - first_pair[0] * second[1], axis=(0, 1)))
        wilson_loops.append(real_part)
        wilson_loops.append(imag_part)
    return jnp.stack(wilson_loops)

def clover(wilson_loops, start_x, start_z, count_x, count_z, time_slab):
    leaves = []
    for plane_num, pair in enumerate(plane_pairs):
        for leaf_set in ((), (pair[0],), (pair[1],), pair):
            shift_x = -1 if 0 in leaf_set else 0
            shift_z = -1 if 2 in leaf_set else 0
            shift_t = -1 if 3 in leaf_set else 0
            leaf_piece = wilson_loops[2 * plane_num:2 * plane_num + 2, 1 + shift_t:1 + shift_t + time_slab + 2, start_x + shift_x:start_x + shift_x + count_x, start_z + shift_z:start_z + shift_z + count_z, :]
            if 1 in leaf_set:
                leaf_piece = jnp.roll(leaf_piece, 1, axis=4)
            leaves.append(leaf_piece)
    return jnp.concatenate(leaves).astype(jnp.bfloat16)

def stacked(feat_ext):
    return jnp.concatenate([jnp.roll(feat_ext, 1, axis=4), feat_ext, jnp.roll(feat_ext, -1, axis=4)])

def window(stacked_feats, offset, time_slab, count_x, count_z):
    step_x = offset // 9
    step_z = offset // 3 % 3
    step_t = offset % 3
    part_view = stacked_feats[:, step_t:step_t + time_slab, step_x:step_x + count_x, step_z:step_z + count_z, :]
    return part_view.reshape(stacked_feats.shape[0], -1)

def convolve(stacked_feats, kernel, conv_bias, time_slab, count_x, count_z):
    running = None
    for offset in range(27):
        term = lax.dot_general(kernel[offset], window(stacked_feats, offset, time_slab, count_x, count_z), (((0,), (0,)), ((), ())), preferred_element_type=jnp.float32)
        running = term if running is None else running + term
    return running + conv_bias[:, None]

def kernel_grad(stacked_feats, hidden_low, time_slab, count_x, count_z):
    parts_list = []
    for offset in range(27):
        parts_list.append(lax.dot_general(window(stacked_feats, offset, time_slab, count_x, count_z), hidden_low, (((1,), (1,)), ((), ())), preferred_element_type=jnp.float32))
    return jnp.stack(parts_list).reshape(81, 48, -1)

def link_mask(pattern, link_parity, time_pos, x_pos, z_pos, y_pos):
    summed = pattern[:, 0][:, None, None, None, None] * x_pos[None, None, :, None, None] + pattern[:, 1][:, None, None, None, None] * y_pos[None, None, None, None, :] + pattern[:, 2][:, None, None, None, None] * z_pos[None, None, None, :, None] + pattern[:, 3][:, None, None, None, None] * time_pos[None, :, None, None, None] + link_parity[:, None, None, None, None]
    return (summed % 2 == 0).astype(jnp.float32).reshape(4, -1)

def head_and_grads(hidden, active, head_weight, cotangent_rows):
    activation = jnp.tanh(hidden)
    coefficients = active * lax.dot_general(head_weight, activation, (((0,), (0,)), ((), ())), precision=lax.Precision.HIGHEST, preferred_element_type=jnp.float32)
    grad_scale = 1.0 / math.sqrt(ROWS)
    coef_grad = active * cotangent_rows * grad_scale
    act_grad = jnp.dot(head_weight, coef_grad, precision=lax.Precision.HIGHEST, preferred_element_type=jnp.float32)
    hidden_grad = act_grad * (1.0 - activation * activation)
    grad_bias = lax.optimization_barrier(jnp.sum(hidden_grad, axis=1))
    grad_head = lax.dot_general(activation, coef_grad, (((1,), (1,)), ((), ())), precision=lax.Precision.HIGHEST, preferred_element_type=jnp.float32)
    return (coefficients, hidden_grad.astype(jnp.bfloat16), grad_bias, grad_head)

def reference(gauge_links, pattern, link_parity, conv_weight, conv_bias, head_weight, cotangent):
    lattice = gauge_links.reshape(4, 2, 3, 3, TL, NX, NZ, LY)
    extended = jnp.pad(lattice, [(0, 0)] * 5 + [(0, 1), (0, 1), (0, 0)], mode='wrap')
    wilson_loops = plaquettes(extended)
    padded = jnp.pad(wilson_loops, [(0, 0), (0, 0), (1, 0), (1, 0), (0, 0)], mode='wrap')
    features = clover(padded, 1, 1, NX, NZ, TS)
    feat_ext = jnp.pad(features, [(0, 0), (0, 0), (1, 1), (1, 1), (0, 0)], mode='wrap')
    stacked_feats = stacked(feat_ext)
    kernel = conv_weight.reshape(27, 144, -1)
    hidden = convolve(stacked_feats, kernel, conv_bias, TS, NX, NZ)
    active = link_mask(pattern, link_parity, jnp.arange(TS, dtype=jnp.int32), jnp.arange(NX, dtype=jnp.int32), jnp.arange(NZ, dtype=jnp.int32), jnp.arange(LY, dtype=jnp.int32))
    coefficients, hidden_low, grad_bias, grad_head = head_and_grads(hidden, active, head_weight, cotangent.reshape(4, -1))
    grad_kernel = kernel_grad(stacked_feats, hidden_low, TS, NX, NZ)
    return (coefficients.reshape(4, TS, NX, NZ * LY), grad_kernel, grad_bias, grad_head)
```

```python
import math

import jax
import jax.numpy as jnp
from jax import lax
from jax.experimental import pallas as pl
from jax.experimental.pallas import tpu as pltpu
from jax.sharding import PartitionSpec as P

LY = 64
ROWS = 1024
F32 = jnp.float32
BF16 = jnp.bfloat16

plane_pairs = ((0, 1), (0, 2), (0, 3), (1, 2), (1, 3), (2, 3))
INTERPRET = False
PARAMS = pltpu.CompilerParams(vmem_limit_bytes=56 * 2**20)


def lanes(shape):
    return lax.broadcasted_iota(jnp.int32, shape, len(shape) - 1)


def shift_y(x, by):
    if by == 0:
        return x
    axis = x.ndim - 1
    inner = pltpu.roll(x, (-by) % 128, axis)
    wrapped = pltpu.roll(x, (64 - by) % 128, axis)
    y = lanes(x.shape) % LY
    crossed = (y >= LY - by) if by > 0 else (y < -by)
    return jnp.where(crossed, wrapped, inner)


def leaf_starts(pair, leaf):
    back = ((), (pair[0],), (pair[1],), pair)[leaf]
    return tuple(0 if d in back else 1 for d in range(4))


LEAVES = [
    (p, leaf) + leaf_starts(pair, leaf) for p, pair in enumerate(plane_pairs) for leaf in range(4)
]


def weights_body(w_ref, out_ref, sum_ref):
    sum_ref[...] = jnp.zeros_like(sum_ref)

    def step(k, carry):
        dx = lax.div(k, 9)
        dz = lax.rem(lax.div(k, 3), 3)
        dt = lax.rem(k, 3)
        for dy in range(3):
            block = w_ref[k * 3 + dy].astype(F32)
            for p, leaf, sx, sy, sz, st in LEAVES:
                at = (((dt + st) * 4 + dz + sz) * 4 + dx + sx) * 4 + dy + sy
                c = 8 * p + 2 * leaf
                sum_ref[at, 2 * p : 2 * p + 2, :] += block[c : c + 2]
        return carry

    lax.fori_loop(0, 27, step, 0)
    for g in range(16):
        full = sum_ref[g * 16 : (g + 1) * 16].reshape(256, 64)
        high = full.astype(BF16).astype(F32)
        both = jnp.concatenate([high, full - high], axis=1)
        out_ref[g] = both.T.astype(BF16)


def loops_body(l_ref, xh_ref, zh_ref, o0_ref, o1_ref, xs_ref, zs_ref, pq_ref):
    pq_ref[...] = jnp.zeros_like(pq_ref)

    def stage(c, carry):
        for tau in range(5):
            xs_ref[c, pl.ds(4 * tau + 1, 2, stride=2), :] = xh_ref[c, tau]
            zs_ref[c, 4 * tau + 2 : 4 * tau + 4, :] = zh_ref[c, tau]
        return carry

    lax.fori_loop(0, 54, stage, 0)
    row = lax.broadcasted_iota(jnp.int32, (8, 128), 0)
    odd_x = row % 2 == 1
    high_z = row % 4 >= 2
    upper = lanes((8, 128)) >= LY

    def comp(d, ri, i, j):
        return ((d * 2 + ri) * 3 + i) * 3 + j

    def at_site(d, k):
        return [
            [[l_ref[comp(d, ri, i, j), 8 * k : 8 * k + 8, :] for j in range(3)] for i in range(3)]
            for ri in range(2)
        ]

    def ahead(d, step, k):
        def one(ri, i, j):
            c = comp(d, ri, i, j)
            if step == 3:
                if k < 2:
                    return l_ref[c, 8 * k + 4 : 8 * k + 12, :]
                return pltpu.roll(l_ref[c, 16:24, :], 4, 0)
            own = l_ref[c, 8 * k : 8 * k + 8, :]
            if step == 0:
                return jnp.where(odd_x, xs_ref[c - 18, 8 * k : 8 * k + 8, :], pltpu.roll(own, 7, 0))
            if step == 1:
                return shift_y(own, 1)
            h = c if d < 2 else c - 18
            beyond = jnp.where(high_z, zs_ref[h, 8 * k : 8 * k + 8, :], pltpu.roll(own, 6, 0))
            return pltpu.roll(jnp.where(upper, own, beyond), LY, 1)

        return [[[one(ri, i, j) for j in range(3)] for i in range(3)] for ri in range(2)]

    def product(a, b, i, j):
        re = a[0][i][0] * b[0][0][j] - a[1][i][0] * b[1][0][j]
        im = a[0][i][0] * b[1][0][j] + a[1][i][0] * b[0][0][j]
        for m in (1, 2):
            re = re + a[0][i][m] * b[0][m][j] - a[1][i][m] * b[1][m][j]
            im = im + a[0][i][m] * b[1][m][j] + a[1][i][m] * b[0][m][j]
        return re, im

    for k in range(3):
        for p, (mu, nu) in enumerate(plane_pairs):
            u_mu = at_site(mu, k)
            u_nu = at_site(nu, k)
            nu_ahead = ahead(nu, mu, k)
            mu_ahead = ahead(mu, nu, k)
            re = im = None
            for i in range(3):
                for j in range(3):
                    r1, i1 = product(u_mu, nu_ahead, i, j)
                    r2, i2 = product(u_nu, mu_ahead, i, j)
                    re_term = r1 * r2 + i1 * i2
                    im_term = i1 * r2 - r1 * i2
                    re = re_term if re is None else re + re_term
                    im = im_term if im is None else im + im_term
            pq_ref[pl.ds(128 * k + 2 * p, 8, stride=16), :] = re
            pq_ref[pl.ds(128 * k + 2 * p + 1, 8, stride=16), :] = im
    for tau in range(5):
        for x in range(2):
            r = tau * 4 + x
            o0_ref[x, tau] = pq_ref[r * 16 : r * 16 + 16, :].astype(BF16)
            r = tau * 4 + 2 + x
            o1_ref[x, tau] = pq_ref[r * 16 : r * 16 + 16, :].astype(BF16)


def layer_body(
    pos_ref, pat_ref, par_ref, el_ref, e_ref, er_ref, w_ref, bias_ref, head_ref, cot_ref,
    coef_ref, g_ref, q_ref, first_ref,
):
    upper = lanes((16, 128)) >= LY

    def build(tau, carry):
        for xi in range(5):
            src, x = ((el_ref, 0), (el_ref, 1), (e_ref, 0), (e_ref, 1), (er_ref, 0))[xi]
            tiles = [src[i, x, tau].astype(F32) for i in range(4)]
            for zs in range(6):
                if zs % 2 == 0:
                    tile = tiles[zs // 2]
                else:
                    mixed = jnp.where(upper, tiles[zs // 2], tiles[zs // 2 + 1])
                    tile = pltpu.roll(mixed, LY, 1)
                for dy in range(4):
                    lo = xi * 64 + dy * 16
                    q_ref[tau * 6 + zs, lo : lo + 16, :] = shift_y(tile, dy - 2).astype(BF16)
        return carry

    lax.fori_loop(0, 5, build, 0)

    def columns(t, x, g):
        at = (t + g // 4) * 6 + g % 4
        rows = slice(x * 64, x * 64 + 256)
        return jnp.concatenate([q_ref[at, rows, :], q_ref[at + 2, rows, :]], axis=1)

    lane = lanes((1, 256))
    y_pos = lane % LY
    z_pos = pos_ref[1] + lane // LY
    bias_sum = jnp.zeros((64, 256), F32)
    head_sums = [jnp.zeros((64, 256), F32) for _ in range(4)]
    lows = {}
    for t in range(2):
        for x in range(2):
            acc = jnp.zeros((128, 256), F32)
            for g in range(16):
                acc = acc + jnp.dot(w_ref[g], columns(t, x, g), preferred_element_type=F32)
            hidden = acc[:64] + acc[64:] + bias_ref[...]
            act = jnp.tanh(hidden)
            act_grad = jnp.zeros((64, 256), F32)
            for mu in range(4):
                fixed = pat_ref[mu, 0] * (pos_ref[0] + x) + pat_ref[mu, 3] * t + par_ref[mu]
                summed = pat_ref[mu, 1] * y_pos + pat_ref[mu, 2] * z_pos + fixed
                active = ((summed & 1) == 0).astype(F32)
                weight = head_ref[:, mu : mu + 1]
                coef = active * jnp.sum(weight * act, axis=0, keepdims=True)
                coef_ref[mu, t, x : x + 1, :] = coef
                coef_grad = active * cot_ref[mu, t, x : x + 1, :] * (1.0 / math.sqrt(ROWS))
                act_grad = act_grad + weight * coef_grad
                head_sums[mu] = head_sums[mu] + act * coef_grad
            hidden_grad = act_grad * (1.0 - act * act)
            bias_sum = bias_sum + hidden_grad
            lows[t, x] = hidden_grad.astype(BF16)

    small = jnp.zeros((64, 128), F32)
    spot = lanes((64, 128))
    for i, total in enumerate(head_sums + [bias_sum]):
        small = jnp.where(spot == i, jnp.sum(total, axis=1, keepdims=True), small)
    small = small.T

    def grad(g):
        acc = jnp.zeros((256, 64), F32)
        for t in range(2):
            for x in range(2):
                acc = acc + lax.dot_general(
                    columns(t, x, g), lows[t, x], (((1,), (1,)), ((), ())),
                    preferred_element_type=F32,
                )
        return acc

    for j in range(8):
        pair = jnp.concatenate([grad(j), grad(j + 8)], axis=1)
        if j == 0:
            first_ref[...] = pair[:16]
            rounded = small.astype(BF16).astype(F32)
            for row, part in ((12, rounded), (8, small - rounded)):
                first_ref[row : row + 4, 0:64] = part[0:4]
                first_ref[row : row + 1, 64:128] = part[4:5]
            pair = jnp.concatenate([first_ref[...], pair[16:]], axis=0)
        g_ref[j * 16 : (j + 1) * 16] = pair.reshape(16, 16, 128).astype(BF16)


def total_body(me_ref, in_ref, out_ref, sum_ref):
    sum_ref[...] = jnp.sum(in_ref[...].astype(F32), axis=0)
    count = sum_ref.shape[0]

    @pl.when(me_ref[0] == 8 // count)
    def _():
        at = 8 % count
        small = sum_ref[at : at + 4] + sum_ref[at + 4 : at + 8]
        rounded = small.astype(BF16).astype(F32)
        sum_ref[at : at + 4] = small - rounded
        sum_ref[at + 4 : at + 8] = rounded

    out_ref[...] = jnp.broadcast_to(sum_ref[...].astype(BF16)[None], out_ref.shape)


def expand_body(g_ref, k_ref, b_ref, h_ref, full_ref):
    for j in range(8):
        both = g_ref[j * 16 : (j + 1) * 16].astype(F32)
        full_ref[j * 16 : (j + 1) * 16] = both[:, :, :64]
        full_ref[(j + 8) * 16 : (j + 9) * 16] = both[:, :, 64:]

    def step(k, carry):
        dx = lax.div(k, 9)
        dz = lax.rem(lax.div(k, 3), 3)
        dt = lax.rem(k, 3)
        for dy in range(3):
            for p, leaf, sx, sy, sz, st in LEAVES:
                at = (((dt + st) * 4 + dz + sz) * 4 + dx + sx) * 4 + dy + sy
                c = 8 * p + 2 * leaf
                k_ref[k * 3 + dy, c : c + 2, :] = full_ref[at, 2 * p : 2 * p + 2, :]
        return carry

    lax.fori_loop(0, 27, step, 0)
    small = g_ref[0].astype(F32)
    small = small[12:16] + small[8:12]
    b_ref[...] = small[0:1, 64:128]
    h_ref[...] = jnp.concatenate([small, small], axis=0).T[0:64, 0:4]


def call(body, outs, scratch, *args, smem=0, name):
    vmem = pl.BlockSpec(memory_space=pltpu.VMEM)
    specs = [pl.BlockSpec(memory_space=pltpu.SMEM)] * smem + [vmem] * (len(args) - smem)
    return pl.pallas_call(
        body,
        out_shape=outs,
        in_specs=specs,
        out_specs=jax.tree.map(lambda _: vmem, outs),
        scratch_shapes=scratch,
        compiler_params=PARAMS,
        interpret=INTERPRET,
        name=name,
    )(*args)


def shifted(x, axis, by):
    count = lax.axis_size(axis)
    return lax.ppermute(x, axis, [(i, (i + by) % count) for i in range(count)])


def per_device(gauge_links, pattern, link_parity, conv_weight, conv_bias, head_weight, cotangent):
    rows = gauge_links.reshape(72, 6, 2, 2, 128).transpose(0, 1, 3, 2, 4)
    next_x = shifted(rows[18:, :5, :, 0, :], "xy", -1)
    edge_z = jnp.concatenate([rows[:36, :5, 0], rows[54:, :5, 0]])
    next_z = shifted(edge_z, "gz", -1)
    shape = jax.ShapeDtypeStruct
    weights = call(
        weights_body, shape((16, 128, 256), BF16), [pltpu.VMEM((256, 16, 64), F32)], conv_weight,
        name="weights",
    )
    half = shape((2, 5, 16, 128), BF16)
    low_z, high_z = call(
        loops_body, (half, half),
        [pltpu.VMEM((54, 24, 128), F32), pltpu.VMEM((54, 24, 128), F32), pltpu.VMEM((384, 128), F32)],
        rows.reshape(72, 24, 128), next_x, next_z, name="loops",
    )
    before_z = shifted(high_z, "gz", 1)
    after_z = shifted(low_z, "gz", -1)
    block = jnp.stack([before_z, low_z, high_z, after_z])
    before_x = shifted(block, "xy", 1)
    after_x = shifted(block, "xy", -1)
    pos = jnp.stack([lax.axis_index("xy") * 2, lax.axis_index("gz") * 4]).astype(jnp.int32)
    coefficients, grads = call(
        layer_body, (shape((4, 2, 2, 256), F32), shape((128, 16, 128), BF16)),
        [pltpu.VMEM((30, 320, 128), BF16), pltpu.VMEM((16, 128), F32)],
        pos, pattern, link_parity, before_x, block, after_x, weights, conv_bias[:, None],
        head_weight, cotangent, smem=3, name="layer",
    )
    both = ("xy", "gz")
    count = lax.axis_size(both)
    chunks = grads.reshape(count, 2048 // count, 128)
    chunks = lax.all_to_all(chunks, both, 0, 0, tiled=True)
    me = lax.axis_index(both).reshape(1)
    chunks = call(
        total_body, shape(chunks.shape, BF16), [pltpu.VMEM(chunks.shape[1:], F32)], me, chunks,
        smem=1, name="total",
    )
    chunks = lax.all_to_all(chunks, both, 0, 0, tiled=True)
    grad_kernel, grad_bias, grad_head = call(
        expand_body, (shape((81, 48, 64), F32), shape((1, 64), F32), shape((64, 4), F32)),
        [pltpu.VMEM((256, 16, 64), F32)], chunks.reshape(128, 16, 128), name="expand",
    )
    return coefficients, grad_kernel, grad_bias.reshape(64), grad_head


def solution(mesh):
    return jax.shard_map(
        per_device,
        mesh=mesh,
        in_specs=(
            P(None, None, None, None, None, "xy", "gz"),
            P(),
            P(),
            P(),
            P(),
            P(),
            P(None, None, "xy", "gz"),
        ),
        out_specs=(P(None, None, "xy", "gz"), P(), P(), P()),
        check_vma=False,
    )
```

```python
import math

import jax
import jax.numpy as jnp
import numpy as np
from jax import lax
from jax.experimental import pallas as pl
from jax.experimental.pallas import tpu as pltpu
from jax.sharding import PartitionSpec as P

LY = 64
ROWS = 1024
F32 = jnp.float32
BF16 = jnp.bfloat16

plane_pairs = ((0, 1), (0, 2), (0, 3), (1, 2), (1, 3), (2, 3))
INTERPRET = False
PARAMS = pltpu.CompilerParams(vmem_limit_bytes=56 * 2**20)


def lanes(shape):
    return lax.broadcasted_iota(jnp.int32, shape, len(shape) - 1)


def shift_y(x, by):
    if by == 0:
        return x
    axis = x.ndim - 1
    inner = pltpu.roll(x, (-by) % 128, axis)
    wrapped = pltpu.roll(x, (64 - by) % 128, axis)
    y = lanes(x.shape) % LY
    crossed = (y >= LY - by) if by > 0 else (y < -by)
    return jnp.where(crossed, wrapped, inner)


def plane_tables():
    tiles, keep, spread = [], [], np.zeros((6, 144, 512), np.float32)
    for p, pair in enumerate(plane_pairs):
        spans = [range(0 if d in pair else 1, 4) for d in range(4)]
        tiles.append([(z, y) for z in spans[2] for y in spans[1]])
        kept = {}
        table = np.zeros((16 * len(tiles[p]), 256), np.float32)
        for i, (z, y) in enumerate(tiles[p]):
            for x in spans[0]:
                for t in spans[3]:
                    table[16 * i + 4 * x + t, len(kept)] = 1
                    kept[x, y, z, t] = len(kept)
        keep.append(table)
        for leaf, back in enumerate(((), (pair[0],), (pair[1],), pair)):
            sx, sy, sz, st = (0 if d in back else 1 for d in range(4))
            for k in range(81):
                dx, dz, dt, dy = k // 27, k // 9 % 3, k // 3 % 3, k % 3
                spread[p, kept[dx + sx, dy + sy, dz + sz, dt + st], leaf * 128 + k] = 1
    return tiles, keep, spread


TILES, KEEP, SPREAD = plane_tables()
SIZES = [16 * len(t) for t in TILES]
STARTS = [sum(SIZES[:p]) for p in range(6)]
NT = (((1,), (1,)), ((), ()))


def weights_body(w_ref, spread_ref, keep_ref, head_ref, bias_ref, out_ref, small_ref):
    for p in range(6):
        table = keep_ref[STARTS[p] : STARTS[p] + SIZES[p], :]
        for r in range(2):
            full = jnp.zeros((64, 144), F32)
            for leaf in range(4):
                full = full + lax.dot_general(
                    w_ref[8 * p + 2 * leaf + r], spread_ref[p, :, leaf * 128 : leaf * 128 + 81], NT,
                    preferred_element_type=F32,
                )
            high = full.astype(BF16)
            low = (full - high.astype(F32)).astype(BF16)
            both = jnp.concatenate([high, low], axis=0)
            out_ref[2 * p + r, :, 0 : SIZES[p]] = lax.dot_general(
                both, table[:, :144], NT, preferred_element_type=F32
            ).astype(BF16)
    small_ref[...] = jnp.concatenate([head_ref[...], bias_ref[...], jnp.zeros((3, 64), F32)], axis=0).T


def loops_body(l_ref, xh_ref, zh_ref, o0_ref, o1_ref, xs_ref, zs_ref, pq_ref, tile_ref):
    def stage(c, carry):
        for tau in range(5):
            xs_ref[c, pl.ds(4 * tau + 1, 2, stride=2), :] = xh_ref[c, tau]
            zs_ref[c, 4 * tau + 2 : 4 * tau + 4, :] = zh_ref[c, tau]
        return carry

    lax.fori_loop(0, 54, stage, 0)
    row = lax.broadcasted_iota(jnp.int32, (8, 128), 0)
    odd_x = row % 2 == 1
    high_z = row % 4 >= 2
    upper = lanes((8, 128)) >= LY

    def comp(d, ri, i, j):
        return ((d * 2 + ri) * 3 + i) * 3 + j

    def at_site(d, k):
        return [
            [[l_ref[comp(d, ri, i, j), 8 * k : 8 * k + 8, :] for j in range(3)] for i in range(3)]
            for ri in range(2)
        ]

    def ahead(d, step, k):
        def one(ri, i, j):
            c = comp(d, ri, i, j)
            if step == 3:
                if k < 2:
                    return l_ref[c, 8 * k + 4 : 8 * k + 12, :]
                return pltpu.roll(l_ref[c, 16:24, :], 4, 0)
            own = l_ref[c, 8 * k : 8 * k + 8, :]
            if step == 0:
                return jnp.where(odd_x, xs_ref[c - 18, 8 * k : 8 * k + 8, :], pltpu.roll(own, 7, 0))
            if step == 1:
                return shift_y(own, 1)
            h = c if d < 2 else c - 18
            beyond = jnp.where(high_z, zs_ref[h, 8 * k : 8 * k + 8, :], pltpu.roll(own, 6, 0))
            return pltpu.roll(jnp.where(upper, own, beyond), LY, 1)

        return [[[one(ri, i, j) for j in range(3)] for i in range(3)] for ri in range(2)]

    def product(a, b, i, j):
        re = a[0][i][0] * b[0][0][j] - a[1][i][0] * b[1][0][j]
        im = a[0][i][0] * b[1][0][j] + a[1][i][0] * b[0][0][j]
        for m in (1, 2):
            re = re + a[0][i][m] * b[0][m][j] - a[1][i][m] * b[1][m][j]
            im = im + a[0][i][m] * b[1][m][j] + a[1][i][m] * b[0][m][j]
        return re, im

    for k in range(3):
        for p, (mu, nu) in enumerate(plane_pairs):
            u_mu = at_site(mu, k)
            u_nu = at_site(nu, k)
            nu_ahead = ahead(nu, mu, k)
            mu_ahead = ahead(mu, nu, k)
            re = im = None
            for i in range(3):
                for j in range(3):
                    r1, i1 = product(u_mu, nu_ahead, i, j)
                    r2, i2 = product(u_nu, mu_ahead, i, j)
                    re_term = r1 * r2 + i1 * i2
                    im_term = i1 * r2 - r1 * i2
                    re = re_term if re is None else re + re_term
                    im = im_term if im is None else im + im_term
            pq_ref[2 * p, 8 * k : 8 * k + 8, :] = re
            pq_ref[2 * p + 1, 8 * k : 8 * k + 8, :] = im
    for c in range(12):
        for lb, o_ref in enumerate((o0_ref, o1_ref)):
            for t in range(2):
                for x in range(2):
                    tile_ref[c, lb, t * 8 + x * 4 : t * 8 + x * 4 + 4, :] = pq_ref[
                        c, pl.ds(4 * t + 2 * lb + x, 4, stride=4), :
                    ]
            o_ref[c] = tile_ref[c, lb].astype(BF16)


def layer_body(
    x0_ref, z0_ref, pat_ref, par_ref, el_ref, e_ref, er_ref, w_ref, small_ref, keep_ref, cot_ref,
    coef_ref, g_ref, a_ref, low_ref, rows_ref,
):
    first = lax.broadcasted_iota(jnp.int32, (8, 128), 0) < 4
    lane = lanes((8, 128))
    upper = lane >= LY

    def crossed(by):
        y = lane % LY
        return (y >= LY - by) if by > 0 else (y < -by)

    for p in range(6):
        offsets = sorted({y for _, y in TILES[p]})
        for r in range(2):
            c = 2 * p + r
            for t in range(2):
                part = slice(8 * t, 8 * t + 8)
                cols = []
                for i in range(4):
                    left, own, right = (ref[i, c].astype(F32)[part] for ref in (el_ref, e_ref, er_ref))
                    cols.append((
                        (left, own),
                        (
                            pltpu.roll(jnp.where(first, own, left), 4, 0),
                            pltpu.roll(jnp.where(first, right, own), 4, 0),
                        ),
                    ))
                for x in range(2):
                    for y in offsets:
                        by = y - 2
                        made = []
                        for h in range(2):
                            plain, other = [], []
                            for i in range(4):
                                v = cols[i][x][h]
                                near = v if by == 0 else pltpu.roll(v, (-by) % 128, 1)
                                far = pltpu.roll(v, (LY - by) % 128, 1)
                                if by == 0:
                                    plain.append(near)
                                    other.append(far)
                                else:
                                    plain.append(jnp.where(crossed(by), far, near))
                                    other.append(jnp.where(crossed(by), near, far))
                            made.append([
                                plain[z // 2] if z % 2 == 0 else jnp.where(upper, other[z // 2 + 1], other[z // 2])
                                for z in range(6)
                            ])
                        both = [jnp.concatenate([u, v], axis=0).astype(BF16) for u, v in zip(*made)]
                        for n, (z, y_at) in enumerate(TILES[p]):
                            if y_at == y:
                                for lb in range(2):
                                    col = (t * 4 + x * 2 + lb) * 128
                                    a_ref[c, 16 * n : 16 * n + 16, col : col + 128] = both[z + 2 * lb]

    lane = lanes((1, 256))
    y_pos = lane % LY
    z_pos = z0_ref[0] + lane // LY
    bias_sum = jnp.zeros((64, 256), F32)
    head_sums = [jnp.zeros((64, 256), F32) for _ in range(4)]
    for t in range(2):
        for x in range(2):
            cols = slice((t * 2 + x) * 256, (t * 2 + x) * 256 + 256)
            acc = jnp.zeros((128, 256), F32)
            for c in range(12):
                size = SIZES[c // 2]
                acc = acc + jnp.dot(
                    w_ref[c, :, 0:size], a_ref[c, 0:size, cols], preferred_element_type=F32
                )
            hidden = acc[:64] + acc[64:] + small_ref[:, 4:5]
            act = jnp.tanh(hidden)
            act_grad = jnp.zeros((64, 256), F32)
            for mu in range(4):
                fixed = pat_ref[mu, 0] * (x0_ref[0] + x) + pat_ref[mu, 3] * t + par_ref[mu]
                summed = pat_ref[mu, 1] * y_pos + pat_ref[mu, 2] * z_pos + fixed
                active = ((summed & 1) == 0).astype(F32)
                weight = small_ref[:, mu : mu + 1]
                coef = active * jnp.sum(weight * act, axis=0, keepdims=True)
                coef_ref[mu, t, x : x + 1, :] = coef
                coef_grad = active * cot_ref[mu, t, x : x + 1, :] * (1.0 / math.sqrt(ROWS))
                act_grad = act_grad + weight * coef_grad
                head_sums[mu] = head_sums[mu] + act * coef_grad
            hidden_grad = act_grad * (1.0 - act * act)
            bias_sum = bias_sum + hidden_grad
            low_ref[:, cols] = hidden_grad.astype(BF16)

    spot = lanes((64, 128))
    small = jnp.zeros((64, 128), F32)
    for i, total in enumerate(head_sums + [bias_sum]):
        value = jnp.sum(total, axis=1, keepdims=True)
        rounded = value.astype(BF16).astype(F32)
        small = jnp.where(spot == i, rounded, jnp.where(spot == i + 8, value - rounded, small))

    def put(j, value):
        rows_ref[pl.ds(j, 64, stride=16), :] = value

    ends = [jnp.zeros((64, 128), F32), jnp.zeros((64, 128), F32)]
    for c in range(12):
        start, size = STARTS[c // 2], SIZES[c // 2]
        grad = lax.dot_general(low_ref[...], a_ref[c, 0:size, :], NT, preferred_element_type=F32)
        kept = jnp.dot(grad.astype(BF16), keep_ref[start : start + size, :], preferred_element_type=F32)
        put(c, kept[:, :128])
        end = kept[:, 128:]
        ends[c // 8] = ends[c // 8] + (pltpu.roll(end, 16 * (c % 8), 1) if c % 8 else end)
    put(12, ends[0])
    put(13, ends[1])
    put(14, small)
    put(15, jnp.zeros((64, 128), F32))
    g_ref[...] = rows_ref[...].reshape(64, 16, 128).astype(BF16)


def total_body(me_ref, in_ref, out_ref):
    total = jnp.sum(in_ref[...].astype(F32), axis=0)
    row = me_ref[0] * total.shape[0] + lax.broadcasted_iota(jnp.int32, total.shape, 0)
    lane = lanes(total.shape)
    whole = jnp.where(lane < 8, total + pltpu.roll(total, 120, 1), 0.0)
    rounded = whole.astype(BF16).astype(F32)
    rest = pltpu.roll(whole - rounded, 8, 1)
    total = jnp.where(row % 16 == 14, jnp.where(lane < 8, rounded, rest), total)
    out_ref[...] = jnp.broadcast_to(total.astype(BF16)[None], out_ref.shape)


def expand_body(g_ref, spread_ref, k_ref, b_ref, h_ref, rows_ref):
    rows_ref[...] = g_ref[...].astype(F32).reshape(1024, 128)

    def get(j):
        return rows_ref[pl.ds(j, 64, stride=16), :]

    ends = [get(12), get(13)]
    for c in range(12):
        p, r = c // 2, c % 2
        end = ends[c // 8]
        end = pltpu.roll(end, 128 - 16 * (c % 8), 1) if c % 8 else end
        kept = jnp.concatenate([get(c), end[:, :16]], axis=1).astype(BF16)
        full = jnp.dot(kept, spread_ref[p], preferred_element_type=F32)
        for leaf in range(4):
            k_ref[8 * p + 2 * leaf + r] = full[:, leaf * 128 : leaf * 128 + 81]
    small = get(14)
    small = (small + pltpu.roll(small, 120, 1)).T
    h_ref[...] = small[0:4]
    b_ref[...] = small[4:5]


def call(body, outs, scratch, *args, smem=0, name):
    vmem = pl.BlockSpec(memory_space=pltpu.VMEM)
    specs = [pl.BlockSpec(memory_space=pltpu.SMEM)] * smem + [vmem] * (len(args) - smem)
    return pl.pallas_call(
        body,
        out_shape=outs,
        in_specs=specs,
        out_specs=jax.tree.map(lambda _: vmem, outs),
        scratch_shapes=scratch,
        compiler_params=PARAMS,
        interpret=INTERPRET,
        name=name,
    )(*args)


def shifted(x, axis, by):
    count = lax.axis_size(axis)
    return lax.ppermute(x, axis, [(i, (i + by) % count) for i in range(count)])


def per_device(gauge_links, pattern, link_parity, conv_weight, conv_bias, head_weight, cotangent):
    rows = gauge_links.reshape(72, 6, 2, 2, 128).transpose(0, 1, 3, 2, 4)
    next_x = shifted(rows[18:, :5, :, 0, :], "xy", -1)
    edge_z = jnp.concatenate([rows[:36, :5, 0], rows[54:, :5, 0]])
    next_z = shifted(edge_z, "gz", -1)
    shape = jax.ShapeDtypeStruct
    keep = jnp.asarray(np.concatenate(KEEP), BF16)
    spread = jnp.asarray(SPREAD, BF16)
    weights, small = call(
        weights_body, (shape((12, 128, 256), BF16), shape((64, 8), F32)), [],
        conv_weight.transpose(1, 2, 0), spread, keep, head_weight.T, conv_bias[None], name="weights",
    )
    half = shape((12, 16, 128), BF16)
    halo = pltpu.VMEM((54, 24, 128), F32)
    low_z, high_z = call(
        loops_body, (half, half),
        [halo, halo, pltpu.VMEM((12, 24, 128), F32), pltpu.VMEM((12, 2, 16, 128), F32)],
        rows.reshape(72, 24, 128), next_x, next_z, name="loops",
    )
    before_z = shifted(high_z, "gz", 1)
    after_z = shifted(low_z, "gz", -1)
    block = jnp.stack([before_z, low_z, high_z, after_z])
    before_x = shifted(block, "xy", 1)
    after_x = shifted(block, "xy", -1)
    x_first = (lax.axis_index("xy") * 2).reshape(1)
    z_first = (lax.axis_index("gz") * 4).reshape(1)
    coefficients, grads = call(
        layer_body, (shape((4, 2, 2, 256), F32), shape((64, 16, 128), BF16)),
        [pltpu.VMEM((12, 256, 1024), BF16), pltpu.VMEM((64, 1024), BF16), pltpu.VMEM((1024, 128), F32)],
        x_first, z_first, pattern, link_parity, before_x, block, after_x, weights, small, keep,
        cotangent, smem=4, name="layer",
    )
    both = ("xy", "gz")
    count = lax.axis_size(both)
    chunks = grads.reshape(count, 1024 // count, 128)
    chunks = lax.all_to_all(chunks, both, 0, 0, tiled=True)
    me = lax.axis_index(both).reshape(1)
    chunks = call(total_body, shape(chunks.shape, BF16), [], me, chunks, smem=1, name="total")
    chunks = lax.all_to_all(chunks, both, 0, 0, tiled=True)
    grad_kernel, grad_bias, grad_head = call(
        expand_body, (shape((48, 64, 81), F32), shape((1, 64), F32), shape((4, 64), F32)),
        [pltpu.VMEM((1024, 128), F32)], chunks.reshape(64, 16, 128), spread, name="expand",
    )
    return coefficients, grad_kernel.transpose(2, 0, 1), grad_bias.reshape(64), grad_head.T


def solution(mesh):
    return jax.shard_map(
        per_device,
        mesh=mesh,
        in_specs=(
            P(None, None, None, None, None, "xy", "gz"),
            P(),
            P(),
            P(),
            P(),
            P(),
            P(None, None, "xy", "gz"),
        ),
        out_specs=(P(None, None, "xy", "gz"), P(), P(), P()),
        check_vma=False,
    )
```

```python
import functools
import math

import jax
import jax.numpy as jnp
import numpy as np
from jax import lax
from jax.experimental import pallas as pl
from jax.experimental.pallas import tpu as pltpu
from jax.sharding import PartitionSpec as P

LY = 64
ROWS = 1024
F32 = jnp.float32
BF16 = jnp.bfloat16

plane_pairs = ((0, 1), (0, 2), (0, 3), (1, 2), (1, 3), (2, 3))
INTERPRET = False
PARAMS = pltpu.CompilerParams(vmem_limit_bytes=56 * 2**20)


def lanes(shape):
    return lax.broadcasted_iota(jnp.int32, shape, len(shape) - 1)


def shift_y(x, by):
    if by == 0:
        return x
    axis = x.ndim - 1
    inner = pltpu.roll(x, (-by) % 128, axis)
    wrapped = pltpu.roll(x, (64 - by) % 128, axis)
    y = lanes(x.shape) % LY
    crossed = (y >= LY - by) if by > 0 else (y < -by)
    return jnp.where(crossed, wrapped, inner)


def plane_tables():
    tiles, keep, spread = [], [], np.zeros((6, 144, 512), np.float32)
    for p, pair in enumerate(plane_pairs):
        spans = [range(0 if d in pair else 1, 4) for d in range(4)]
        tiles.append([(z, y) for z in spans[2] for y in spans[1]])
        kept = {}
        table = np.zeros((16 * len(tiles[p]), 256), np.float32)
        for i, (z, y) in enumerate(tiles[p]):
            for x in spans[0]:
                for t in spans[3]:
                    table[16 * i + 4 * x + t, len(kept)] = 1
                    kept[x, y, z, t] = len(kept)
        keep.append(table)
        for leaf, back in enumerate(((), (pair[0],), (pair[1],), pair)):
            sx, sy, sz, st = (0 if d in back else 1 for d in range(4))
            for k in range(81):
                dx, dz, dt, dy = k // 27, k // 9 % 3, k // 3 % 3, k % 3
                spread[p, kept[dx + sx, dy + sy, dz + sz, dt + st], leaf * 128 + k] = 1
    return tiles, keep, spread


TILES, KEEP, SPREAD = plane_tables()
SIZES = [16 * len(t) for t in TILES]
STARTS = [sum(SIZES[:p]) for p in range(6)]
NT = (((1,), (1,)), ((), ()))


def weights_body(planes, w_ref, spread_ref, keep_ref, head_ref, bias_ref, out_ref, small_ref):
    for p in planes:
        table = keep_ref[STARTS[p] : STARTS[p] + SIZES[p], :]
        for r in range(2):
            full = jnp.zeros((64, 144), F32)
            for leaf in range(4):
                full = full + lax.dot_general(
                    w_ref[8 * p + 2 * leaf + r], spread_ref[p, :, leaf * 128 : leaf * 128 + 81], NT,
                    preferred_element_type=F32,
                )
            high = full.astype(BF16)
            low = (full - high.astype(F32)).astype(BF16)
            both = jnp.concatenate([high, low], axis=0)
            out_ref[2 * (p - planes[0]) + r, :, 0 : SIZES[p]] = lax.dot_general(
                both, table[:, :144], NT, preferred_element_type=F32
            ).astype(BF16)
    small_ref[...] = jnp.concatenate([head_ref[...], bias_ref[...], jnp.zeros((3, 64), F32)], axis=0).T


def run(copies):
    for copy in copies:
        copy.start()
    for copy in copies:
        copy.wait()


def send_body(l_ref, x_ref, z_ref, sems):
    z_part = l_ref.at[:, :, :, :, 0:5, :, 0:128]
    run([
        pltpu.make_async_copy(l_ref.at[1:4, :, :, :, 0:5, 0:1, :], x_ref, sems.at[0]),
        pltpu.make_async_copy(z_part.at[0:2], z_ref.at[0:2], sems.at[1]),
        pltpu.make_async_copy(z_part.at[3:4], z_ref.at[2:3], sems.at[2]),
    ])


def loops_body(
    links_ref, x_any, z_any, o0_ref, o1_ref, l_ref, xh_ref, zh_ref, xs_ref, zs_ref, pq_ref, tile_ref, sems
):
    copies = [
        pltpu.make_async_copy(x_any, xh_ref, sems.at[12]),
        pltpu.make_async_copy(z_any, zh_ref, sems.at[13]),
    ]
    for tau in range(6):
        for lb in range(2):
            at = tau * 4 + lb * 2
            copies.append(
                pltpu.make_async_copy(
                    links_ref.at[:, :, :, :, tau, :, lb * 128 : lb * 128 + 128],
                    l_ref.at[:, :, :, :, at : at + 2, :],
                    sems.at[tau * 2 + lb],
                )
            )
    run(copies)

    def stage(c, carry):
        d, ri = lax.div(c, 6), lax.rem(c, 6)
        ri, i = lax.div(ri, 3), lax.rem(ri, 3)
        for j in range(3):
            for tau in range(5):
                for lb in range(2):
                    row = 4 * tau + 2 * lb + 1
                    xs_ref[d, ri, i, j, row : row + 1, :] = xh_ref[
                        d, ri, i, j, tau, :, lb * 128 : lb * 128 + 128
                    ]
                zs_ref[d, ri, i, j, 4 * tau + 2 : 4 * tau + 4, :] = zh_ref[d, ri, i, j, tau]
        return carry

    lax.fori_loop(0, 18, stage, 0)
    row = lax.broadcasted_iota(jnp.int32, (8, 128), 0)
    odd_x = row % 2 == 1
    high_z = row % 4 >= 2
    upper = lanes((8, 128)) >= LY

    def at_site(d, k):
        part = slice(8 * k, 8 * k + 8)
        return [
            [[l_ref[d, ri, i, j, part, :] for j in range(3)] for i in range(3)] for ri in range(2)
        ]

    def ahead(d, step, k):
        part = slice(8 * k, 8 * k + 8)

        def one(ri, i, j):
            if step == 3:
                if k < 2:
                    return l_ref[d, ri, i, j, 8 * k + 4 : 8 * k + 12, :]
                return pltpu.roll(l_ref[d, ri, i, j, 16:24, :], 4, 0)
            own = l_ref[d, ri, i, j, part, :]
            if step == 0:
                return jnp.where(odd_x, xs_ref[d - 1, ri, i, j, part, :], pltpu.roll(own, 7, 0))
            if step == 1:
                return shift_y(own, 1)
            edge = zs_ref[min(d, 2), ri, i, j, part, :]
            beyond = jnp.where(high_z, edge, pltpu.roll(own, 6, 0))
            return pltpu.roll(jnp.where(upper, own, beyond), LY, 1)

        return [[[one(ri, i, j) for j in range(3)] for i in range(3)] for ri in range(2)]

    def product(a, b, i, j):
        re = a[0][i][0] * b[0][0][j] - a[1][i][0] * b[1][0][j]
        im = a[0][i][0] * b[1][0][j] + a[1][i][0] * b[0][0][j]
        for m in (1, 2):
            re = re + a[0][i][m] * b[0][m][j] - a[1][i][m] * b[1][m][j]
            im = im + a[0][i][m] * b[1][m][j] + a[1][i][m] * b[0][m][j]
        return re, im

    for k in range(3):
        for p, (mu, nu) in enumerate(plane_pairs):
            u_mu = at_site(mu, k)
            u_nu = at_site(nu, k)
            nu_ahead = ahead(nu, mu, k)
            mu_ahead = ahead(mu, nu, k)
            re = im = None
            for i in range(3):
                for j in range(3):
                    r1, i1 = product(u_mu, nu_ahead, i, j)
                    r2, i2 = product(u_nu, mu_ahead, i, j)
                    re_term = r1 * r2 + i1 * i2
                    im_term = i1 * r2 - r1 * i2
                    re = re_term if re is None else re + re_term
                    im = im_term if im is None else im + im_term
            pq_ref[2 * p, 8 * k : 8 * k + 8, :] = re
            pq_ref[2 * p + 1, 8 * k : 8 * k + 8, :] = im
    for c in range(12):
        for lb, o_ref in enumerate((o0_ref, o1_ref)):
            for t in range(2):
                for x in range(2):
                    tile_ref[c, lb, t * 8 + x * 4 : t * 8 + x * 4 + 4, :] = pq_ref[
                        c, pl.ds(4 * t + 2 * lb + x, 4, stride=4), :
                    ]
            o_ref[c] = tile_ref[c, lb].astype(BF16)


def layer_body(
    x0_ref, z0_ref, pat_ref, par_ref, el_any, e_any, er_any, w0_any, w1_any, keep_any, small_ref, cot_ref,
    coef_ref, g_ref, el_ref, e_ref, er_ref, w_ref, keep_ref, a_ref, low_ref, rows_ref, sems,
):
    halo = [
        pltpu.make_async_copy(src, dst, sems.at[i])
        for i, (src, dst) in enumerate(((el_any, el_ref), (e_any, e_ref), (er_any, er_ref)))
    ]
    later = [
        pltpu.make_async_copy(w0_any, w_ref.at[0:6], sems.at[3]),
        pltpu.make_async_copy(w1_any, w_ref.at[6:12], sems.at[4]),
        pltpu.make_async_copy(keep_any, keep_ref, sems.at[5]),
    ]
    for copy in halo + later:
        copy.start()
    for copy in halo:
        copy.wait()
    first = lax.broadcasted_iota(jnp.int32, (8, 128), 0) < 4
    lane = lanes((8, 128))
    upper = lane >= LY

    def crossed(by):
        y = lane % LY
        return (y >= LY - by) if by > 0 else (y < -by)

    for p in range(6):
        offsets = sorted({y for _, y in TILES[p]})
        for r in range(2):
            c = 2 * p + r
            for t in range(2):
                part = slice(8 * t, 8 * t + 8)
                cols = []
                for i in range(4):
                    left, own, right = (ref[i, c].astype(F32)[part] for ref in (el_ref, e_ref, er_ref))
                    cols.append((
                        (left, own),
                        (
                            pltpu.roll(jnp.where(first, own, left), 4, 0),
                            pltpu.roll(jnp.where(first, right, own), 4, 0),
                        ),
                    ))
                for x in range(2):
                    for y in offsets:
                        by = y - 2
                        made = []
                        for h in range(2):
                            plain, other = [], []
                            for i in range(4):
                                v = cols[i][x][h]
                                near = v if by == 0 else pltpu.roll(v, (-by) % 128, 1)
                                far = pltpu.roll(v, (LY - by) % 128, 1)
                                if by == 0:
                                    plain.append(near)
                                    other.append(far)
                                else:
                                    plain.append(jnp.where(crossed(by), far, near))
                                    other.append(jnp.where(crossed(by), near, far))
                            made.append([
                                plain[z // 2] if z % 2 == 0 else jnp.where(upper, other[z // 2 + 1], other[z // 2])
                                for z in range(6)
                            ])
                        both = [jnp.concatenate([u, v], axis=0).astype(BF16) for u, v in zip(*made)]
                        for n, (z, y_at) in enumerate(TILES[p]):
                            if y_at == y:
                                for lb in range(2):
                                    col = (t * 4 + x * 2 + lb) * 128
                                    a_ref[c, 16 * n : 16 * n + 16, col : col + 128] = both[z + 2 * lb]

    for copy in later:
        copy.wait()
    lane = lanes((1, 256))
    y_pos = lane % LY
    z_pos = z0_ref[0] + lane // LY
    bias_sum = jnp.zeros((64, 256), F32)
    head_sums = [jnp.zeros((64, 256), F32) for _ in range(4)]
    for t in range(2):
        for x in range(2):
            cols = slice((t * 2 + x) * 256, (t * 2 + x) * 256 + 256)
            acc = jnp.zeros((128, 256), F32)
            for c in range(12):
                size = SIZES[c // 2]
                acc = acc + jnp.dot(
                    w_ref[c, :, 0:size], a_ref[c, 0:size, cols], preferred_element_type=F32
                )
            hidden = acc[:64] + acc[64:] + small_ref[:, 4:5]
            act = jnp.tanh(hidden)
            act_grad = jnp.zeros((64, 256), F32)
            for mu in range(4):
                fixed = pat_ref[mu, 0] * (x0_ref[0] + x) + pat_ref[mu, 3] * t + par_ref[mu]
                summed = pat_ref[mu, 1] * y_pos + pat_ref[mu, 2] * z_pos + fixed
                active = ((summed & 1) == 0).astype(F32)
                weight = small_ref[:, mu : mu + 1]
                coef = active * jnp.sum(weight * act, axis=0, keepdims=True)
                coef_ref[mu, t, x : x + 1, :] = coef
                coef_grad = active * cot_ref[mu, t, x : x + 1, :] * (1.0 / math.sqrt(ROWS))
                act_grad = act_grad + weight * coef_grad
                head_sums[mu] = head_sums[mu] + act * coef_grad
            hidden_grad = act_grad * (1.0 - act * act)
            bias_sum = bias_sum + hidden_grad
            low_ref[:, cols] = hidden_grad.astype(BF16)

    spot = lanes((64, 128))
    small = jnp.zeros((64, 128), F32)
    for i, total in enumerate(head_sums + [bias_sum]):
        value = jnp.sum(total, axis=1, keepdims=True)
        rounded = value.astype(BF16).astype(F32)
        small = jnp.where(spot == i, rounded, jnp.where(spot == i + 8, value - rounded, small))

    def put(j, value):
        rows_ref[pl.ds(j, 64, stride=16), :] = value

    ends = [jnp.zeros((64, 128), F32), jnp.zeros((64, 128), F32)]
    for c in range(12):
        start, size = STARTS[c // 2], SIZES[c // 2]
        grad = lax.dot_general(low_ref[...], a_ref[c, 0:size, :], NT, preferred_element_type=F32)
        kept = jnp.dot(grad.astype(BF16), keep_ref[start : start + size, :], preferred_element_type=F32)
        put(c, kept[:, :128])
        end = kept[:, 128:]
        ends[c // 8] = ends[c // 8] + (pltpu.roll(end, 16 * (c % 8), 1) if c % 8 else end)
    put(12, ends[0])
    put(13, ends[1])
    put(14, small)
    put(15, jnp.zeros((64, 128), F32))
    g_ref[...] = rows_ref[...].reshape(64, 16, 128).astype(BF16)


def total_body(me_ref, in_ref, out_ref):
    total = jnp.sum(in_ref[...].astype(F32), axis=0)
    row = me_ref[0] * total.shape[0] + lax.broadcasted_iota(jnp.int32, total.shape, 0)
    lane = lanes(total.shape)
    whole = jnp.where(lane < 8, total + pltpu.roll(total, 120, 1), 0.0)
    rounded = whole.astype(BF16).astype(F32)
    rest = pltpu.roll(whole - rounded, 8, 1)
    total = jnp.where(row % 16 == 14, jnp.where(lane < 8, rounded, rest), total)
    out_ref[...] = jnp.broadcast_to(total.astype(BF16)[None], out_ref.shape)


def expand_body(g_ref, spread_ref, k_any, b_ref, h_ref, rows_ref, k_ref, sems):
    rows_ref[...] = g_ref[...].astype(F32).reshape(1024, 128)

    def get(j):
        return rows_ref[pl.ds(j, 64, stride=16), :]

    ends = [get(12), get(13)]
    copies = []
    for p in range(6):
        for r in range(2):
            c = 2 * p + r
            end = ends[c // 8]
            end = pltpu.roll(end, 128 - 16 * (c % 8), 1) if c % 8 else end
            kept = jnp.concatenate([get(c), end[:, :16]], axis=1).astype(BF16)
            full = jnp.dot(kept, spread_ref[p], preferred_element_type=F32)
            for leaf in range(4):
                k_ref[8 * p + 2 * leaf + r] = full[:, leaf * 128 : leaf * 128 + 81]
        part = slice(8 * p, 8 * p + 8)
        copies.append(pltpu.make_async_copy(k_ref.at[part], k_any.at[part], sems.at[p]))
        copies[-1].start()
    small = get(14)
    small = (small + pltpu.roll(small, 120, 1)).T
    h_ref[...] = small[0:4]
    b_ref[...] = small[4:5]
    for copy in copies:
        copy.wait()


def call(body, outs, scratch, *args, smem=0, away=(), outs_away=(), name):
    def spec(i, away):
        return pl.BlockSpec(memory_space=pl.ANY if i in away else pltpu.VMEM)

    specs = [pl.BlockSpec(memory_space=pltpu.SMEM)] * smem
    return pl.pallas_call(
        body,
        out_shape=outs,
        in_specs=specs + [spec(i, away) for i in range(smem, len(args))],
        out_specs=tuple(spec(i, outs_away) for i in range(len(outs))),
        scratch_shapes=scratch,
        compiler_params=PARAMS,
        interpret=INTERPRET,
        name=name,
    )(*args)


def shifted(x, axis, by):
    count = lax.axis_size(axis)
    return lax.ppermute(x, axis, [(i, (i + by) % count) for i in range(count)])


def per_device(gauge_links, pattern, link_parity, conv_weight, conv_bias, head_weight, cotangent):
    shape = jax.ShapeDtypeStruct
    sems = pltpu.SemaphoreType.DMA
    x_edge, z_edge = call(
        send_body, (shape((3, 2, 3, 3, 5, 1, 256), F32), shape((3, 2, 3, 3, 5, 2, 128), F32)), [sems((3,))],
        gauge_links, away=(0,), outs_away=(0, 1), name="send",
    )
    next_x = shifted(x_edge, "xy", -1)
    next_z = shifted(z_edge, "gz", -1)
    keep = jnp.asarray(np.concatenate(KEEP), BF16)
    spread = jnp.asarray(SPREAD, BF16)
    weights = []
    for planes in ((0, 1, 2), (3, 4, 5)):
        weights.append(call(
            functools.partial(weights_body, planes), (shape((6, 128, 256), BF16), shape((64, 8), F32)), [],
            conv_weight.transpose(1, 2, 0), spread, keep, head_weight.T, conv_bias[None], name="weights",
        ))
    next_x, next_z, weights[0] = lax.optimization_barrier((next_x, next_z, weights[0]))
    half = shape((12, 16, 128), BF16)
    halo = pltpu.VMEM((3, 2, 3, 3, 24, 128), F32)
    low_z, high_z = call(
        loops_body, (half, half),
        [
            pltpu.VMEM((4, 2, 3, 3, 24, 128), F32), pltpu.VMEM(next_x.shape, F32), pltpu.VMEM(next_z.shape, F32),
            halo, halo, pltpu.VMEM((12, 24, 128), F32), pltpu.VMEM((12, 2, 16, 128), F32), sems((14,)),
        ],
        gauge_links, next_x, next_z, away=(0, 1, 2), name="loops",
    )
    before_z = shifted(high_z, "gz", 1)
    after_z = shifted(low_z, "gz", -1)
    block = jnp.stack([before_z, low_z, high_z, after_z])
    before_x = shifted(block, "xy", 1)
    after_x = shifted(block, "xy", -1)
    x_first = (lax.axis_index("xy") * 2).reshape(1)
    z_first = (lax.axis_index("gz") * 4).reshape(1)
    coefficients, grads = call(
        layer_body, (shape((4, 2, 2, 256), F32), shape((64, 16, 128), BF16)),
        [pltpu.VMEM(block.shape, BF16)] * 3
        + [
            pltpu.VMEM((12, 128, 256), BF16), pltpu.VMEM(keep.shape, BF16), pltpu.VMEM((12, 256, 1024), BF16),
            pltpu.VMEM((64, 1024), BF16), pltpu.VMEM((1024, 128), F32), sems((6,)),
        ],
        x_first, z_first, pattern, link_parity, before_x, block, after_x, weights[0][0], weights[1][0], keep,
        weights[0][1], cotangent, smem=4, away=range(4, 10), name="layer",
    )
    both = ("xy", "gz")
    count = lax.axis_size(both)
    chunks = grads.reshape(count, 1024 // count, 128)
    chunks = lax.all_to_all(chunks, both, 0, 0, tiled=True)
    me = lax.axis_index(both).reshape(1)
    chunks = call(total_body, (shape(chunks.shape, BF16),), [], me, chunks, smem=1, name="total")[0]
    chunks = lax.all_to_all(chunks, both, 0, 0, tiled=True)
    grad_kernel, grad_bias, grad_head = call(
        expand_body, (shape((48, 64, 81), F32), shape((1, 64), F32), shape((4, 64), F32)),
        [pltpu.VMEM((1024, 128), F32), pltpu.VMEM((48, 64, 81), F32), sems((6,))],
        chunks.reshape(64, 16, 128), spread, outs_away=(0,), name="expand",
    )
    return coefficients, grad_kernel.transpose(2, 0, 1), grad_bias.reshape(64), grad_head.T


def solution(mesh):
    return jax.shard_map(
        per_device,
        mesh=mesh,
        in_specs=(
            P(None, None, None, None, None, "xy", "gz"),
            P(),
            P(),
            P(),
            P(),
            P(),
            P(None, None, "xy", "gz"),
        ),
        out_specs=(P(None, None, "xy", "gz"), P(), P(), P()),
        check_vma=False,
    )
```

```python
import math

import jax
import jax.numpy as jnp
import numpy as np
from jax import lax
from jax.experimental import pallas as pl
from jax.experimental.pallas import tpu as pltpu
from jax.sharding import PartitionSpec as P

LY = 64
ROWS = 1024
F32 = jnp.float32
BF16 = jnp.bfloat16

plane_pairs = ((0, 1), (0, 2), (0, 3), (1, 2), (1, 3), (2, 3))
INTERPRET = False
PARAMS = pltpu.CompilerParams(vmem_limit_bytes=56 * 2**20)


def lanes(shape):
    return lax.broadcasted_iota(jnp.int32, shape, len(shape) - 1)


def shift_y(x, by):
    if by == 0:
        return x
    axis = x.ndim - 1
    inner = pltpu.roll(x, (-by) % 128, axis)
    wrapped = pltpu.roll(x, (64 - by) % 128, axis)
    y = lanes(x.shape) % LY
    crossed = (y >= LY - by) if by > 0 else (y < -by)
    return jnp.where(crossed, wrapped, inner)


def plane_tables():
    tiles, keep, spread = [], [], np.zeros((6, 144, 512), np.float32)
    for p, pair in enumerate(plane_pairs):
        spans = [range(0 if d in pair else 1, 4) for d in range(4)]
        tiles.append([(z, y) for z in spans[2] for y in spans[1]])
        kept = {}
        table = np.zeros((16 * len(tiles[p]), 256), np.float32)
        for i, (z, y) in enumerate(tiles[p]):
            for x in spans[0]:
                for t in spans[3]:
                    table[16 * i + 4 * x + t, len(kept)] = 1
                    kept[x, y, z, t] = len(kept)
        keep.append(table)
        for leaf, back in enumerate(((), (pair[0],), (pair[1],), pair)):
            sx, sy, sz, st = (0 if d in back else 1 for d in range(4))
            for k in range(81):
                dx, dz, dt, dy = k // 27, k // 9 % 3, k // 3 % 3, k % 3
                spread[p, kept[dx + sx, dy + sy, dz + sz, dt + st], leaf * 128 + k] = 1
    return tiles, keep, spread


TILES, KEEP, SPREAD = plane_tables()
SIZES = [16 * len(t) for t in TILES]
STARTS = [sum(SIZES[:p]) for p in range(6)]
NT = (((1,), (1,)), ((), ()))


def weights_body(w_ref, spread_ref, keep_ref, head_ref, bias_ref, out_ref, small_ref):
    for p in range(6):
        table = keep_ref[STARTS[p] : STARTS[p] + SIZES[p], :]
        for r in range(2):
            full = jnp.zeros((64, 144), F32)
            for leaf in range(4):
                full = full + lax.dot_general(
                    w_ref[8 * p + 2 * leaf + r], spread_ref[p, :, leaf * 128 : leaf * 128 + 81], NT,
                    preferred_element_type=F32,
                )
            high = full.astype(BF16)
            low = (full - high.astype(F32)).astype(BF16)
            both = jnp.concatenate([high, low], axis=0)
            out_ref[2 * p + r, :, 0 : SIZES[p]] = lax.dot_general(
                both, table[:, :144], NT, preferred_element_type=F32
            ).astype(BF16)
    small_ref[...] = jnp.concatenate([head_ref[...], bias_ref[...], jnp.zeros((3, 64), F32)], axis=0).T


def run(copies):
    for copy in copies:
        copy.start()
    for copy in copies:
        copy.wait()


def fetch(links_ref, l_ref, sems, slices):
    return [
        pltpu.make_async_copy(
            links_ref.at[:, :, :, :, tau, :, lb * 128 : lb * 128 + 128],
            l_ref.at[0:4, :, :, :, tau * 4 + lb * 2 : tau * 4 + lb * 2 + 2, :],
            sems.at[tau * 2 + lb],
        )
        for tau in range(slices)
        for lb in range(2)
    ]


def send_body(links_ref, x_ref, z_ref, l_ref, sems):
    run(fetch(links_ref, l_ref, sems, 5))
    rows_ref = l_ref.reshape(90 * 24, 128)
    for tau in range(5):
        for half in range(2):
            at = tau * 2 + half
            x_ref[at] = rows_ref[pl.ds(18 * 24 + tau * 4 + half * 2, 54, stride=24), :].astype(BF16)
            row = tau * 4 + half
            first = rows_ref[pl.ds(row, 36, stride=24), :]
            last = rows_ref[pl.ds(54 * 24 + row, 18, stride=24), :]
            z_ref[at] = jnp.concatenate([first, last], axis=0).astype(BF16)


def loops_body(
    links_ref, xh_ref, zh_ref, o0_ref, o1_ref, l_ref, xs_ref, zs_ref, pq_ref, tile_ref, sems
):
    copies = fetch(links_ref, l_ref, sems, 6)
    for copy in copies:
        copy.start()
    for tau in range(5):
        for half in range(2):
            at = tau * 2 + half
            xs_ref[pl.ds(tau * 4 + half * 2 + 1, 54, stride=24), :] = xh_ref[at].astype(F32)
            zs_ref[pl.ds(tau * 4 + 2 + half, 54, stride=24), :] = zh_ref[at].astype(F32)
    for copy in copies:
        copy.wait()
    row = lax.broadcasted_iota(jnp.int32, (8, 128), 0)
    odd_x = row % 2 == 1
    high_z = row % 4 >= 2
    upper = lanes((8, 128)) >= LY

    def at_site(d, k):
        part = slice(8 * k, 8 * k + 8)
        return [
            [[l_ref[d, ri, i, j, part, :] for j in range(3)] for i in range(3)] for ri in range(2)
        ]

    def border(d, ri, i, j, k):
        row = (((d * 2 + ri) * 3 + i) * 3 + j) * 24 + 8 * k
        return slice(row, row + 8)

    def ahead(d, step, k):
        part = slice(8 * k, 8 * k + 8)

        def one(ri, i, j):
            if step == 3:
                if k < 2:
                    return l_ref[d, ri, i, j, 8 * k + 4 : 8 * k + 12, :]
                return pltpu.roll(l_ref[d, ri, i, j, 16:24, :], 4, 0)
            own = l_ref[d, ri, i, j, part, :]
            if step == 0:
                return jnp.where(odd_x, xs_ref[border(d - 1, ri, i, j, k), :], pltpu.roll(own, 7, 0))
            if step == 1:
                return shift_y(own, 1)
            edge = zs_ref[border(min(d, 2), ri, i, j, k), :]
            beyond = jnp.where(high_z, edge, pltpu.roll(own, 6, 0))
            return pltpu.roll(jnp.where(upper, own, beyond), LY, 1)

        return [[[one(ri, i, j) for j in range(3)] for i in range(3)] for ri in range(2)]

    def product(a, b, i, j):
        re = a[0][i][0] * b[0][0][j] - a[1][i][0] * b[1][0][j]
        im = a[0][i][0] * b[1][0][j] + a[1][i][0] * b[0][0][j]
        for m in (1, 2):
            re = re + a[0][i][m] * b[0][m][j] - a[1][i][m] * b[1][m][j]
            im = im + a[0][i][m] * b[1][m][j] + a[1][i][m] * b[0][m][j]
        return re, im

    for k in range(3):
        for p, (mu, nu) in enumerate(plane_pairs):
            u_mu = at_site(mu, k)
            u_nu = at_site(nu, k)
            nu_ahead = ahead(nu, mu, k)
            mu_ahead = ahead(mu, nu, k)
            re = im = None
            for i in range(3):
                for j in range(3):
                    r1, i1 = product(u_mu, nu_ahead, i, j)
                    r2, i2 = product(u_nu, mu_ahead, i, j)
                    re_term = r1 * r2 + i1 * i2
                    im_term = i1 * r2 - r1 * i2
                    re = re_term if re is None else re + re_term
                    im = im_term if im is None else im + im_term
            pq_ref[2 * p, 8 * k : 8 * k + 8, :] = re
            pq_ref[2 * p + 1, 8 * k : 8 * k + 8, :] = im
    for c in range(12):
        for lb, o_ref in enumerate((o0_ref, o1_ref)):
            for t in range(2):
                for x in range(2):
                    tile_ref[c, lb, t * 8 + x * 4 : t * 8 + x * 4 + 4, :] = pq_ref[
                        c, pl.ds(4 * t + 2 * lb + x, 4, stride=4), :
                    ]
            o_ref[c] = tile_ref[c, lb].astype(BF16)


def layer_body(
    x0_ref, z0_ref, pat_ref, par_ref, el_ref, e_ref, er_ref, w_ref, small_ref, keep_ref, cot_ref,
    coef_ref, g_ref, a_ref, low_ref, rows_ref,
):
    first = lax.broadcasted_iota(jnp.int32, (8, 128), 0) < 4
    lane = lanes((8, 128))
    upper = lane >= LY

    def crossed(by):
        y = lane % LY
        return (y >= LY - by) if by > 0 else (y < -by)

    for p in range(6):
        offsets = sorted({y for _, y in TILES[p]})
        for r in range(2):
            c = 2 * p + r
            for t in range(2):
                part = slice(8 * t, 8 * t + 8)
                cols = []
                for i in range(4):
                    left, own, right = (ref[i, c].astype(F32)[part] for ref in (el_ref, e_ref, er_ref))
                    cols.append((
                        (left, own),
                        (
                            pltpu.roll(jnp.where(first, own, left), 4, 0),
                            pltpu.roll(jnp.where(first, right, own), 4, 0),
                        ),
                    ))
                for x in range(2):
                    for y in offsets:
                        by = y - 2
                        made = []
                        for h in range(2):
                            plain, other = [], []
                            for i in range(4):
                                v = cols[i][x][h]
                                near = v if by == 0 else pltpu.roll(v, (-by) % 128, 1)
                                far = pltpu.roll(v, (LY - by) % 128, 1)
                                if by == 0:
                                    plain.append(near)
                                    other.append(far)
                                else:
                                    plain.append(jnp.where(crossed(by), far, near))
                                    other.append(jnp.where(crossed(by), near, far))
                            made.append([
                                plain[z // 2] if z % 2 == 0 else jnp.where(upper, other[z // 2 + 1], other[z // 2])
                                for z in range(6)
                            ])
                        both = [jnp.concatenate([u, v], axis=0).astype(BF16) for u, v in zip(*made)]
                        for n, (z, y_at) in enumerate(TILES[p]):
                            if y_at == y:
                                for lb in range(2):
                                    col = (t * 4 + x * 2 + lb) * 128
                                    a_ref[c, 16 * n : 16 * n + 16, col : col + 128] = both[z + 2 * lb]

    lane = lanes((1, 256))
    y_pos = lane % LY
    z_pos = z0_ref[0] + lane // LY
    bias_sum = jnp.zeros((64, 256), F32)
    head_sums = [jnp.zeros((64, 256), F32) for _ in range(4)]
    for t in range(2):
        for x in range(2):
            cols = slice((t * 2 + x) * 256, (t * 2 + x) * 256 + 256)
            acc = jnp.zeros((128, 256), F32)
            for c in range(12):
                size = SIZES[c // 2]
                acc = acc + jnp.dot(
                    w_ref[c, :, 0:size], a_ref[c, 0:size, cols], preferred_element_type=F32
                )
            hidden = acc[:64] + acc[64:] + small_ref[:, 4:5]
            act = jnp.tanh(hidden)
            act_grad = jnp.zeros((64, 256), F32)
            for mu in range(4):
                fixed = pat_ref[mu, 0] * (x0_ref[0] + x) + pat_ref[mu, 3] * t + par_ref[mu]
                summed = pat_ref[mu, 1] * y_pos + pat_ref[mu, 2] * z_pos + fixed
                active = ((summed & 1) == 0).astype(F32)
                weight = small_ref[:, mu : mu + 1]
                coef = active * jnp.sum(weight * act, axis=0, keepdims=True)
                coef_ref[mu, t, x : x + 1, :] = coef
                coef_grad = active * cot_ref[mu, t, x : x + 1, :] * (1.0 / math.sqrt(ROWS))
                act_grad = act_grad + weight * coef_grad
                head_sums[mu] = head_sums[mu] + act * coef_grad
            hidden_grad = act_grad * (1.0 - act * act)
            bias_sum = bias_sum + hidden_grad
            low_ref[:, cols] = hidden_grad.astype(BF16)

    spot = lanes((64, 128))
    small = jnp.zeros((64, 128), F32)
    for i, total in enumerate(head_sums + [bias_sum]):
        value = jnp.sum(total, axis=1, keepdims=True)
        rounded = value.astype(BF16).astype(F32)
        small = jnp.where(spot == i, rounded, jnp.where(spot == i + 8, value - rounded, small))

    def put(j, value):
        rows_ref[pl.ds(j, 64, stride=16), :] = value

    ends = [jnp.zeros((64, 128), F32), jnp.zeros((64, 128), F32)]
    for c in range(12):
        start, size = STARTS[c // 2], SIZES[c // 2]
        grad = lax.dot_general(low_ref[...], a_ref[c, 0:size, :], NT, preferred_element_type=F32)
        kept = jnp.dot(grad.astype(BF16), keep_ref[start : start + size, :], preferred_element_type=F32)
        put(c, kept[:, :128])
        end = kept[:, 128:]
        ends[c // 8] = ends[c // 8] + (pltpu.roll(end, 16 * (c % 8), 1) if c % 8 else end)
    put(12, ends[0])
    put(13, ends[1])
    put(14, small)
    put(15, jnp.zeros((64, 128), F32))
    g_ref[...] = rows_ref[...].reshape(64, 16, 128).astype(BF16)


def total_body(me_ref, in_ref, out_ref):
    total = jnp.sum(in_ref[...].astype(F32), axis=0)
    row = me_ref[0] * total.shape[0] + lax.broadcasted_iota(jnp.int32, total.shape, 0)
    lane = lanes(total.shape)
    whole = jnp.where(lane < 8, total + pltpu.roll(total, 120, 1), 0.0)
    rounded = whole.astype(BF16).astype(F32)
    rest = pltpu.roll(whole - rounded, 8, 1)
    total = jnp.where(row % 16 == 14, jnp.where(lane < 8, rounded, rest), total)
    out_ref[...] = jnp.broadcast_to(total.astype(BF16)[None], out_ref.shape)


def expand_body(g_ref, spread_ref, k_ref, b_ref, h_ref, rows_ref):
    rows_ref[...] = g_ref[...].astype(F32).reshape(1024, 128)

    def get(j):
        return rows_ref[pl.ds(j, 64, stride=16), :]

    ends = [get(12), get(13)]
    for c in range(12):
        p, r = c // 2, c % 2
        end = ends[c // 8]
        end = pltpu.roll(end, 128 - 16 * (c % 8), 1) if c % 8 else end
        kept = jnp.concatenate([get(c), end[:, :16]], axis=1).astype(BF16)
        full = jnp.dot(kept, spread_ref[p], preferred_element_type=F32)
        for leaf in range(4):
            k_ref[8 * p + 2 * leaf + r] = full[:, leaf * 128 : leaf * 128 + 81]
    small = get(14)
    small = (small + pltpu.roll(small, 120, 1)).T
    h_ref[...] = small[0:4]
    b_ref[...] = small[4:5]


def call(body, outs, scratch, *args, smem=0, away=(), name):
    def spec(i, away):
        return pl.BlockSpec(memory_space=pl.ANY if i in away else pltpu.VMEM)

    specs = [pl.BlockSpec(memory_space=pltpu.SMEM)] * smem
    return pl.pallas_call(
        body,
        out_shape=outs,
        in_specs=specs + [spec(i, away) for i in range(smem, len(args))],
        out_specs=(pl.BlockSpec(memory_space=pltpu.VMEM),) * len(outs),
        scratch_shapes=scratch,
        compiler_params=PARAMS,
        interpret=INTERPRET,
        name=name,
    )(*args)


def shifted(x, axis, by):
    count = lax.axis_size(axis)
    return lax.ppermute(x, axis, [(i, (i + by) % count) for i in range(count)])


def per_device(gauge_links, pattern, link_parity, conv_weight, conv_bias, head_weight, cotangent):
    shape = jax.ShapeDtypeStruct
    sems = pltpu.SemaphoreType.DMA
    edge = shape((10, 54, 128), BF16)
    links = pltpu.VMEM((5, 2, 3, 3, 24, 128), F32)
    x_edge, z_edge = call(
        send_body, (edge, edge), [links, sems((10,))], gauge_links, away=(0,), name="send"
    )
    next_x = shifted(x_edge, "xy", -1)
    next_z = shifted(z_edge, "gz", -1)
    keep = jnp.asarray(np.concatenate(KEEP), BF16)
    spread = jnp.asarray(SPREAD, BF16)
    weights, small = call(
        weights_body, (shape((12, 128, 256), BF16), shape((64, 8), F32)), [],
        conv_weight.transpose(1, 2, 0), spread, keep, head_weight.T, conv_bias[None], name="weights",
    )
    half = shape((12, 16, 128), BF16)
    border = pltpu.VMEM((57 * 24, 128), F32)
    low_z, high_z = call(
        loops_body, (half, half),
        [links, border, border, pltpu.VMEM((14, 24, 128), F32), pltpu.VMEM((12, 2, 16, 128), F32), sems((12,))],
        gauge_links, next_x, next_z, away=(0,), name="loops",
    )
    before_z = shifted(high_z, "gz", 1)
    after_z = shifted(low_z, "gz", -1)
    block = jnp.stack([before_z, low_z, high_z, after_z])
    before_x = shifted(block, "xy", 1)
    after_x = shifted(block, "xy", -1)
    x_first = (lax.axis_index("xy") * 2).reshape(1)
    z_first = (lax.axis_index("gz") * 4).reshape(1)
    coefficients, grads = call(
        layer_body, (shape((4, 2, 2, 256), F32), shape((64, 16, 128), BF16)),
        [pltpu.VMEM((12, 256, 1024), BF16), pltpu.VMEM((64, 1024), BF16), pltpu.VMEM((1024, 128), F32)],
        x_first, z_first, pattern, link_parity, before_x, block, after_x, weights, small, keep,
        cotangent, smem=4, name="layer",
    )
    both = ("xy", "gz")
    count = lax.axis_size(both)
    chunks = grads.reshape(count, 1024 // count, 128)
    chunks = lax.all_to_all(chunks, both, 0, 0, tiled=True)
    me = lax.axis_index(both).reshape(1)
    chunks = call(total_body, (shape(chunks.shape, BF16),), [], me, chunks, smem=1, name="total")[0]
    chunks = lax.all_to_all(chunks, both, 0, 0, tiled=True)
    grad_kernel, grad_bias, grad_head = call(
        expand_body, (shape((48, 64, 81), F32), shape((1, 64), F32), shape((4, 64), F32)),
        [pltpu.VMEM((1024, 128), F32)], chunks.reshape(64, 16, 128), spread, name="expand",
    )
    return coefficients, grad_kernel.transpose(2, 0, 1), grad_bias.reshape(64), grad_head.T


def solution(mesh):
    return jax.shard_map(
        per_device,
        mesh=mesh,
        in_specs=(
            P(None, None, None, None, None, "xy", "gz"),
            P(),
            P(),
            P(),
            P(),
            P(),
            P(None, None, "xy", "gz"),
        ),
        out_specs=(P(None, None, "xy", "gz"), P(), P(), P()),
        check_vma=False,
    )
```

```python
import math

import jax
import jax.numpy as jnp
import numpy as np
from jax import lax
from jax.experimental import pallas as pl
from jax.experimental.pallas import tpu as pltpu
from jax.sharding import PartitionSpec as P

LY = 64
ROWS = 1024
F32 = jnp.float32
BF16 = jnp.bfloat16

plane_pairs = ((0, 1), (0, 2), (0, 3), (1, 2), (1, 3), (2, 3))
INTERPRET = False
PARAMS = pltpu.CompilerParams(vmem_limit_bytes=56 * 2**20)


def lanes(shape):
    return lax.broadcasted_iota(jnp.int32, shape, len(shape) - 1)


def shift_y(x, by):
    if by == 0:
        return x
    axis = x.ndim - 1
    inner = pltpu.roll(x, (-by) % 128, axis)
    wrapped = pltpu.roll(x, (64 - by) % 128, axis)
    y = lanes(x.shape) % LY
    crossed = (y >= LY - by) if by > 0 else (y < -by)
    return jnp.where(crossed, wrapped, inner)


def plane_tables():
    tiles, keep, spread = [], [], np.zeros((6, 144, 512), np.float32)
    for p, pair in enumerate(plane_pairs):
        spans = [range(0 if d in pair else 1, 4) for d in range(4)]
        tiles.append([(z, y) for z in spans[2] for y in spans[1]])
        kept = {}
        table = np.zeros((16 * len(tiles[p]), 256), np.float32)
        for i, (z, y) in enumerate(tiles[p]):
            for x in spans[0]:
                for t in spans[3]:
                    table[16 * i + 4 * x + t, len(kept)] = 1
                    kept[x, y, z, t] = len(kept)
        keep.append(table)
        for leaf, back in enumerate(((), (pair[0],), (pair[1],), pair)):
            sx, sy, sz, st = (0 if d in back else 1 for d in range(4))
            for k in range(81):
                dx, dz, dt, dy = k // 27, k // 9 % 3, k // 3 % 3, k % 3
                spread[p, kept[dx + sx, dy + sy, dz + sz, dt + st], leaf * 128 + k] = 1
    return tiles, keep, spread


TILES, KEEP, SPREAD = plane_tables()
SIZES = [16 * len(t) for t in TILES]
STARTS = [sum(SIZES[:p]) for p in range(6)]
NT = (((1,), (1,)), ((), ()))


def weights_body(w_ref, spread_ref, keep_ref, head_ref, bias_ref, out_ref, small_ref):
    for p in range(6):
        table = keep_ref[STARTS[p] : STARTS[p] + SIZES[p], :]
        for r in range(2):
            full = jnp.zeros((64, 144), F32)
            for leaf in range(4):
                full = full + lax.dot_general(
                    w_ref[8 * p + 2 * leaf + r], spread_ref[p, :, leaf * 128 : leaf * 128 + 81], NT,
                    preferred_element_type=F32,
                )
            high = full.astype(BF16)
            low = (full - high.astype(F32)).astype(BF16)
            both = jnp.concatenate([high, low], axis=0)
            out_ref[2 * p + r, :, 0 : SIZES[p]] = lax.dot_general(
                both, table[:, :144], NT, preferred_element_type=F32
            ).astype(BF16)
    small_ref[...] = jnp.concatenate([head_ref[...], bias_ref[...], jnp.zeros((3, 64), F32)], axis=0).T


def place(c, x):
    return 64 + 5 * c if x == 1 else (32 + 5 * c if c < 6 else 5 * (c - 6))


def run(copies):
    for copy in copies:
        copy.start()
    for copy in copies:
        copy.wait()


def fetch(links_ref, l_ref, sems, slices):
    return [
        pltpu.make_async_copy(
            links_ref.at[:, :, :, :, tau, :, lb * 128 : lb * 128 + 128],
            l_ref.at[0:4, :, :, :, tau * 4 + lb * 2 : tau * 4 + lb * 2 + 2, :],
            sems.at[tau * 2 + lb],
        )
        for tau in range(slices)
        for lb in range(2)
    ]


def send_body(links_ref, x_ref, z_ref, l_ref, sems):
    run(fetch(links_ref, l_ref, sems, 5))
    rows_ref = l_ref.reshape(90 * 24, 128)
    for tau in range(5):
        for half in range(2):
            at = tau * 2 + half
            x_ref[at] = rows_ref[pl.ds(18 * 24 + tau * 4 + half * 2, 54, stride=24), :].astype(BF16)
            row = tau * 4 + half
            first = rows_ref[pl.ds(row, 36, stride=24), :]
            last = rows_ref[pl.ds(54 * 24 + row, 18, stride=24), :]
            z_ref[at] = jnp.concatenate([first, last], axis=0).astype(BF16)


def loops_body(
    links_ref, xh_ref, zh_ref, o0_ref, o1_ref, l_ref, xs_ref, zs_ref, pq_ref, tile_ref, sems
):
    copies = fetch(links_ref, l_ref, sems, 6)
    for copy in copies:
        copy.start()
    for tau in range(5):
        for half in range(2):
            at = tau * 2 + half
            xs_ref[pl.ds(tau * 4 + half * 2 + 1, 54, stride=24), :] = xh_ref[at].astype(F32)
            zs_ref[pl.ds(tau * 4 + 2 + half, 54, stride=24), :] = zh_ref[at].astype(F32)
    tile_ref[...] = jnp.zeros_like(tile_ref)
    for copy in copies:
        copy.wait()
    row = lax.broadcasted_iota(jnp.int32, (8, 128), 0)
    odd_x = row % 2 == 1
    high_z = row % 4 >= 2
    upper = lanes((8, 128)) >= LY

    def at_site(d, k):
        part = slice(8 * k, 8 * k + 8)
        return [
            [[l_ref[d, ri, i, j, part, :] for j in range(3)] for i in range(3)] for ri in range(2)
        ]

    def border(d, ri, i, j, k):
        row = (((d * 2 + ri) * 3 + i) * 3 + j) * 24 + 8 * k
        return slice(row, row + 8)

    def ahead(d, step, k):
        part = slice(8 * k, 8 * k + 8)

        def one(ri, i, j):
            if step == 3:
                if k < 2:
                    return l_ref[d, ri, i, j, 8 * k + 4 : 8 * k + 12, :]
                return pltpu.roll(l_ref[d, ri, i, j, 16:24, :], 4, 0)
            own = l_ref[d, ri, i, j, part, :]
            if step == 0:
                return jnp.where(odd_x, xs_ref[border(d - 1, ri, i, j, k), :], pltpu.roll(own, 7, 0))
            if step == 1:
                return shift_y(own, 1)
            edge = zs_ref[border(min(d, 2), ri, i, j, k), :]
            beyond = jnp.where(high_z, edge, pltpu.roll(own, 6, 0))
            return pltpu.roll(jnp.where(upper, own, beyond), LY, 1)

        return [[[one(ri, i, j) for j in range(3)] for i in range(3)] for ri in range(2)]

    def product(a, b, i, j):
        re = a[0][i][0] * b[0][0][j] - a[1][i][0] * b[1][0][j]
        im = a[0][i][0] * b[1][0][j] + a[1][i][0] * b[0][0][j]
        for m in (1, 2):
            re = re + a[0][i][m] * b[0][m][j] - a[1][i][m] * b[1][m][j]
            im = im + a[0][i][m] * b[1][m][j] + a[1][i][m] * b[0][m][j]
        return re, im

    for k in range(3):
        for p, (mu, nu) in enumerate(plane_pairs):
            u_mu = at_site(mu, k)
            u_nu = at_site(nu, k)
            nu_ahead = ahead(nu, mu, k)
            mu_ahead = ahead(mu, nu, k)
            re = im = None
            for i in range(3):
                for j in range(3):
                    r1, i1 = product(u_mu, nu_ahead, i, j)
                    r2, i2 = product(u_nu, mu_ahead, i, j)
                    re_term = r1 * r2 + i1 * i2
                    im_term = i1 * r2 - r1 * i2
                    re = re_term if re is None else re + re_term
                    im = im_term if im is None else im + im_term
            pq_ref[2 * p, 8 * k : 8 * k + 8, :] = re
            pq_ref[2 * p + 1, 8 * k : 8 * k + 8, :] = im
    for c in range(12):
        for lb, o_ref in enumerate((o0_ref, o1_ref)):
            for x in range(2):
                row = place(c, x)
                tile_ref[lb, row : row + 5, :] = pq_ref[c, pl.ds(2 * lb + x, 5, stride=4), :]
    o0_ref[...] = tile_ref[0].astype(BF16)
    o1_ref[...] = tile_ref[1].astype(BF16)


def layer_body(
    x0_ref, z0_ref, pat_ref, par_ref, before_ref, z0_own, z1_own, z2_own, z3_own, after_ref, w_ref, small_ref,
    keep_ref, cot_ref, coef_ref, g_ref, a_ref, low_ref, rows_ref, left_ref, own_ref, right_ref,
):
    left_ref[...] = before_ref[...].astype(F32)
    right_ref[...] = after_ref[...].astype(F32)
    for i, ref in enumerate((z0_own, z1_own, z2_own, z3_own)):
        own_ref[i] = ref[...].astype(F32)

    def piece(i, x, c, t):
        if x == 0 and c >= 6:
            return jnp.zeros((4, 128), F32)
        if x < 2:
            ref, row = left_ref, place(c, x) - 32
        elif x < 4:
            ref, row = own_ref, place(c, x - 2)
        else:
            ref, row = right_ref, place(c, 0)
        return ref[i, row + t : row + t + 4, :]

    lane = lanes((8, 128))
    upper = lane >= LY

    def crossed(by):
        y = lane % LY
        return (y >= LY - by) if by > 0 else (y < -by)

    for p in range(6):
        offsets = sorted({y for _, y in TILES[p]})
        for r in range(2):
            c = 2 * p + r
            for t in range(2):
                cols = []
                for i in range(4):
                    pieces = [piece(i, x, c, t) for x in range(5)]
                    cols.append([
                        [jnp.concatenate(pieces[x + 2 * h : x + 2 * h + 2], axis=0) for h in range(2)]
                        for x in range(2)
                    ])
                for x in range(2):
                    for y in offsets:
                        by = y - 2
                        made = []
                        for h in range(2):
                            plain, other = [], []
                            for i in range(4):
                                v = cols[i][x][h]
                                near = v if by == 0 else pltpu.roll(v, (-by) % 128, 1)
                                far = pltpu.roll(v, (LY - by) % 128, 1)
                                if by == 0:
                                    plain.append(near)
                                    other.append(far)
                                else:
                                    plain.append(jnp.where(crossed(by), far, near))
                                    other.append(jnp.where(crossed(by), near, far))
                            made.append([
                                plain[z // 2] if z % 2 == 0 else jnp.where(upper, other[z // 2 + 1], other[z // 2])
                                for z in range(6)
                            ])
                        both = [jnp.concatenate([u, v], axis=0).astype(BF16) for u, v in zip(*made)]
                        for n, (z, y_at) in enumerate(TILES[p]):
                            if y_at == y:
                                for lb in range(2):
                                    col = (t * 4 + x * 2 + lb) * 128
                                    a_ref[c, 16 * n : 16 * n + 16, col : col + 128] = both[z + 2 * lb]

    lane = lanes((1, 256))
    y_pos = lane % LY
    z_pos = z0_ref[0] + lane // LY
    bias_sum = jnp.zeros((64, 256), F32)
    head_sums = [jnp.zeros((64, 256), F32) for _ in range(4)]
    for t in range(2):
        for x in range(2):
            cols = slice((t * 2 + x) * 256, (t * 2 + x) * 256 + 256)
            acc = jnp.zeros((128, 256), F32)
            for c in range(12):
                size = SIZES[c // 2]
                acc = acc + jnp.dot(
                    w_ref[c, :, 0:size], a_ref[c, 0:size, cols], preferred_element_type=F32
                )
            hidden = acc[:64] + acc[64:] + small_ref[:, 4:5]
            act = jnp.tanh(hidden)
            act_grad = jnp.zeros((64, 256), F32)
            for mu in range(4):
                fixed = pat_ref[mu, 0] * (x0_ref[0] + x) + pat_ref[mu, 3] * t + par_ref[mu]
                summed = pat_ref[mu, 1] * y_pos + pat_ref[mu, 2] * z_pos + fixed
                active = ((summed & 1) == 0).astype(F32)
                weight = small_ref[:, mu : mu + 1]
                coef = active * jnp.sum(weight * act, axis=0, keepdims=True)
                coef_ref[mu, t, x : x + 1, :] = coef
                coef_grad = active * cot_ref[mu, t, x : x + 1, :] * (1.0 / math.sqrt(ROWS))
                act_grad = act_grad + weight * coef_grad
                head_sums[mu] = head_sums[mu] + act * coef_grad
            hidden_grad = act_grad * (1.0 - act * act)
            bias_sum = bias_sum + hidden_grad
            low_ref[:, cols] = hidden_grad.astype(BF16)

    spot = lanes((64, 128))
    small = jnp.zeros((64, 128), F32)
    for i, total in enumerate(head_sums + [bias_sum]):
        value = jnp.sum(total, axis=1, keepdims=True)
        rounded = value.astype(BF16).astype(F32)
        small = jnp.where(spot == i, rounded, jnp.where(spot == i + 8, value - rounded, small))

    def put(j, value):
        rows_ref[pl.ds(j, 64, stride=16), :] = value

    ends = [jnp.zeros((64, 128), F32), jnp.zeros((64, 128), F32)]
    for c in range(12):
        start, size = STARTS[c // 2], SIZES[c // 2]
        grad = lax.dot_general(low_ref[...], a_ref[c, 0:size, :], NT, preferred_element_type=F32)
        kept = jnp.dot(grad.astype(BF16), keep_ref[start : start + size, :], preferred_element_type=F32)
        put(c, kept[:, :128])
        end = kept[:, 128:]
        ends[c // 8] = ends[c // 8] + (pltpu.roll(end, 16 * (c % 8), 1) if c % 8 else end)
    put(12, ends[0])
    put(13, ends[1])
    put(14, small)
    put(15, jnp.zeros((64, 128), F32))
    g_ref[...] = rows_ref[...].reshape(64, 16, 128).astype(BF16)


def total_body(me_ref, in_ref, out_ref):
    total = jnp.sum(in_ref[...].astype(F32), axis=0)
    row = me_ref[0] * total.shape[0] + lax.broadcasted_iota(jnp.int32, total.shape, 0)
    lane = lanes(total.shape)
    whole = jnp.where(lane < 8, total + pltpu.roll(total, 120, 1), 0.0)
    rounded = whole.astype(BF16).astype(F32)
    rest = pltpu.roll(whole - rounded, 8, 1)
    total = jnp.where(row % 16 == 14, jnp.where(lane < 8, rounded, rest), total)
    out_ref[...] = jnp.broadcast_to(total.astype(BF16)[None], out_ref.shape)


def expand_body(g_ref, spread_ref, k_ref, b_ref, h_ref, rows_ref):
    rows_ref[...] = g_ref[...].astype(F32).reshape(1024, 128)

    def get(j):
        return rows_ref[pl.ds(j, 64, stride=16), :]

    ends = [get(12), get(13)]
    for c in range(12):
        p, r = c // 2, c % 2
        end = ends[c // 8]
        end = pltpu.roll(end, 128 - 16 * (c % 8), 1) if c % 8 else end
        kept = jnp.concatenate([get(c), end[:, :16]], axis=1).astype(BF16)
        full = jnp.dot(kept, spread_ref[p], preferred_element_type=F32)
        for leaf in range(4):
            k_ref[8 * p + 2 * leaf + r] = full[:, leaf * 128 : leaf * 128 + 81]
    small = get(14)
    small = (small + pltpu.roll(small, 120, 1)).T
    h_ref[...] = small[0:4]
    b_ref[...] = small[4:5]


def call(body, outs, scratch, *args, smem=0, away=(), name):
    def spec(i, away):
        return pl.BlockSpec(memory_space=pl.ANY if i in away else pltpu.VMEM)

    specs = [pl.BlockSpec(memory_space=pltpu.SMEM)] * smem
    return pl.pallas_call(
        body,
        out_shape=outs,
        in_specs=specs + [spec(i, away) for i in range(smem, len(args))],
        out_specs=(pl.BlockSpec(memory_space=pltpu.VMEM),) * len(outs),
        scratch_shapes=scratch,
        compiler_params=PARAMS,
        interpret=INTERPRET,
        name=name,
    )(*args)


def shifted(x, axis, by):
    count = lax.axis_size(axis)
    return lax.ppermute(x, axis, [(i, (i + by) % count) for i in range(count)])


def per_device(gauge_links, pattern, link_parity, conv_weight, conv_bias, head_weight, cotangent):
    shape = jax.ShapeDtypeStruct
    sems = pltpu.SemaphoreType.DMA
    edge = shape((10, 54, 128), BF16)
    links = pltpu.VMEM((5, 2, 3, 3, 24, 128), F32)
    x_edge, z_edge = call(
        send_body, (edge, edge), [links, sems((10,))], gauge_links, away=(0,), name="send"
    )
    next_x = shifted(x_edge, "xy", -1)
    next_z = shifted(z_edge, "gz", -1)
    keep = jnp.asarray(np.concatenate(KEEP), BF16)
    spread = jnp.asarray(SPREAD, BF16)
    weights, small = call(
        weights_body, (shape((12, 128, 256), BF16), shape((64, 8), F32)), [],
        conv_weight.transpose(1, 2, 0), spread, keep, head_weight.T, conv_bias[None], name="weights",
    )
    next_x, next_z, weights, small = lax.optimization_barrier((next_x, next_z, weights, small))
    half = shape((128, 128), BF16)
    border = pltpu.VMEM((57 * 24, 128), F32)
    low_z, high_z = call(
        loops_body, (half, half),
        [links, border, border, pltpu.VMEM((14, 24, 128), F32), pltpu.VMEM((2, 128, 128), F32), sems((12,))],
        gauge_links, next_x, next_z, away=(0,), name="loops",
    )
    before_z = shifted(high_z, "gz", 1)
    after_z = shifted(low_z, "gz", -1)
    layers = [before_z, low_z, high_z, after_z]
    right_going = jnp.stack([v[32:] for v in layers])
    before_x = shifted(right_going, "xy", 1)
    held = lax.optimization_barrier((right_going, *layers))
    after_x = shifted(jnp.stack([v[:64] for v in held[1:]]), "xy", -1)
    x_first = (lax.axis_index("xy") * 2).reshape(1)
    z_first = (lax.axis_index("gz") * 4).reshape(1)
    coefficients, grads = call(
        layer_body, (shape((4, 2, 2, 256), F32), shape((64, 16, 128), BF16)),
        [pltpu.VMEM((12, 256, 1024), BF16), pltpu.VMEM((64, 1024), BF16), pltpu.VMEM((1024, 128), F32)]
        + [pltpu.VMEM((4, n, 128), F32) for n in (96, 128, 64)],
        x_first, z_first, pattern, link_parity, before_x, *layers, after_x, weights, small, keep, cotangent,
        smem=4, name="layer",
    )
    both = ("xy", "gz")
    count = lax.axis_size(both)
    chunks = grads.reshape(count, 1024 // count, 128)
    chunks = lax.all_to_all(chunks, both, 0, 0, tiled=True)
    me = lax.axis_index(both).reshape(1)
    chunks = call(total_body, (shape(chunks.shape, BF16),), [], me, chunks, smem=1, name="total")[0]
    chunks = lax.all_to_all(chunks, both, 0, 0, tiled=True)
    grad_kernel, grad_bias, grad_head = call(
        expand_body, (shape((48, 64, 81), F32), shape((1, 64), F32), shape((4, 64), F32)),
        [pltpu.VMEM((1024, 128), F32)], chunks.reshape(64, 16, 128), spread, name="expand",
    )
    return coefficients, grad_kernel.transpose(2, 0, 1), grad_bias.reshape(64), grad_head.T


def solution(mesh):
    return jax.shard_map(
        per_device,
        mesh=mesh,
        in_specs=(
            P(None, None, None, None, None, "xy", "gz"),
            P(),
            P(),
            P(),
            P(),
            P(),
            P(None, None, "xy", "gz"),
        ),
        out_specs=(P(None, None, "xy", "gz"), P(), P(), P()),
        check_vma=False,
    )
```

```python
import functools
import math

import jax
import jax.numpy as jnp
import numpy as np
from jax import lax
from jax.experimental import pallas as pl
from jax.experimental.pallas import tpu as pltpu
from jax.sharding import PartitionSpec as P

LY = 64
ROWS = 1024
F32 = jnp.float32
BF16 = jnp.bfloat16

plane_pairs = ((0, 1), (0, 2), (0, 3), (1, 2), (1, 3), (2, 3))
INTERPRET = False
PARAMS = pltpu.CompilerParams(vmem_limit_bytes=56 * 2**20)


def lanes(shape):
    return lax.broadcasted_iota(jnp.int32, shape, len(shape) - 1)


def shift_y(x, by):
    if by == 0:
        return x
    axis = x.ndim - 1
    inner = pltpu.roll(x, (-by) % 128, axis)
    wrapped = pltpu.roll(x, (64 - by) % 128, axis)
    y = lanes(x.shape) % LY
    crossed = (y >= LY - by) if by > 0 else (y < -by)
    return jnp.where(crossed, wrapped, inner)


def plane_tables():
    tiles, keep, spread = [], [], np.zeros((6, 144, 512), np.float32)
    for p, pair in enumerate(plane_pairs):
        spans = [range(0 if d in pair else 1, 4) for d in range(4)]
        tiles.append([(z, y) for z in spans[2] for y in spans[1]])
        kept = {}
        table = np.zeros((16 * len(tiles[p]), 256), np.float32)
        for i, (z, y) in enumerate(tiles[p]):
            for x in spans[0]:
                for t in spans[3]:
                    table[16 * i + 4 * x + t, len(kept)] = 1
                    kept[x, y, z, t] = len(kept)
        keep.append(table)
        for leaf, back in enumerate(((), (pair[0],), (pair[1],), pair)):
            sx, sy, sz, st = (0 if d in back else 1 for d in range(4))
            for k in range(81):
                dx, dz, dt, dy = k // 27, k // 9 % 3, k // 3 % 3, k % 3
                spread[p, kept[dx + sx, dy + sy, dz + sz, dt + st], leaf * 128 + k] = 1
    return tiles, keep, spread


TILES, KEEP, SPREAD = plane_tables()
SIZES = [16 * len(t) for t in TILES]
STARTS = [sum(SIZES[:p]) for p in range(6)]
NT = (((1,), (1,)), ((), ()))


def weights_body(w_ref, spread_ref, keep_ref, head_ref, bias_ref, out_ref, small_ref):
    for p in range(6):
        table = keep_ref[STARTS[p] : STARTS[p] + SIZES[p], :]
        for r in range(2):
            full = jnp.zeros((64, 144), F32)
            for leaf in range(4):
                full = full + lax.dot_general(
                    w_ref[8 * p + 2 * leaf + r], spread_ref[p, :, leaf * 128 : leaf * 128 + 81], NT,
                    preferred_element_type=F32,
                )
            high = full.astype(BF16)
            low = (full - high.astype(F32)).astype(BF16)
            both = jnp.concatenate([high, low], axis=0)
            out_ref[2 * p + r, :, 0 : SIZES[p]] = lax.dot_general(
                both, table[:, :144], NT, preferred_element_type=F32
            ).astype(BF16)
    small_ref[...] = jnp.concatenate([head_ref[...], bias_ref[...], jnp.zeros((3, 64), F32)], axis=0).T


def run(copies):
    for copy in copies:
        copy.start()
    for copy in copies:
        copy.wait()


def fetch(links_ref, l_ref, sems, slices):
    return [
        pltpu.make_async_copy(
            links_ref.at[:, :, :, :, tau, :, lb * 128 : lb * 128 + 128],
            l_ref.at[0:4, :, :, :, tau * 4 + lb * 2 : tau * 4 + lb * 2 + 2, :],
            sems.at[tau * 2 + lb],
        )
        for tau in range(slices)
        for lb in range(2)
    ]


def send_body(links_ref, x_ref, z_ref, l_ref, sems):
    run(fetch(links_ref, l_ref, sems, 5))
    rows_ref = l_ref.reshape(90 * 24, 128)
    for tau in range(5):
        for half in range(2):
            at = tau * 2 + half
            x_ref[at] = rows_ref[pl.ds(18 * 24 + tau * 4 + half * 2, 54, stride=24), :].astype(BF16)
            row = tau * 4 + half
            first = rows_ref[pl.ds(row, 36, stride=24), :]
            last = rows_ref[pl.ds(54 * 24 + row, 18, stride=24), :]
            z_ref[at] = jnp.concatenate([first, last], axis=0).astype(BF16)


def loops_body(planes, *refs):
    if 0 in planes:
        links_ref, z_edge, x_edge, low_in, high_in, o0_ref, o1_ref, l_ref = refs[:8]
        zs_ref, xs_ref, pq_ref, tile_ref, sems = refs[8:]
        o0_ref[64:128] = low_in[...]
        o1_ref[64:128] = high_in[...]
    else:
        links_ref, z_edge, o0_ref, o1_ref, l_ref, zs_ref, pq_ref, tile_ref, sems = refs
    copies = fetch(links_ref, l_ref, sems, 6)
    for copy in copies:
        copy.start()
    for tau in range(5):
        for half in range(2):
            at = tau * 2 + half
            zs_ref[pl.ds(tau * 4 + 2 + half, 54, stride=24), :] = z_edge[at].astype(F32)
            if 0 in planes:
                xs_ref[pl.ds(tau * 4 + half * 2 + 1, 54, stride=24), :] = x_edge[at].astype(F32)
    tile_ref[...] = jnp.zeros_like(tile_ref)
    for copy in copies:
        copy.wait()
    row = lax.broadcasted_iota(jnp.int32, (8, 128), 0)
    odd_x = row % 2 == 1
    high_z = row % 4 >= 2
    upper = lanes((8, 128)) >= LY

    def at_site(d, k):
        part = slice(8 * k, 8 * k + 8)
        return [
            [[l_ref[d, ri, i, j, part, :] for j in range(3)] for i in range(3)] for ri in range(2)
        ]

    def border(d, ri, i, j, k):
        row = (((d * 2 + ri) * 3 + i) * 3 + j) * 24 + 8 * k
        return slice(row, row + 8)

    def ahead(d, step, k):
        part = slice(8 * k, 8 * k + 8)

        def one(ri, i, j):
            if step == 3:
                if k < 2:
                    return l_ref[d, ri, i, j, 8 * k + 4 : 8 * k + 12, :]
                return pltpu.roll(l_ref[d, ri, i, j, 16:24, :], 4, 0)
            own = l_ref[d, ri, i, j, part, :]
            if step == 0:
                return jnp.where(odd_x, xs_ref[border(d - 1, ri, i, j, k), :], pltpu.roll(own, 7, 0))
            if step == 1:
                return shift_y(own, 1)
            edge = zs_ref[border(min(d, 2), ri, i, j, k), :]
            beyond = jnp.where(high_z, edge, pltpu.roll(own, 6, 0))
            return pltpu.roll(jnp.where(upper, own, beyond), LY, 1)

        return [[[one(ri, i, j) for j in range(3)] for i in range(3)] for ri in range(2)]

    def product(a, b, i, j):
        re = a[0][i][0] * b[0][0][j] - a[1][i][0] * b[1][0][j]
        im = a[0][i][0] * b[1][0][j] + a[1][i][0] * b[0][0][j]
        for m in (1, 2):
            re = re + a[0][i][m] * b[0][m][j] - a[1][i][m] * b[1][m][j]
            im = im + a[0][i][m] * b[1][m][j] + a[1][i][m] * b[0][m][j]
        return re, im

    for k in range(3):
        for p in planes:
            mu, nu = plane_pairs[p]
            c = 2 * (p - planes[0])
            u_mu = at_site(mu, k)
            u_nu = at_site(nu, k)
            nu_ahead = ahead(nu, mu, k)
            mu_ahead = ahead(mu, nu, k)
            re = im = None
            for i in range(3):
                for j in range(3):
                    r1, i1 = product(u_mu, nu_ahead, i, j)
                    r2, i2 = product(u_nu, mu_ahead, i, j)
                    re_term = r1 * r2 + i1 * i2
                    im_term = i1 * r2 - r1 * i2
                    re = re_term if re is None else re + re_term
                    im = im_term if im is None else im + im_term
            pq_ref[c, 8 * k : 8 * k + 8, :] = re
            pq_ref[c + 1, 8 * k : 8 * k + 8, :] = im
    for c in range(6):
        for lb in range(2):
            for x in range(2):
                row = 32 * x + 5 * c
                tile_ref[lb, row : row + 5, :] = pq_ref[c, pl.ds(2 * lb + x, 5, stride=4), :]
    o0_ref[0:64] = tile_ref[0].astype(BF16)
    o1_ref[0:64] = tile_ref[1].astype(BF16)


def join_body(*refs):
    right_ref, left_ref, own_ref = refs[4:]
    for i in range(4):
        right_ref[i, 0:64] = refs[i][0:64]
        right_ref[i, 64:96] = refs[i][96:128]
        left_ref[i, 0:32] = refs[i][64:96]
        left_ref[i, 32:64] = refs[i][0:32]
        own_ref[i] = refs[i][...]


def layer_body(
    x0_ref, z0_ref, pat_ref, par_ref, before_in, own_in, after_in, w_ref, small_ref, keep_ref, cot_ref,
    coef_ref, g_ref, a_ref, low_ref, rows_ref, before_ref, own_ref, after_ref,
):
    before_ref[...] = before_in[...].astype(F32)
    own_ref[...] = own_in[...].astype(F32)
    after_ref[...] = after_in[...].astype(F32)

    def piece(i, x, c, t):
        with_x = c < 6
        row = 5 * (c % 6) + t
        if x == 0 and not with_x:
            return jnp.zeros((4, 128), F32)
        if x < 2:
            ref, row = before_ref, row + (32 * x if with_x else 64)
        elif x < 4:
            ref, row = own_ref, row + 32 * (x - 2) + (0 if with_x else 64)
        else:
            ref, row = after_ref, row + (32 if with_x else 0)
        return ref[i, row : row + 4, :]

    lane = lanes((8, 128))
    upper = lane >= LY

    def crossed(by):
        y = lane % LY
        return (y >= LY - by) if by > 0 else (y < -by)

    for p in range(6):
        offsets = sorted({y for _, y in TILES[p]})
        for r in range(2):
            c = 2 * p + r
            for t in range(2):
                cols = []
                for i in range(4):
                    pieces = [piece(i, x, c, t) for x in range(5)]
                    cols.append([
                        [jnp.concatenate(pieces[x + 2 * h : x + 2 * h + 2], axis=0) for h in range(2)]
                        for x in range(2)
                    ])
                for x in range(2):
                    for y in offsets:
                        by = y - 2
                        made = []
                        for h in range(2):
                            plain, other = [], []
                            for i in range(4):
                                v = cols[i][x][h]
                                near = v if by == 0 else pltpu.roll(v, (-by) % 128, 1)
                                far = pltpu.roll(v, (LY - by) % 128, 1)
                                if by == 0:
                                    plain.append(near)
                                    other.append(far)
                                else:
                                    plain.append(jnp.where(crossed(by), far, near))
                                    other.append(jnp.where(crossed(by), near, far))
                            made.append([
                                plain[z // 2] if z % 2 == 0 else jnp.where(upper, other[z // 2 + 1], other[z // 2])
                                for z in range(6)
                            ])
                        both = [jnp.concatenate([u, v], axis=0).astype(BF16) for u, v in zip(*made)]
                        for n, (z, y_at) in enumerate(TILES[p]):
                            if y_at == y:
                                for lb in range(2):
                                    col = (t * 4 + x * 2 + lb) * 128
                                    a_ref[c, 16 * n : 16 * n + 16, col : col + 128] = both[z + 2 * lb]

    lane = lanes((1, 256))
    y_pos = lane % LY
    z_pos = z0_ref[0] + lane // LY
    bias_sum = jnp.zeros((64, 256), F32)
    head_sums = [jnp.zeros((64, 256), F32) for _ in range(4)]
    for t in range(2):
        for x in range(2):
            cols = slice((t * 2 + x) * 256, (t * 2 + x) * 256 + 256)
            acc = jnp.zeros((128, 256), F32)
            for c in range(12):
                size = SIZES[c // 2]
                acc = acc + jnp.dot(
                    w_ref[c, :, 0:size], a_ref[c, 0:size, cols], preferred_element_type=F32
                )
            hidden = acc[:64] + acc[64:] + small_ref[:, 4:5]
            act = jnp.tanh(hidden)
            act_grad = jnp.zeros((64, 256), F32)
            for mu in range(4):
                fixed = pat_ref[mu, 0] * (x0_ref[0] + x) + pat_ref[mu, 3] * t + par_ref[mu]
                summed = pat_ref[mu, 1] * y_pos + pat_ref[mu, 2] * z_pos + fixed
                active = ((summed & 1) == 0).astype(F32)
                weight = small_ref[:, mu : mu + 1]
                coef = active * jnp.sum(weight * act, axis=0, keepdims=True)
                coef_ref[mu, t, x : x + 1, :] = coef
                coef_grad = active * cot_ref[mu, t, x : x + 1, :] * (1.0 / math.sqrt(ROWS))
                act_grad = act_grad + weight * coef_grad
                head_sums[mu] = head_sums[mu] + act * coef_grad
            hidden_grad = act_grad * (1.0 - act * act)
            bias_sum = bias_sum + hidden_grad
            low_ref[:, cols] = hidden_grad.astype(BF16)

    spot = lanes((64, 128))
    small = jnp.zeros((64, 128), F32)
    for i, total in enumerate(head_sums + [bias_sum]):
        value = jnp.sum(total, axis=1, keepdims=True)
        rounded = value.astype(BF16).astype(F32)
        small = jnp.where(spot == i, rounded, jnp.where(spot == i + 8, value - rounded, small))

    def put(j, value):
        rows_ref[pl.ds(j, 64, stride=16), :] = value

    ends = [jnp.zeros((64, 128), F32), jnp.zeros((64, 128), F32)]
    for c in range(12):
        start, size = STARTS[c // 2], SIZES[c // 2]
        grad = lax.dot_general(low_ref[...], a_ref[c, 0:size, :], NT, preferred_element_type=F32)
        kept = jnp.dot(grad.astype(BF16), keep_ref[start : start + size, :], preferred_element_type=F32)
        put(c, kept[:, :128])
        end = kept[:, 128:]
        ends[c // 8] = ends[c // 8] + (pltpu.roll(end, 16 * (c % 8), 1) if c % 8 else end)
    put(12, ends[0])
    put(13, ends[1])
    put(14, small)
    put(15, jnp.zeros((64, 128), F32))
    g_ref[...] = rows_ref[...].reshape(64, 16, 128).astype(BF16)


def total_body(me_ref, in_ref, out_ref):
    total = jnp.sum(in_ref[...].astype(F32), axis=0)
    row = me_ref[0] * total.shape[0] + lax.broadcasted_iota(jnp.int32, total.shape, 0)
    lane = lanes(total.shape)
    whole = jnp.where(lane < 8, total + pltpu.roll(total, 120, 1), 0.0)
    rounded = whole.astype(BF16).astype(F32)
    rest = pltpu.roll(whole - rounded, 8, 1)
    total = jnp.where(row % 16 == 14, jnp.where(lane < 8, rounded, rest), total)
    out_ref[...] = jnp.broadcast_to(total.astype(BF16)[None], out_ref.shape)


def expand_body(g_ref, spread_ref, k_ref, b_ref, h_ref, rows_ref):
    rows_ref[...] = g_ref[...].astype(F32).reshape(1024, 128)

    def get(j):
        return rows_ref[pl.ds(j, 64, stride=16), :]

    ends = [get(12), get(13)]
    for c in range(12):
        p, r = c // 2, c % 2
        end = ends[c // 8]
        end = pltpu.roll(end, 128 - 16 * (c % 8), 1) if c % 8 else end
        kept = jnp.concatenate([get(c), end[:, :16]], axis=1).astype(BF16)
        full = jnp.dot(kept, spread_ref[p], preferred_element_type=F32)
        for leaf in range(4):
            k_ref[8 * p + 2 * leaf + r] = full[:, leaf * 128 : leaf * 128 + 81]
    small = get(14)
    small = (small + pltpu.roll(small, 120, 1)).T
    h_ref[...] = small[0:4]
    b_ref[...] = small[4:5]


def call(body, outs, scratch, *args, smem=0, away=(), name):
    def spec(i, away):
        return pl.BlockSpec(memory_space=pl.ANY if i in away else pltpu.VMEM)

    specs = [pl.BlockSpec(memory_space=pltpu.SMEM)] * smem
    return pl.pallas_call(
        body,
        out_shape=outs,
        in_specs=specs + [spec(i, away) for i in range(smem, len(args))],
        out_specs=(pl.BlockSpec(memory_space=pltpu.VMEM),) * len(outs),
        scratch_shapes=scratch,
        compiler_params=PARAMS,
        interpret=INTERPRET,
        name=name,
    )(*args)


def shifted(x, axis, by):
    count = lax.axis_size(axis)
    return lax.ppermute(x, axis, [(i, (i + by) % count) for i in range(count)])


def per_device(gauge_links, pattern, link_parity, conv_weight, conv_bias, head_weight, cotangent):
    shape = jax.ShapeDtypeStruct
    sems = pltpu.SemaphoreType.DMA
    edge = shape((10, 54, 128), BF16)
    links = pltpu.VMEM((5, 2, 3, 3, 24, 128), F32)
    x_edge, z_edge = call(
        send_body, (edge, edge), [links, sems((10,))], gauge_links, away=(0,), name="send"
    )
    next_x = shifted(x_edge, "xy", -1)
    next_z = shifted(z_edge, "gz", -1)
    keep = jnp.asarray(np.concatenate(KEEP), BF16)
    spread = jnp.asarray(SPREAD, BF16)
    weights, small = call(
        weights_body, (shape((12, 128, 256), BF16), shape((64, 8), F32)), [],
        conv_weight.transpose(1, 2, 0), spread, keep, head_weight.T, conv_bias[None], name="weights",
    )
    border = pltpu.VMEM((57 * 24, 128), F32)

    def loops(planes, *edges):
        half = shape((128 if 0 in planes else 64, 128), BF16)
        return call(
            functools.partial(loops_body, planes), (half, half),
            [links] + ([border, border] if 0 in planes else [border])
            + [pltpu.VMEM((8, 24, 128), F32), pltpu.VMEM((2, 64, 128), F32), sems((12,))],
            gauge_links, *edges, away=(0,), name="loops",
        )

    without_x = loops((3, 4, 5), next_z)
    next_x, weights, small, *without_x = lax.optimization_barrier((next_x, weights, small, *without_x))
    low_z, high_z = loops((0, 1, 2), next_z, next_x, *without_x)
    right_going, left_going, block = call(
        join_body, tuple(shape((4, n, 128), BF16) for n in (96, 64, 128)), [],
        shifted(high_z, "gz", 1), low_z, high_z, shifted(low_z, "gz", -1), name="join",
    )
    before_x = shifted(right_going, "xy", 1)
    after_x = shifted(left_going, "xy", -1)
    x_first = (lax.axis_index("xy") * 2).reshape(1)
    z_first = (lax.axis_index("gz") * 4).reshape(1)
    coefficients, grads = call(
        layer_body, (shape((4, 2, 2, 256), F32), shape((64, 16, 128), BF16)),
        [pltpu.VMEM((12, 256, 1024), BF16), pltpu.VMEM((64, 1024), BF16), pltpu.VMEM((1024, 128), F32)]
        + [pltpu.VMEM((4, n, 128), F32) for n in (96, 128, 64)],
        x_first, z_first, pattern, link_parity, before_x, block, after_x, weights, small, keep, cotangent,
        smem=4, name="layer",
    )
    both = ("xy", "gz")
    count = lax.axis_size(both)
    chunks = grads.reshape(count, 1024 // count, 128)
    chunks = lax.all_to_all(chunks, both, 0, 0, tiled=True)
    me = lax.axis_index(both).reshape(1)
    chunks = call(total_body, (shape(chunks.shape, BF16),), [], me, chunks, smem=1, name="total")[0]
    chunks = lax.all_to_all(chunks, both, 0, 0, tiled=True)
    grad_kernel, grad_bias, grad_head = call(
        expand_body, (shape((48, 64, 81), F32), shape((1, 64), F32), shape((4, 64), F32)),
        [pltpu.VMEM((1024, 128), F32)], chunks.reshape(64, 16, 128), spread, name="expand",
    )
    return coefficients, grad_kernel.transpose(2, 0, 1), grad_bias.reshape(64), grad_head.T


def solution(mesh):
    return jax.shard_map(
        per_device,
        mesh=mesh,
        in_specs=(
            P(None, None, None, None, None, "xy", "gz"),
            P(),
            P(),
            P(),
            P(),
            P(),
            P(None, None, "xy", "gz"),
        ),
        out_specs=(P(None, None, "xy", "gz"), P(), P(), P()),
        check_vma=False,
    )
```

```python
import math

import jax
import jax.numpy as jnp
import numpy as np
from jax import lax
from jax.experimental import pallas as pl
from jax.experimental.pallas import tpu as pltpu
from jax.sharding import PartitionSpec as P

LY = 64
ROWS = 1024
F32 = jnp.float32
BF16 = jnp.bfloat16

plane_pairs = ((0, 1), (0, 2), (0, 3), (1, 2), (1, 3), (2, 3))
INTERPRET = False
PARAMS = pltpu.CompilerParams(vmem_limit_bytes=56 * 2**20)


def lanes(shape):
    return lax.broadcasted_iota(jnp.int32, shape, len(shape) - 1)


def shift_y(x, by):
    if by == 0:
        return x
    axis = x.ndim - 1
    inner = pltpu.roll(x, (-by) % 128, axis)
    wrapped = pltpu.roll(x, (64 - by) % 128, axis)
    y = lanes(x.shape) % LY
    crossed = (y >= LY - by) if by > 0 else (y < -by)
    return jnp.where(crossed, wrapped, inner)


def plane_tables():
    tiles, keep, spread = [], [], np.zeros((6, 144, 512), np.float32)
    for p, pair in enumerate(plane_pairs):
        spans = [range(0 if d in pair else 1, 4) for d in range(4)]
        tiles.append([(z, y) for z in spans[2] for y in spans[1]])
        kept = {}
        table = np.zeros((16 * len(tiles[p]), 256), np.float32)
        for i, (z, y) in enumerate(tiles[p]):
            for x in spans[0]:
                for t in spans[3]:
                    table[16 * i + 4 * x + t, len(kept)] = 1
                    kept[x, y, z, t] = len(kept)
        keep.append(table)
        for leaf, back in enumerate(((), (pair[0],), (pair[1],), pair)):
            sx, sy, sz, st = (0 if d in back else 1 for d in range(4))
            for k in range(81):
                dx, dz, dt, dy = k // 27, k // 9 % 3, k // 3 % 3, k % 3
                spread[p, kept[dx + sx, dy + sy, dz + sz, dt + st], leaf * 128 + k] = 1
    return tiles, keep, spread


TILES, KEEP, SPREAD = plane_tables()
SIZES = [16 * len(t) for t in TILES]
STARTS = [sum(SIZES[:p]) for p in range(6)]
NT = (((1,), (1,)), ((), ()))


def weights_body(w_ref, spread_ref, keep_ref, head_ref, bias_ref, out_ref, small_ref):
    for p in range(6):
        table = keep_ref[STARTS[p] : STARTS[p] + SIZES[p], :]
        for r in range(2):
            full = jnp.zeros((64, 144), F32)
            for leaf in range(4):
                full = full + lax.dot_general(
                    w_ref[8 * p + 2 * leaf + r], spread_ref[p, :, leaf * 128 : leaf * 128 + 81], NT,
                    preferred_element_type=F32,
                )
            high = full.astype(BF16)
            low = (full - high.astype(F32)).astype(BF16)
            both = jnp.concatenate([high, low], axis=0)
            out_ref[2 * p + r, :, 0 : SIZES[p]] = lax.dot_general(
                both, table[:, :144], NT, preferred_element_type=F32
            ).astype(BF16)
    small_ref[...] = jnp.concatenate([head_ref[...], bias_ref[...], jnp.zeros((3, 64), F32)], axis=0).T


def place(c, x):
    return 64 + 32 * (c // 6) + 5 * (c % 6) if x == 1 else (32 + 5 * c if c < 6 else 5 * (c - 6))


def group(g):
    return slice(32 * g, 32 * g + 32)


def run(copies):
    for copy in copies:
        copy.start()
    for copy in copies:
        copy.wait()


def fetch(links_ref, l_ref, sems, slices):
    return [
        pltpu.make_async_copy(
            links_ref.at[:, :, :, :, tau, :, lb * 128 : lb * 128 + 128],
            l_ref.at[0:4, :, :, :, tau * 4 + lb * 2 : tau * 4 + lb * 2 + 2, :],
            sems.at[tau * 2 + lb],
        )
        for tau in range(slices)
        for lb in range(2)
    ]


def send_body(links_ref, x_ref, z_ref, l_ref, sems):
    run(fetch(links_ref, l_ref, sems, 5))
    rows_ref = l_ref.reshape(90 * 24, 128)
    for tau in range(5):
        for half in range(2):
            at = tau * 2 + half
            x_ref[at] = rows_ref[pl.ds(18 * 24 + tau * 4 + half * 2, 54, stride=24), :].astype(BF16)
            row = tau * 4 + half
            first = rows_ref[pl.ds(row, 36, stride=24), :]
            last = rows_ref[pl.ds(54 * 24 + row, 18, stride=24), :]
            z_ref[at] = jnp.concatenate([first, last], axis=0).astype(BF16)


def loops_body(
    links_ref, xh_ref, zh_ref, o0_ref, o1_ref, l_ref, xs_ref, zs_ref, pq_ref, tile_ref, sems
):
    copies = fetch(links_ref, l_ref, sems, 6)
    for copy in copies:
        copy.start()
    for tau in range(5):
        for half in range(2):
            at = tau * 2 + half
            xs_ref[pl.ds(tau * 4 + half * 2 + 1, 54, stride=24), :] = xh_ref[at].astype(F32)
            zs_ref[pl.ds(tau * 4 + 2 + half, 54, stride=24), :] = zh_ref[at].astype(F32)
    tile_ref[...] = jnp.zeros_like(tile_ref)
    for copy in copies:
        copy.wait()
    row = lax.broadcasted_iota(jnp.int32, (8, 128), 0)
    odd_x = row % 2 == 1
    high_z = row % 4 >= 2
    upper = lanes((8, 128)) >= LY

    def at_site(d, k):
        part = slice(8 * k, 8 * k + 8)
        return [
            [[l_ref[d, ri, i, j, part, :] for j in range(3)] for i in range(3)] for ri in range(2)
        ]

    def border(d, ri, i, j, k):
        row = (((d * 2 + ri) * 3 + i) * 3 + j) * 24 + 8 * k
        return slice(row, row + 8)

    def ahead(d, step, k):
        part = slice(8 * k, 8 * k + 8)

        def one(ri, i, j):
            if step == 3:
                if k < 2:
                    return l_ref[d, ri, i, j, 8 * k + 4 : 8 * k + 12, :]
                return pltpu.roll(l_ref[d, ri, i, j, 16:24, :], 4, 0)
            own = l_ref[d, ri, i, j, part, :]
            if step == 0:
                return jnp.where(odd_x, xs_ref[border(d - 1, ri, i, j, k), :], pltpu.roll(own, 7, 0))
            if step == 1:
                return shift_y(own, 1)
            edge = zs_ref[border(min(d, 2), ri, i, j, k), :]
            beyond = jnp.where(high_z, edge, pltpu.roll(own, 6, 0))
            return pltpu.roll(jnp.where(upper, own, beyond), LY, 1)

        return [[[one(ri, i, j) for j in range(3)] for i in range(3)] for ri in range(2)]

    def product(a, b, i, j):
        re = a[0][i][0] * b[0][0][j] - a[1][i][0] * b[1][0][j]
        im = a[0][i][0] * b[1][0][j] + a[1][i][0] * b[0][0][j]
        for m in (1, 2):
            re = re + a[0][i][m] * b[0][m][j] - a[1][i][m] * b[1][m][j]
            im = im + a[0][i][m] * b[1][m][j] + a[1][i][m] * b[0][m][j]
        return re, im

    for k in range(3):
        for p, (mu, nu) in enumerate(plane_pairs):
            u_mu = at_site(mu, k)
            u_nu = at_site(nu, k)
            nu_ahead = ahead(nu, mu, k)
            mu_ahead = ahead(mu, nu, k)
            re = im = None
            for i in range(3):
                for j in range(3):
                    r1, i1 = product(u_mu, nu_ahead, i, j)
                    r2, i2 = product(u_nu, mu_ahead, i, j)
                    re_term = r1 * r2 + i1 * i2
                    im_term = i1 * r2 - r1 * i2
                    re = re_term if re is None else re + re_term
                    im = im_term if im is None else im + im_term
            pq_ref[2 * p, 8 * k : 8 * k + 8, :] = re
            pq_ref[2 * p + 1, 8 * k : 8 * k + 8, :] = im
    for c in range(12):
        for lb, o_ref in enumerate((o0_ref, o1_ref)):
            for x in range(2):
                row = place(c, x)
                tile_ref[lb, row : row + 5, :] = pq_ref[c, pl.ds(2 * lb + x, 5, stride=4), :]
    o0_ref[...] = tile_ref[0].astype(BF16)
    o1_ref[...] = tile_ref[1].astype(BF16)


def layer_body(
    odd_ref, x0_ref, z0_ref, pat_ref, par_ref, second_in, own_in, first_in, w_ref, small_ref, keep_ref, cot_ref,
    coef_ref, g_ref, a_ref, low_ref, rows_ref, left_ref, own_ref, right_ref,
):
    odd = odd_ref[0] == 1
    own_ref[...] = own_in[...].astype(F32)
    left_ref[...] = jnp.where(odd, second_in[:, 32:].astype(F32), first_in[:, 32:].astype(F32))
    right_ref[...] = jnp.where(odd, first_in[:, :64].astype(F32), second_in[:, :64].astype(F32))

    def piece(i, x, c, t):
        if x == 0 and c >= 6:
            return jnp.zeros((4, 128), F32)
        if x < 2:
            ref, row = left_ref, place(c, x) - 32
        elif x < 4:
            ref, row = own_ref, place(c, x - 2)
        else:
            ref, row = right_ref, place(c, 0)
        return ref[i, row + t : row + t + 4, :]

    lane = lanes((8, 128))
    upper = lane >= LY

    def crossed(by):
        y = lane % LY
        return (y >= LY - by) if by > 0 else (y < -by)

    for p in range(6):
        offsets = sorted({y for _, y in TILES[p]})
        for r in range(2):
            c = 2 * p + r
            for t in range(2):
                cols = []
                for i in range(4):
                    pieces = [piece(i, x, c, t) for x in range(5)]
                    cols.append([
                        [jnp.concatenate(pieces[x + 2 * h : x + 2 * h + 2], axis=0) for h in range(2)]
                        for x in range(2)
                    ])
                for x in range(2):
                    for y in offsets:
                        by = y - 2
                        made = []
                        for h in range(2):
                            plain, other = [], []
                            for i in range(4):
                                v = cols[i][x][h]
                                near = v if by == 0 else pltpu.roll(v, (-by) % 128, 1)
                                far = pltpu.roll(v, (LY - by) % 128, 1)
                                if by == 0:
                                    plain.append(near)
                                    other.append(far)
                                else:
                                    plain.append(jnp.where(crossed(by), far, near))
                                    other.append(jnp.where(crossed(by), near, far))
                            made.append([
                                plain[z // 2] if z % 2 == 0 else jnp.where(upper, other[z // 2 + 1], other[z // 2])
                                for z in range(6)
                            ])
                        both = [jnp.concatenate([u, v], axis=0).astype(BF16) for u, v in zip(*made)]
                        for n, (z, y_at) in enumerate(TILES[p]):
                            if y_at == y:
                                for lb in range(2):
                                    col = (t * 4 + x * 2 + lb) * 128
                                    a_ref[c, 16 * n : 16 * n + 16, col : col + 128] = both[z + 2 * lb]

    lane = lanes((1, 256))
    y_pos = lane % LY
    z_pos = z0_ref[0] + lane // LY
    bias_sum = jnp.zeros((64, 256), F32)
    head_sums = [jnp.zeros((64, 256), F32) for _ in range(4)]
    for t in range(2):
        for x in range(2):
            cols = slice((t * 2 + x) * 256, (t * 2 + x) * 256 + 256)
            acc = jnp.zeros((128, 256), F32)
            for c in range(12):
                size = SIZES[c // 2]
                acc = acc + jnp.dot(
                    w_ref[c, :, 0:size], a_ref[c, 0:size, cols], preferred_element_type=F32
                )
            hidden = acc[:64] + acc[64:] + small_ref[:, 4:5]
            act = jnp.tanh(hidden)
            act_grad = jnp.zeros((64, 256), F32)
            for mu in range(4):
                fixed = pat_ref[mu, 0] * (x0_ref[0] + x) + pat_ref[mu, 3] * t + par_ref[mu]
                summed = pat_ref[mu, 1] * y_pos + pat_ref[mu, 2] * z_pos + fixed
                active = ((summed & 1) == 0).astype(F32)
                weight = small_ref[:, mu : mu + 1]
                coef = active * jnp.sum(weight * act, axis=0, keepdims=True)
                coef_ref[mu, t, x : x + 1, :] = coef
                coef_grad = active * cot_ref[mu, t, x : x + 1, :] * (1.0 / math.sqrt(ROWS))
                act_grad = act_grad + weight * coef_grad
                head_sums[mu] = head_sums[mu] + act * coef_grad
            hidden_grad = act_grad * (1.0 - act * act)
            bias_sum = bias_sum + hidden_grad
            low_ref[:, cols] = hidden_grad.astype(BF16)

    spot = lanes((64, 128))
    small = jnp.zeros((64, 128), F32)
    for i, total in enumerate(head_sums + [bias_sum]):
        value = jnp.sum(total, axis=1, keepdims=True)
        rounded = value.astype(BF16).astype(F32)
        small = jnp.where(spot == i, rounded, jnp.where(spot == i + 8, value - rounded, small))

    def put(j, value):
        rows_ref[pl.ds(j, 64, stride=16), :] = value

    ends = [jnp.zeros((64, 128), F32), jnp.zeros((64, 128), F32)]
    for c in range(12):
        start, size = STARTS[c // 2], SIZES[c // 2]
        grad = lax.dot_general(low_ref[...], a_ref[c, 0:size, :], NT, preferred_element_type=F32)
        kept = jnp.dot(grad.astype(BF16), keep_ref[start : start + size, :], preferred_element_type=F32)
        put(c, kept[:, :128])
        end = kept[:, 128:]
        ends[c // 8] = ends[c // 8] + (pltpu.roll(end, 16 * (c % 8), 1) if c % 8 else end)
    put(12, ends[0])
    put(13, ends[1])
    put(14, small)
    put(15, jnp.zeros((64, 128), F32))
    g_ref[...] = rows_ref[...].reshape(64, 16, 128).astype(BF16)


def total_body(me_ref, in_ref, out_ref):
    total = jnp.sum(in_ref[...].astype(F32), axis=0)
    row = me_ref[0] * total.shape[0] + lax.broadcasted_iota(jnp.int32, total.shape, 0)
    lane = lanes(total.shape)
    whole = jnp.where(lane < 8, total + pltpu.roll(total, 120, 1), 0.0)
    rounded = whole.astype(BF16).astype(F32)
    rest = pltpu.roll(whole - rounded, 8, 1)
    total = jnp.where(row % 16 == 14, jnp.where(lane < 8, rounded, rest), total)
    out_ref[...] = jnp.broadcast_to(total.astype(BF16)[None], out_ref.shape)


def expand_body(g_ref, spread_ref, k_ref, b_ref, h_ref, rows_ref):
    rows_ref[...] = g_ref[...].astype(F32).reshape(1024, 128)

    def get(j):
        return rows_ref[pl.ds(j, 64, stride=16), :]

    ends = [get(12), get(13)]
    for c in range(12):
        p, r = c // 2, c % 2
        end = ends[c // 8]
        end = pltpu.roll(end, 128 - 16 * (c % 8), 1) if c % 8 else end
        kept = jnp.concatenate([get(c), end[:, :16]], axis=1).astype(BF16)
        full = jnp.dot(kept, spread_ref[p], preferred_element_type=F32)
        for leaf in range(4):
            k_ref[8 * p + 2 * leaf + r] = full[:, leaf * 128 : leaf * 128 + 81]
    small = get(14)
    small = (small + pltpu.roll(small, 120, 1)).T
    h_ref[...] = small[0:4]
    b_ref[...] = small[4:5]


def call(body, outs, scratch, *args, smem=0, away=(), name):
    def spec(i, away):
        return pl.BlockSpec(memory_space=pl.ANY if i in away else pltpu.VMEM)

    specs = [pl.BlockSpec(memory_space=pltpu.SMEM)] * smem
    return pl.pallas_call(
        body,
        out_shape=outs,
        in_specs=specs + [spec(i, away) for i in range(smem, len(args))],
        out_specs=(pl.BlockSpec(memory_space=pltpu.VMEM),) * len(outs),
        scratch_shapes=scratch,
        compiler_params=PARAMS,
        interpret=INTERPRET,
        name=name,
    )(*args)


def shifted(x, axis, by):
    count = lax.axis_size(axis)
    return lax.ppermute(x, axis, [(i, (i + by) % count) for i in range(count)])


def swapped(x, axis, least):
    count = lax.axis_size(axis)
    pairs = [(i % count, (i + 1) % count) for i in range(least, least + count, 2)]
    return lax.ppermute(x, axis, pairs + [(j, i) for i, j in pairs])


def per_device(gauge_links, pattern, link_parity, conv_weight, conv_bias, head_weight, cotangent):
    shape = jax.ShapeDtypeStruct
    sems = pltpu.SemaphoreType.DMA
    edge = shape((10, 54, 128), BF16)
    links = pltpu.VMEM((5, 2, 3, 3, 24, 128), F32)
    x_edge, z_edge = call(
        send_body, (edge, edge), [links, sems((10,))], gauge_links, away=(0,), name="send"
    )
    next_x = shifted(x_edge, "xy", -1)
    next_z = shifted(z_edge, "gz", -1)
    keep = jnp.asarray(np.concatenate(KEEP), BF16)
    spread = jnp.asarray(SPREAD, BF16)
    weights, small = call(
        weights_body, (shape((12, 128, 256), BF16), shape((64, 8), F32)), [],
        conv_weight.transpose(1, 2, 0), spread, keep, head_weight.T, conv_bias[None], name="weights",
    )
    next_x, next_z, weights, small = lax.optimization_barrier((next_x, next_z, weights, small))
    half = shape((128, 128), BF16)
    odd = (lax.axis_index("xy") % 2).reshape(1)
    border = pltpu.VMEM((57 * 24, 128), F32)
    low_z, high_z = call(
        loops_body, (half, half),
        [links, border, border, pltpu.VMEM((14, 24, 128), F32), pltpu.VMEM((2, 128, 128), F32), sems((12,))],
        gauge_links, next_x, next_z, away=(0,), name="loops",
    )
    before_z = shifted(high_z, "gz", 1)
    after_z = shifted(low_z, "gz", -1)
    block = jnp.stack([before_z, low_z, high_z, after_z])
    first = swapped(block, "xy", 1)
    second = swapped(block, "xy", 0)
    x_first = (lax.axis_index("xy") * 2).reshape(1)
    z_first = (lax.axis_index("gz") * 4).reshape(1)
    coefficients, grads = call(
        layer_body, (shape((4, 2, 2, 256), F32), shape((64, 16, 128), BF16)),
        [pltpu.VMEM((12, 256, 1024), BF16), pltpu.VMEM((64, 1024), BF16), pltpu.VMEM((1024, 128), F32)]
        + [pltpu.VMEM((4, n, 128), F32) for n in (96, 128, 64)],
        odd, x_first, z_first, pattern, link_parity, second, block, first, weights, small, keep, cotangent,
        smem=5, name="layer",
    )
    both = ("xy", "gz")
    count = lax.axis_size(both)
    chunks = grads.reshape(count, 1024 // count, 128)
    chunks = lax.all_to_all(chunks, both, 0, 0, tiled=True)
    me = lax.axis_index(both).reshape(1)
    chunks = call(total_body, (shape(chunks.shape, BF16),), [], me, chunks, smem=1, name="total")[0]
    chunks = lax.all_to_all(chunks, both, 0, 0, tiled=True)
    grad_kernel, grad_bias, grad_head = call(
        expand_body, (shape((48, 64, 81), F32), shape((1, 64), F32), shape((4, 64), F32)),
        [pltpu.VMEM((1024, 128), F32)], chunks.reshape(64, 16, 128), spread, name="expand",
    )
    return coefficients, grad_kernel.transpose(2, 0, 1), grad_bias.reshape(64), grad_head.T


def solution(mesh):
    return jax.shard_map(
        per_device,
        mesh=mesh,
        in_specs=(
            P(None, None, None, None, None, "xy", "gz"),
            P(),
            P(),
            P(),
            P(),
            P(),
            P(None, None, "xy", "gz"),
        ),
        out_specs=(P(None, None, "xy", "gz"), P(), P(), P()),
        check_vma=False,
    )
```

```python
import math

import jax
import jax.numpy as jnp
import numpy as np
from jax import lax
from jax.experimental import pallas as pl
from jax.experimental.pallas import tpu as pltpu
from jax.sharding import PartitionSpec as P

LY = 64
ROWS = 1024
F32 = jnp.float32
BF16 = jnp.bfloat16

plane_pairs = ((0, 1), (0, 2), (0, 3), (1, 2), (1, 3), (2, 3))
INTERPRET = False
PARAMS = pltpu.CompilerParams(vmem_limit_bytes=56 * 2**20)


def lanes(shape):
    return lax.broadcasted_iota(jnp.int32, shape, len(shape) - 1)


def shift_y(x, by):
    if by == 0:
        return x
    axis = x.ndim - 1
    inner = pltpu.roll(x, (-by) % 128, axis)
    wrapped = pltpu.roll(x, (64 - by) % 128, axis)
    y = lanes(x.shape) % LY
    crossed = (y >= LY - by) if by > 0 else (y < -by)
    return jnp.where(crossed, wrapped, inner)


def plane_tables():
    tiles, keep, spread = [], [], np.zeros((6, 144, 512), np.float32)
    for p, pair in enumerate(plane_pairs):
        spans = [range(0 if d in pair else 1, 4) for d in range(4)]
        tiles.append([(z, y) for z in spans[2] for y in spans[1]])
        kept = {}
        table = np.zeros((16 * len(tiles[p]), 256), np.float32)
        for i, (z, y) in enumerate(tiles[p]):
            for x in spans[0]:
                for t in spans[3]:
                    table[16 * i + 4 * x + t, len(kept)] = 1
                    kept[x, y, z, t] = len(kept)
        keep.append(table)
        for leaf, back in enumerate(((), (pair[0],), (pair[1],), pair)):
            sx, sy, sz, st = (0 if d in back else 1 for d in range(4))
            for k in range(81):
                dx, dz, dt, dy = k // 27, k // 9 % 3, k // 3 % 3, k % 3
                spread[p, kept[dx + sx, dy + sy, dz + sz, dt + st], leaf * 128 + k] = 1
    return tiles, keep, spread


TILES, KEEP, SPREAD = plane_tables()
SIZES = [16 * len(t) for t in TILES]
STARTS = [sum(SIZES[:p]) for p in range(6)]
NT = (((1,), (1,)), ((), ()))


def weights_body(w_ref, spread_ref, keep_ref, head_ref, bias_ref, out_ref, small_ref):
    for p in range(6):
        table = keep_ref[STARTS[p] : STARTS[p] + SIZES[p], :]
        for r in range(2):
            full = jnp.zeros((64, 144), F32)
            for leaf in range(4):
                full = full + lax.dot_general(
                    w_ref[8 * p + 2 * leaf + r], spread_ref[p, :, leaf * 128 : leaf * 128 + 81], NT,
                    preferred_element_type=F32,
                )
            high = full.astype(BF16)
            low = (full - high.astype(F32)).astype(BF16)
            both = jnp.concatenate([high, low], axis=0)
            out_ref[2 * p + r, :, 0 : SIZES[p]] = lax.dot_general(
                both, table[:, :144], NT, preferred_element_type=F32
            ).astype(BF16)
    small_ref[...] = jnp.concatenate([head_ref[...], bias_ref[...], jnp.zeros((3, 64), F32)], axis=0).T


def place(c, x):
    return 64 + 32 * (c // 6) + 5 * (c % 6) if x == 1 else (32 + 5 * c if c < 6 else 5 * (c - 6))


def fetch(links_ref, l_ref, sems, slices):
    return [
        pltpu.make_async_copy(
            links_ref.at[:, :, :, :, tau, :, lb * 128 : lb * 128 + 128],
            l_ref.at[0:4, :, :, :, tau * 4 + lb * 2 : tau * 4 + lb * 2 + 2, :],
            sems.at[tau * 2 + lb],
        )
        for tau in range(slices)
        for lb in range(2)
    ]


def send_body(links_ref, x_ref, z_ref, l_ref, sems):
    copies = fetch(links_ref, l_ref, sems, 5)
    for copy in copies:
        copy.start()
    rows_ref = l_ref.reshape(90 * 24, 128)
    for tau in range(5):
        for copy in copies[2 * tau : 2 * tau + 2]:
            copy.wait()
        for half in range(2):
            at = tau * 2 + half
            x_ref[at] = rows_ref[pl.ds(18 * 24 + tau * 4 + half * 2, 54, stride=24), :].astype(BF16)
            row = tau * 4 + half
            first = rows_ref[pl.ds(row, 36, stride=24), :]
            last = rows_ref[pl.ds(54 * 24 + row, 18, stride=24), :]
            z_ref[at] = jnp.concatenate([first, last], axis=0).astype(BF16)


def loops_body(
    odd_ref, links_ref, xh_ref, zh_ref, o0_ref, o1_ref, l_ref, xs_ref, zs_ref, pq_ref, tile_ref, sems
):
    copies = fetch(links_ref, l_ref, sems, 6)
    for copy in copies:
        copy.start()
    for tau in range(5):
        for half in range(2):
            at = tau * 2 + half
            xs_ref[pl.ds(tau * 4 + half * 2 + 1, 54, stride=24), :] = xh_ref[at].astype(F32)
            zs_ref[pl.ds(tau * 4 + 2 + half, 54, stride=24), :] = zh_ref[at].astype(F32)
    tile_ref[...] = jnp.zeros_like(tile_ref)
    row = lax.broadcasted_iota(jnp.int32, (8, 128), 0)
    odd_x = row % 2 == 1
    high_z = row % 4 >= 2
    upper = lanes((8, 128)) >= LY

    def at_site(d, k):
        part = slice(8 * k, 8 * k + 8)
        return [
            [[l_ref[d, ri, i, j, part, :] for j in range(3)] for i in range(3)] for ri in range(2)
        ]

    def border(d, ri, i, j, k):
        row = (((d * 2 + ri) * 3 + i) * 3 + j) * 24 + 8 * k
        return slice(row, row + 8)

    def ahead(d, step, k):
        part = slice(8 * k, 8 * k + 8)

        def one(ri, i, j):
            if step == 3:
                if k < 2:
                    return l_ref[d, ri, i, j, 8 * k + 4 : 8 * k + 12, :]
                return pltpu.roll(l_ref[d, ri, i, j, 16:24, :], 4, 0)
            own = l_ref[d, ri, i, j, part, :]
            if step == 0:
                return jnp.where(odd_x, xs_ref[border(d - 1, ri, i, j, k), :], pltpu.roll(own, 7, 0))
            if step == 1:
                return shift_y(own, 1)
            edge = zs_ref[border(min(d, 2), ri, i, j, k), :]
            beyond = jnp.where(high_z, edge, pltpu.roll(own, 6, 0))
            return pltpu.roll(jnp.where(upper, own, beyond), LY, 1)

        return [[[one(ri, i, j) for j in range(3)] for i in range(3)] for ri in range(2)]

    def product(a, b, i, j):
        re = a[0][i][0] * b[0][0][j] - a[1][i][0] * b[1][0][j]
        im = a[0][i][0] * b[1][0][j] + a[1][i][0] * b[0][0][j]
        for m in (1, 2):
            re = re + a[0][i][m] * b[0][m][j] - a[1][i][m] * b[1][m][j]
            im = im + a[0][i][m] * b[1][m][j] + a[1][i][m] * b[0][m][j]
        return re, im

    for k in range(3):
        for copy in (copies[:6], copies[6:10], copies[10:])[k]:
            copy.wait()
        for p, (mu, nu) in enumerate(plane_pairs):
            u_mu = at_site(mu, k)
            u_nu = at_site(nu, k)
            nu_ahead = ahead(nu, mu, k)
            mu_ahead = ahead(mu, nu, k)
            re = im = None
            for i in range(3):
                for j in range(3):
                    r1, i1 = product(u_mu, nu_ahead, i, j)
                    r2, i2 = product(u_nu, mu_ahead, i, j)
                    re_term = r1 * r2 + i1 * i2
                    im_term = i1 * r2 - r1 * i2
                    re = re_term if re is None else re + re_term
                    im = im_term if im is None else im + im_term
            pq_ref[2 * p, 8 * k : 8 * k + 8, :] = re
            pq_ref[2 * p + 1, 8 * k : 8 * k + 8, :] = im
    for c in range(12):
        for lb, o_ref in enumerate((o0_ref, o1_ref)):
            for x in range(2):
                row = place(c, x)
                tile_ref[lb, row : row + 5, :] = pq_ref[c, pl.ds(2 * lb + x, 5, stride=4), :]
    odd = odd_ref[0] == 1
    o0_ref[...] = jnp.where(odd, tile_ref[1], tile_ref[0]).astype(BF16)
    o1_ref[...] = jnp.where(odd, tile_ref[0], tile_ref[1]).astype(BF16)


def layer_body(
    odd_ref, x0_ref, z0_ref, pat_ref, par_ref, second_in, own_in, first_in, w_ref, small_ref, keep_ref, cot_ref,
    coef_ref, g_ref, a_ref, low_ref, rows_ref, left_ref, own_ref, right_ref,
):
    odd = odd_ref[0] == 1
    turned = lax.rem(lax.div(z0_ref[0], 4), 2) == 1
    for i in range(4):

        def pick(ref, part):
            return jnp.where(turned, ref[3 - i, part].astype(F32), ref[i, part].astype(F32))

        own_ref[i] = pick(own_in, slice(0, 128))
        left_ref[i] = jnp.where(odd, pick(second_in, slice(32, 128)), pick(first_in, slice(32, 128)))
        right_ref[i] = jnp.where(odd, pick(first_in, slice(0, 64)), pick(second_in, slice(0, 64)))

    def piece(i, x, c, t):
        if x == 0 and c >= 6:
            return jnp.zeros((4, 128), F32)
        if x < 2:
            ref, row = left_ref, place(c, x) - 32
        elif x < 4:
            ref, row = own_ref, place(c, x - 2)
        else:
            ref, row = right_ref, place(c, 0)
        return ref[i, row + t : row + t + 4, :]

    lane = lanes((8, 128))
    upper = lane >= LY

    def crossed(by):
        y = lane % LY
        return (y >= LY - by) if by > 0 else (y < -by)

    for p in range(6):
        offsets = sorted({y for _, y in TILES[p]})
        for r in range(2):
            c = 2 * p + r
            for t in range(2):
                cols = []
                for i in range(4):
                    pieces = [piece(i, x, c, t) for x in range(5)]
                    cols.append([
                        [jnp.concatenate(pieces[x + 2 * h : x + 2 * h + 2], axis=0) for h in range(2)]
                        for x in range(2)
                    ])
                for x in range(2):
                    for y in offsets:
                        by = y - 2
                        made = []
                        for h in range(2):
                            plain, other = [], []
                            for i in range(4):
                                v = cols[i][x][h]
                                near = v if by == 0 else pltpu.roll(v, (-by) % 128, 1)
                                far = pltpu.roll(v, (LY - by) % 128, 1)
                                if by == 0:
                                    plain.append(near)
                                    other.append(far)
                                else:
                                    plain.append(jnp.where(crossed(by), far, near))
                                    other.append(jnp.where(crossed(by), near, far))
                            made.append([
                                plain[z // 2] if z % 2 == 0 else jnp.where(upper, other[z // 2 + 1], other[z // 2])
                                for z in range(6)
                            ])
                        both = [jnp.concatenate([u, v], axis=0).astype(BF16) for u, v in zip(*made)]
                        for n, (z, y_at) in enumerate(TILES[p]):
                            if y_at == y:
                                for lb in range(2):
                                    col = (t * 4 + x * 2 + lb) * 128
                                    a_ref[c, 16 * n : 16 * n + 16, col : col + 128] = both[z + 2 * lb]

    lane = lanes((1, 256))
    y_pos = lane % LY
    z_pos = z0_ref[0] + lane // LY
    bias_sum = jnp.zeros((64, 256), F32)
    head_sums = [jnp.zeros((64, 256), F32) for _ in range(4)]
    for t in range(2):
        for x in range(2):
            cols = slice((t * 2 + x) * 256, (t * 2 + x) * 256 + 256)
            acc = jnp.zeros((128, 256), F32)
            for c in range(12):
                size = SIZES[c // 2]
                acc = acc + jnp.dot(
                    w_ref[c, :, 0:size], a_ref[c, 0:size, cols], preferred_element_type=F32
                )
            hidden = acc[:64] + acc[64:] + small_ref[:, 4:5]
            act = jnp.tanh(hidden)
            act_grad = jnp.zeros((64, 256), F32)
            for mu in range(4):
                fixed = pat_ref[mu, 0] * (x0_ref[0] + x) + pat_ref[mu, 3] * t + par_ref[mu]
                summed = pat_ref[mu, 1] * y_pos + pat_ref[mu, 2] * z_pos + fixed
                active = ((summed & 1) == 0).astype(F32)
                weight = small_ref[:, mu : mu + 1]
                coef = active * jnp.sum(weight * act, axis=0, keepdims=True)
                coef_ref[mu, t, x : x + 1, :] = coef
                coef_grad = active * cot_ref[mu, t, x : x + 1, :] * (1.0 / math.sqrt(ROWS))
                act_grad = act_grad + weight * coef_grad
                head_sums[mu] = head_sums[mu] + act * coef_grad
            hidden_grad = act_grad * (1.0 - act * act)
            bias_sum = bias_sum + hidden_grad
            low_ref[:, cols] = hidden_grad.astype(BF16)

    spot = lanes((64, 128))
    small = jnp.zeros((64, 128), F32)
    for i, total in enumerate(head_sums + [bias_sum]):
        value = jnp.sum(total, axis=1, keepdims=True)
        rounded = value.astype(BF16).astype(F32)
        small = jnp.where(spot == i, rounded, jnp.where(spot == i + 8, value - rounded, small))

    def put(j, value):
        rows_ref[pl.ds(j, 64, stride=16), :] = value

    ends = [jnp.zeros((64, 128), F32), jnp.zeros((64, 128), F32)]
    for c in range(12):
        start, size = STARTS[c // 2], SIZES[c // 2]
        grad = lax.dot_general(low_ref[...], a_ref[c, 0:size, :], NT, preferred_element_type=F32)
        kept = jnp.dot(grad.astype(BF16), keep_ref[start : start + size, :], preferred_element_type=F32)
        put(c, kept[:, :128])
        end = kept[:, 128:]
        ends[c // 8] = ends[c // 8] + (pltpu.roll(end, 16 * (c % 8), 1) if c % 8 else end)
    put(12, ends[0])
    put(13, ends[1])
    put(14, small)
    put(15, jnp.zeros((64, 128), F32))
    g_ref[...] = rows_ref[...].reshape(64, 16, 128).astype(BF16)


def total_body(me_ref, in_ref, out_ref):
    total = jnp.sum(in_ref[...].astype(F32), axis=0)
    row = me_ref[0] * total.shape[0] + lax.broadcasted_iota(jnp.int32, total.shape, 0)
    lane = lanes(total.shape)
    whole = jnp.where(lane < 8, total + pltpu.roll(total, 120, 1), 0.0)
    rounded = whole.astype(BF16).astype(F32)
    rest = pltpu.roll(whole - rounded, 8, 1)
    total = jnp.where(row % 16 == 14, jnp.where(lane < 8, rounded, rest), total)
    out_ref[...] = jnp.broadcast_to(total.astype(BF16)[None], out_ref.shape)


def expand_body(g_ref, spread_ref, k_ref, b_ref, h_ref, rows_ref):
    rows_ref[...] = g_ref[...].astype(F32).reshape(1024, 128)

    def get(j):
        return rows_ref[pl.ds(j, 64, stride=16), :]

    ends = [get(12), get(13)]
    for c in range(12):
        p, r = c // 2, c % 2
        end = ends[c // 8]
        end = pltpu.roll(end, 128 - 16 * (c % 8), 1) if c % 8 else end
        kept = jnp.concatenate([get(c), end[:, :16]], axis=1).astype(BF16)
        full = jnp.dot(kept, spread_ref[p], preferred_element_type=F32)
        for leaf in range(4):
            k_ref[8 * p + 2 * leaf + r] = full[:, leaf * 128 : leaf * 128 + 81]
    small = get(14)
    small = (small + pltpu.roll(small, 120, 1)).T
    h_ref[...] = small[0:4]
    b_ref[...] = small[4:5]


def call(body, outs, scratch, *args, smem=0, away=(), name):
    def spec(i, away):
        return pl.BlockSpec(memory_space=pl.ANY if i in away else pltpu.VMEM)

    specs = [pl.BlockSpec(memory_space=pltpu.SMEM)] * smem
    return pl.pallas_call(
        body,
        out_shape=outs,
        in_specs=specs + [spec(i, away) for i in range(smem, len(args))],
        out_specs=(pl.BlockSpec(memory_space=pltpu.VMEM),) * len(outs),
        scratch_shapes=scratch,
        compiler_params=PARAMS,
        interpret=INTERPRET,
        name=name,
    )(*args)


def shifted(x, axis, by):
    count = lax.axis_size(axis)
    return lax.ppermute(x, axis, [(i, (i + by) % count) for i in range(count)])


def swapped(x, axis, least):
    count = lax.axis_size(axis)
    pairs = [(i % count, (i + 1) % count) for i in range(least, least + count, 2)]
    return lax.ppermute(x, axis, pairs + [(j, i) for i, j in pairs])


def per_device(gauge_links, pattern, link_parity, conv_weight, conv_bias, head_weight, cotangent):
    shape = jax.ShapeDtypeStruct
    sems = pltpu.SemaphoreType.DMA
    edge = shape((10, 54, 128), BF16)
    links = pltpu.VMEM((5, 2, 3, 3, 24, 128), F32)
    x_edge, z_edge = call(
        send_body, (edge, edge), [links, sems((10,))], gauge_links, away=(0,), name="send"
    )
    next_x = shifted(x_edge, "xy", -1)
    next_z = shifted(z_edge, "gz", -1)
    keep = jnp.asarray(np.concatenate(KEEP), BF16)
    spread = jnp.asarray(SPREAD, BF16)
    weights, small = call(
        weights_body, (shape((12, 128, 256), BF16), shape((64, 8), F32)), [],
        conv_weight.transpose(1, 2, 0), spread, keep, head_weight.T, conv_bias[None], name="weights",
    )
    next_x, next_z, weights, small = lax.optimization_barrier((next_x, next_z, weights, small))
    half = shape((128, 128), BF16)
    odd = (lax.axis_index("xy") % 2).reshape(1)
    z_odd = (lax.axis_index("gz") % 2).reshape(1)
    border = pltpu.VMEM((57 * 24, 128), F32)
    half_one, half_two = call(
        loops_body, (half, half),
        [links, border, border, pltpu.VMEM((14, 24, 128), F32), pltpu.VMEM((2, 128, 128), F32), sems((12,))],
        z_odd, gauge_links, next_x, next_z, smem=1, away=(1,), name="loops",
    )
    block = jnp.stack([swapped(half_one, "gz", 1), half_one, half_two, swapped(half_two, "gz", 0)])
    first = swapped(block, "xy", 1)
    second = swapped(block, "xy", 0)
    x_first = (lax.axis_index("xy") * 2).reshape(1)
    z_first = (lax.axis_index("gz") * 4).reshape(1)
    coefficients, grads = call(
        layer_body, (shape((4, 2, 2, 256), F32), shape((64, 16, 128), BF16)),
        [pltpu.VMEM((12, 256, 1024), BF16), pltpu.VMEM((64, 1024), BF16), pltpu.VMEM((1024, 128), F32)]
        + [pltpu.VMEM((4, n, 128), F32) for n in (96, 128, 64)],
        odd, x_first, z_first, pattern, link_parity, second, block, first, weights, small, keep, cotangent,
        smem=5, name="layer",
    )
    both = ("xy", "gz")
    count = lax.axis_size(both)
    chunks = grads.reshape(count, 1024 // count, 128)
    chunks = lax.all_to_all(chunks, both, 0, 0, tiled=True)
    me = lax.axis_index(both).reshape(1)
    chunks = call(total_body, (shape(chunks.shape, BF16),), [], me, chunks, smem=1, name="total")[0]
    chunks = lax.all_to_all(chunks, both, 0, 0, tiled=True)
    grad_kernel, grad_bias, grad_head = call(
        expand_body, (shape((48, 64, 81), F32), shape((1, 64), F32), shape((4, 64), F32)),
        [pltpu.VMEM((1024, 128), F32)], chunks.reshape(64, 16, 128), spread, name="expand",
    )
    return coefficients, grad_kernel.transpose(2, 0, 1), grad_bias.reshape(64), grad_head.T


def solution(mesh):
    return jax.shard_map(
        per_device,
        mesh=mesh,
        in_specs=(
            P(None, None, None, None, None, "xy", "gz"),
            P(),
            P(),
            P(),
            P(),
            P(),
            P(None, None, "xy", "gz"),
        ),
        out_specs=(P(None, None, "xy", "gz"), P(), P(), P()),
        check_vma=False,
    )
```

```python
import math

import jax
import jax.numpy as jnp
import numpy as np
from jax import lax
from jax.experimental import pallas as pl
from jax.experimental.pallas import tpu as pltpu
from jax.sharding import PartitionSpec as P

LY = 64
ROWS = 1024
F32 = jnp.float32
BF16 = jnp.bfloat16

plane_pairs = ((0, 1), (0, 2), (0, 3), (1, 2), (1, 3), (2, 3))
INTERPRET = False
PARAMS = pltpu.CompilerParams(vmem_limit_bytes=56 * 2**20)


def lanes(shape):
    return lax.broadcasted_iota(jnp.int32, shape, len(shape) - 1)


def shift_y(x, by):
    if by == 0:
        return x
    axis = x.ndim - 1
    inner = pltpu.roll(x, (-by) % 128, axis)
    wrapped = pltpu.roll(x, (64 - by) % 128, axis)
    y = lanes(x.shape) % LY
    crossed = (y >= LY - by) if by > 0 else (y < -by)
    return jnp.where(crossed, wrapped, inner)


def plane_tables():
    tiles, keep, spread = [], [], np.zeros((6, 144, 512), np.float32)
    for p, pair in enumerate(plane_pairs):
        spans = [range(0 if d in pair else 1, 4) for d in range(4)]
        tiles.append([(z, y) for z in spans[2] for y in spans[1]])
        kept = {}
        table = np.zeros((16 * len(tiles[p]), 256), np.float32)
        for i, (z, y) in enumerate(tiles[p]):
            for x in spans[0]:
                for t in spans[3]:
                    table[16 * i + 4 * x + t, len(kept)] = 1
                    kept[x, y, z, t] = len(kept)
        keep.append(table)
        for leaf, back in enumerate(((), (pair[0],), (pair[1],), pair)):
            sx, sy, sz, st = (0 if d in back else 1 for d in range(4))
            for k in range(81):
                dx, dz, dt, dy = k // 27, k // 9 % 3, k // 3 % 3, k % 3
                spread[p, kept[dx + sx, dy + sy, dz + sz, dt + st], leaf * 128 + k] = 1
    return tiles, keep, spread


TILES, KEEP, SPREAD = plane_tables()
SIZES = [16 * len(t) for t in TILES]
STARTS = [sum(SIZES[:p]) for p in range(6)]
NT = (((1,), (1,)), ((), ()))


def weights_body(w_ref, spread_ref, keep_ref, head_ref, bias_ref, out_ref, small_ref):
    for p in range(6):
        table = keep_ref[STARTS[p] : STARTS[p] + SIZES[p], :]
        for r in range(2):
            full = jnp.zeros((64, 144), F32)
            for leaf in range(4):
                full = full + lax.dot_general(
                    w_ref[8 * p + 2 * leaf + r], spread_ref[p, :, leaf * 128 : leaf * 128 + 81], NT,
                    preferred_element_type=F32,
                )
            high = full.astype(BF16)
            low = (full - high.astype(F32)).astype(BF16)
            both = jnp.concatenate([high, low], axis=0)
            out_ref[2 * p + r, :, 0 : SIZES[p]] = lax.dot_general(
                both, table[:, :144], NT, preferred_element_type=F32
            ).astype(BF16)
    small_ref[...] = jnp.concatenate([head_ref[...], bias_ref[...], jnp.zeros((3, 64), F32)], axis=0).T


def place(c, x):
    return 64 + 32 * (c // 6) + 5 * (c % 6) if x == 1 else (32 + 5 * c if c < 6 else 5 * (c - 6))


def fetch(links_ref, l_ref, sems, slices):
    return [
        pltpu.make_async_copy(
            links_ref.at[:, :, :, :, tau, :, lb * 128 : lb * 128 + 128],
            l_ref.at[0:4, :, :, :, tau * 4 + lb * 2 : tau * 4 + lb * 2 + 2, :],
            sems.at[tau * 2 + lb],
        )
        for tau in range(slices)
        for lb in range(2)
    ]


def send_body(links_ref, x_ref, z_ref, l_ref, sems):
    copies = fetch(links_ref, l_ref, sems, 5)
    for copy in copies:
        copy.start()
    rows_ref = l_ref.reshape(90 * 24, 128)
    for tau in range(5):
        for copy in copies[2 * tau : 2 * tau + 2]:
            copy.wait()
        for half in range(2):
            at = tau * 2 + half
            x_ref[at] = rows_ref[pl.ds(18 * 24 + tau * 4 + half * 2, 54, stride=24), :].astype(BF16)
            row = tau * 4 + half
            first = rows_ref[pl.ds(row, 36, stride=24), :]
            last = rows_ref[pl.ds(54 * 24 + row, 18, stride=24), :]
            z_ref[at] = jnp.concatenate([first, last], axis=0).astype(BF16)


def loops_body(
    odd_ref, links_ref, xh_ref, zh_ref, o0_ref, o1_ref, l_ref, xs_ref, zs_ref, pq_ref, tile_ref, sems
):
    copies = fetch(links_ref, l_ref, sems, 6)
    for copy in copies:
        copy.start()
    for tau in range(5):
        for half in range(2):
            at = tau * 2 + half
            xs_ref[pl.ds(tau * 4 + half * 2 + 1, 54, stride=24), :] = xh_ref[at].astype(F32)
            zs_ref[pl.ds(tau * 4 + 2 + half, 54, stride=24), :] = zh_ref[at].astype(F32)
    tile_ref[...] = jnp.zeros_like(tile_ref)
    row = lax.broadcasted_iota(jnp.int32, (8, 128), 0)
    odd_x = row % 2 == 1
    high_z = row % 4 >= 2
    upper = lanes((8, 128)) >= LY

    def at_site(d, k):
        part = slice(8 * k, 8 * k + 8)
        return [
            [[l_ref[d, ri, i, j, part, :] for j in range(3)] for i in range(3)] for ri in range(2)
        ]

    def border(d, ri, i, j, k):
        row = (((d * 2 + ri) * 3 + i) * 3 + j) * 24 + 8 * k
        return slice(row, row + 8)

    def ahead(d, step, k):
        part = slice(8 * k, 8 * k + 8)

        def one(ri, i, j):
            if step == 3:
                if k < 2:
                    return l_ref[d, ri, i, j, 8 * k + 4 : 8 * k + 12, :]
                return pltpu.roll(l_ref[d, ri, i, j, 16:24, :], 4, 0)
            own = l_ref[d, ri, i, j, part, :]
            if step == 0:
                return jnp.where(odd_x, xs_ref[border(d - 1, ri, i, j, k), :], pltpu.roll(own, 7, 0))
            if step == 1:
                return shift_y(own, 1)
            edge = zs_ref[border(min(d, 2), ri, i, j, k), :]
            beyond = jnp.where(high_z, edge, pltpu.roll(own, 6, 0))
            return pltpu.roll(jnp.where(upper, own, beyond), LY, 1)

        return [[[one(ri, i, j) for j in range(3)] for i in range(3)] for ri in range(2)]

    def product(a, b, i, j):
        re = a[0][i][0] * b[0][0][j] - a[1][i][0] * b[1][0][j]
        im = a[0][i][0] * b[1][0][j] + a[1][i][0] * b[0][0][j]
        for m in (1, 2):
            re = re + a[0][i][m] * b[0][m][j] - a[1][i][m] * b[1][m][j]
            im = im + a[0][i][m] * b[1][m][j] + a[1][i][m] * b[0][m][j]
        return re, im

    for k in range(3):
        for copy in (copies[:6], copies[6:10], copies[10:])[k]:
            copy.wait()
        for p, (mu, nu) in enumerate(plane_pairs):
            u_mu = at_site(mu, k)
            u_nu = at_site(nu, k)
            nu_ahead = ahead(nu, mu, k)
            mu_ahead = ahead(mu, nu, k)
            re = im = None
            for i in range(3):
                for j in range(3):
                    r1, i1 = product(u_mu, nu_ahead, i, j)
                    r2, i2 = product(u_nu, mu_ahead, i, j)
                    re_term = r1 * r2 + i1 * i2
                    im_term = i1 * r2 - r1 * i2
                    re = re_term if re is None else re + re_term
                    im = im_term if im is None else im + im_term
            pq_ref[2 * p, 8 * k : 8 * k + 8, :] = re
            pq_ref[2 * p + 1, 8 * k : 8 * k + 8, :] = im
    for c in range(12):
        for lb, o_ref in enumerate((o0_ref, o1_ref)):
            for x in range(2):
                row = place(c, x)
                tile_ref[lb, row : row + 5, :] = pq_ref[c, pl.ds(2 * lb + x, 5, stride=4), :]
    odd = odd_ref[0] == 1
    o0_ref[...] = jnp.where(odd, tile_ref[1], tile_ref[0]).astype(BF16)
    o1_ref[...] = jnp.where(odd, tile_ref[0], tile_ref[1]).astype(BF16)


def layer_body(
    odd_ref, x0_ref, z0_ref, pat_ref, par_ref, second_in, own_in, first_in, w_ref, small_ref, keep_ref, cot_ref,
    coef_ref, g_ref, a_ref, low_ref, rows_ref, left_ref, own_ref, right_ref,
):
    odd = odd_ref[0] == 1
    turned = lax.rem(lax.div(z0_ref[0], 4), 2) == 1
    for i in range(4):

        def pick(ref, part):
            return jnp.where(turned, ref[3 - i, part].astype(F32), ref[i, part].astype(F32))

        own_ref[i] = pick(own_in, slice(0, 128))
        left_ref[i] = jnp.where(odd, pick(second_in, slice(32, 128)), pick(first_in, slice(32, 128)))
        right_ref[i] = jnp.where(odd, pick(first_in, slice(0, 64)), pick(second_in, slice(0, 64)))

    def piece(i, x, c, t):
        if x == 0 and c >= 6:
            return jnp.zeros((4, 128), F32)
        if x < 2:
            ref, row = left_ref, place(c, x) - 32
        elif x < 4:
            ref, row = own_ref, place(c, x - 2)
        else:
            ref, row = right_ref, place(c, 0)
        return ref[i, row + t : row + t + 4, :]

    lane = lanes((8, 128))
    upper = lane >= LY

    def crossed(by):
        y = lane % LY
        return (y >= LY - by) if by > 0 else (y < -by)

    for p in range(6):
        offsets = sorted({y for _, y in TILES[p]})
        for r in range(2):
            c = 2 * p + r
            for t in range(2):
                cols = []
                for i in range(4):
                    pieces = [piece(i, x, c, t) for x in range(5)]
                    cols.append([
                        [jnp.concatenate(pieces[x + 2 * h : x + 2 * h + 2], axis=0) for h in range(2)]
                        for x in range(2)
                    ])
                for x in range(2):
                    for y in offsets:
                        by = y - 2
                        made = []
                        for h in range(2):
                            plain, other = [], []
                            for i in range(4):
                                v = cols[i][x][h]
                                near = v if by == 0 else pltpu.roll(v, (-by) % 128, 1)
                                far = pltpu.roll(v, (LY - by) % 128, 1)
                                if by == 0:
                                    plain.append(near)
                                    other.append(far)
                                else:
                                    plain.append(jnp.where(crossed(by), far, near))
                                    other.append(jnp.where(crossed(by), near, far))
                            made.append([
                                plain[z // 2] if z % 2 == 0 else jnp.where(upper, other[z // 2 + 1], other[z // 2])
                                for z in range(6)
                            ])
                        both = [jnp.concatenate([u, v], axis=0).astype(BF16) for u, v in zip(*made)]
                        for n, (z, y_at) in enumerate(TILES[p]):
                            if y_at == y:
                                for lb in range(2):
                                    col = (t * 4 + x * 2 + lb) * 128
                                    a_ref[c, 16 * n : 16 * n + 16, col : col + 128] = both[z + 2 * lb]

    lane = lanes((1, 256))
    y_pos = lane % LY
    z_pos = z0_ref[0] + lane // LY
    bias_sum = jnp.zeros((64, 256), F32)
    head_sums = [jnp.zeros((64, 256), F32) for _ in range(4)]
    for t in range(2):
        for x in range(2):
            cols = slice((t * 2 + x) * 256, (t * 2 + x) * 256 + 256)
            acc = jnp.zeros((128, 256), F32)
            for c in range(12):
                size = SIZES[c // 2]
                acc = acc + jnp.dot(
                    w_ref[c, :, 0:size], a_ref[c, 0:size, cols], preferred_element_type=F32
                )
            hidden = acc[:64] + acc[64:] + small_ref[:, 4:5]
            act = jnp.tanh(hidden)
            act_grad = jnp.zeros((64, 256), F32)
            for mu in range(4):
                fixed = pat_ref[mu, 0] * (x0_ref[0] + x) + pat_ref[mu, 3] * t + par_ref[mu]
                summed = pat_ref[mu, 1] * y_pos + pat_ref[mu, 2] * z_pos + fixed
                active = ((summed & 1) == 0).astype(F32)
                weight = small_ref[:, mu : mu + 1]
                coef = active * jnp.sum(weight * act, axis=0, keepdims=True)
                coef_ref[mu, t, x : x + 1, :] = coef
                coef_grad = active * cot_ref[mu, t, x : x + 1, :] * (1.0 / math.sqrt(ROWS))
                act_grad = act_grad + weight * coef_grad
                head_sums[mu] = head_sums[mu] + act * coef_grad
            hidden_grad = act_grad * (1.0 - act * act)
            bias_sum = bias_sum + hidden_grad
            low_ref[:, cols] = hidden_grad.astype(BF16)

    spot = lanes((64, 128))
    small = jnp.zeros((64, 128), F32)
    for i, total in enumerate(head_sums + [bias_sum]):
        value = jnp.sum(total, axis=1, keepdims=True)
        rounded = value.astype(BF16).astype(F32)
        small = jnp.where(spot == i, rounded, jnp.where(spot == i + 8, value - rounded, small))

    def put(j, value):
        rows_ref[pl.ds(j, 64, stride=16), :] = value

    ends = [jnp.zeros((64, 128), F32), jnp.zeros((64, 128), F32)]
    for c in range(12):
        start, size = STARTS[c // 2], SIZES[c // 2]
        grad = lax.dot_general(low_ref[...], a_ref[c, 0:size, :], NT, preferred_element_type=F32)
        kept = jnp.dot(grad.astype(BF16), keep_ref[start : start + size, :], preferred_element_type=F32)
        put(c, kept[:, :128])
        end = kept[:, 128:]
        ends[c // 8] = ends[c // 8] + (pltpu.roll(end, 16 * (c % 8), 1) if c % 8 else end)
    put(12, ends[0])
    put(13, ends[1])
    put(14, small)
    put(15, jnp.zeros((64, 128), F32))
    g_ref[...] = rows_ref[...].reshape(64, 16, 128).astype(BF16)


def total_body(me_ref, in_ref, out_ref):
    total = in_ref[...]
    row = me_ref[0] * total.shape[0] + lax.broadcasted_iota(jnp.int32, total.shape, 0)
    lane = lanes(total.shape)
    whole = jnp.where(lane < 8, total + pltpu.roll(total, 120, 1), 0.0)
    rounded = whole.astype(BF16).astype(F32)
    rest = pltpu.roll(whole - rounded, 8, 1)
    total = jnp.where(row % 16 == 14, jnp.where(lane < 8, rounded, rest), total)
    out_ref[...] = jnp.broadcast_to(total.astype(BF16)[None], out_ref.shape)


def expand_body(g_ref, spread_ref, k_ref, b_ref, h_ref, rows_ref):
    rows_ref[...] = g_ref[...].astype(F32).reshape(1024, 128)

    def get(j):
        return rows_ref[pl.ds(j, 64, stride=16), :]

    ends = [get(12), get(13)]
    for c in range(12):
        p, r = c // 2, c % 2
        end = ends[c // 8]
        end = pltpu.roll(end, 128 - 16 * (c % 8), 1) if c % 8 else end
        kept = jnp.concatenate([get(c), end[:, :16]], axis=1).astype(BF16)
        full = jnp.dot(kept, spread_ref[p], preferred_element_type=F32)
        for leaf in range(4):
            k_ref[8 * p + 2 * leaf + r] = full[:, leaf * 128 : leaf * 128 + 81]
    small = get(14)
    small = (small + pltpu.roll(small, 120, 1)).T
    h_ref[...] = small[0:4]
    b_ref[...] = small[4:5]


def call(body, outs, scratch, *args, smem=0, away=(), name):
    def spec(i, away):
        return pl.BlockSpec(memory_space=pl.ANY if i in away else pltpu.VMEM)

    specs = [pl.BlockSpec(memory_space=pltpu.SMEM)] * smem
    return pl.pallas_call(
        body,
        out_shape=outs,
        in_specs=specs + [spec(i, away) for i in range(smem, len(args))],
        out_specs=(pl.BlockSpec(memory_space=pltpu.VMEM),) * len(outs),
        scratch_shapes=scratch,
        compiler_params=PARAMS,
        interpret=INTERPRET,
        name=name,
    )(*args)


def shifted(x, axis, by):
    count = lax.axis_size(axis)
    return lax.ppermute(x, axis, [(i, (i + by) % count) for i in range(count)])


def swapped(x, axis, least):
    count = lax.axis_size(axis)
    pairs = [(i % count, (i + 1) % count) for i in range(least, least + count, 2)]
    return lax.ppermute(x, axis, pairs + [(j, i) for i, j in pairs])


def per_device(gauge_links, pattern, link_parity, conv_weight, conv_bias, head_weight, cotangent):
    shape = jax.ShapeDtypeStruct
    sems = pltpu.SemaphoreType.DMA
    edge = shape((10, 54, 128), BF16)
    links = pltpu.VMEM((5, 2, 3, 3, 24, 128), F32)
    x_edge, z_edge = call(
        send_body, (edge, edge), [links, sems((10,))], gauge_links, away=(0,), name="send"
    )
    next_x = shifted(x_edge, "xy", -1)
    next_z = shifted(z_edge, "gz", -1)
    keep = jnp.asarray(np.concatenate(KEEP), BF16)
    spread = jnp.asarray(SPREAD, BF16)
    weights, small = call(
        weights_body, (shape((12, 128, 256), BF16), shape((64, 8), F32)), [],
        conv_weight.transpose(1, 2, 0), spread, keep, head_weight.T, conv_bias[None], name="weights",
    )
    next_x, next_z, weights, small = lax.optimization_barrier((next_x, next_z, weights, small))
    half = shape((128, 128), BF16)
    odd = (lax.axis_index("xy") % 2).reshape(1)
    z_odd = (lax.axis_index("gz") % 2).reshape(1)
    border = pltpu.VMEM((57 * 24, 128), F32)
    half_one, half_two = call(
        loops_body, (half, half),
        [links, border, border, pltpu.VMEM((14, 24, 128), F32), pltpu.VMEM((2, 128, 128), F32), sems((12,))],
        z_odd, gauge_links, next_x, next_z, smem=1, away=(1,), name="loops",
    )
    block = jnp.stack([swapped(half_one, "gz", 1), half_one, half_two, swapped(half_two, "gz", 0)])
    first = swapped(block, "xy", 1)
    second = swapped(block, "xy", 0)
    x_first = (lax.axis_index("xy") * 2).reshape(1)
    z_first = (lax.axis_index("gz") * 4).reshape(1)
    coefficients, grads = call(
        layer_body, (shape((4, 2, 2, 256), F32), shape((64, 16, 128), BF16)),
        [pltpu.VMEM((12, 256, 1024), BF16), pltpu.VMEM((64, 1024), BF16), pltpu.VMEM((1024, 128), F32)]
        + [pltpu.VMEM((4, n, 128), F32) for n in (96, 128, 64)],
        odd, x_first, z_first, pattern, link_parity, second, block, first, weights, small, keep, cotangent,
        smem=5, name="layer",
    )
    both = ("xy", "gz")
    count = lax.axis_size(both)
    chunks = grads.reshape(count, 1024 // count, 128)
    chunks = lax.all_to_all(chunks, both, 0, 0, tiled=True)
    me = lax.axis_index(both).reshape(1)
    total = jnp.sum(chunks.astype(F32), axis=0)
    chunks = call(total_body, (shape(chunks.shape, BF16),), [], me, total, smem=1, name="total")[0]
    chunks = lax.all_to_all(chunks, both, 0, 0, tiled=True)
    grad_kernel, grad_bias, grad_head = call(
        expand_body, (shape((48, 64, 81), F32), shape((1, 64), F32), shape((4, 64), F32)),
        [pltpu.VMEM((1024, 128), F32)], chunks.reshape(64, 16, 128), spread, name="expand",
    )
    return coefficients, grad_kernel.transpose(2, 0, 1), grad_bias.reshape(64), grad_head.T


def solution(mesh):
    return jax.shard_map(
        per_device,
        mesh=mesh,
        in_specs=(
            P(None, None, None, None, None, "xy", "gz"),
            P(),
            P(),
            P(),
            P(),
            P(),
            P(None, None, "xy", "gz"),
        ),
        out_specs=(P(None, None, "xy", "gz"), P(), P(), P()),
        check_vma=False,
    )
```

```python
import math

import jax
import jax.numpy as jnp
import numpy as np
from jax import lax
from jax.experimental import pallas as pl
from jax.experimental.pallas import tpu as pltpu
from jax.sharding import PartitionSpec as P

LY = 64
ROWS = 1024
F32 = jnp.float32
BF16 = jnp.bfloat16

plane_pairs = ((0, 1), (0, 2), (0, 3), (1, 2), (1, 3), (2, 3))
INTERPRET = False
PARAMS = pltpu.CompilerParams(vmem_limit_bytes=56 * 2**20)


def lanes(shape):
    return lax.broadcasted_iota(jnp.int32, shape, len(shape) - 1)


def shift_y(x, by):
    if by == 0:
        return x
    axis = x.ndim - 1
    inner = pltpu.roll(x, (-by) % 128, axis)
    wrapped = pltpu.roll(x, (64 - by) % 128, axis)
    y = lanes(x.shape) % LY
    crossed = (y >= LY - by) if by > 0 else (y < -by)
    return jnp.where(crossed, wrapped, inner)


def plane_tables():
    tiles, keep, spread = [], [], np.zeros((6, 144, 512), np.float32)
    for p, pair in enumerate(plane_pairs):
        spans = [range(0 if d in pair else 1, 4) for d in range(4)]
        tiles.append([(z, y) for z in spans[2] for y in spans[1]])
        kept = {}
        table = np.zeros((16 * len(tiles[p]), 256), np.float32)
        for i, (z, y) in enumerate(tiles[p]):
            for x in spans[0]:
                for t in spans[3]:
                    table[16 * i + 4 * x + t, len(kept)] = 1
                    kept[x, y, z, t] = len(kept)
        keep.append(table)
        for leaf, back in enumerate(((), (pair[0],), (pair[1],), pair)):
            sx, sy, sz, st = (0 if d in back else 1 for d in range(4))
            for k in range(81):
                dx, dz, dt, dy = k // 27, k // 9 % 3, k // 3 % 3, k % 3
                spread[p, kept[dx + sx, dy + sy, dz + sz, dt + st], leaf * 128 + k] = 1
    return tiles, keep, spread


TILES, KEEP, SPREAD = plane_tables()
SIZES = [16 * len(t) for t in TILES]
STARTS = [sum(SIZES[:p]) for p in range(6)]
NT = (((1,), (1,)), ((), ()))


def weights_body(w_ref, spread_ref, keep_ref, head_ref, bias_ref, out_ref, small_ref):
    for p in range(6):
        table = keep_ref[STARTS[p] : STARTS[p] + SIZES[p], :]
        for r in range(2):
            full = jnp.zeros((64, 144), F32)
            for leaf in range(4):
                full = full + lax.dot_general(
                    w_ref[8 * p + 2 * leaf + r], spread_ref[p, :, leaf * 128 : leaf * 128 + 81], NT,
                    preferred_element_type=F32,
                )
            high = full.astype(BF16)
            low = (full - high.astype(F32)).astype(BF16)
            both = jnp.concatenate([high, low], axis=0)
            out_ref[2 * p + r, :, 0 : SIZES[p]] = lax.dot_general(
                both, table[:, :144], NT, preferred_element_type=F32
            ).astype(BF16)
    small_ref[...] = jnp.concatenate([head_ref[...], bias_ref[...], jnp.zeros((3, 64), F32)], axis=0).T


def place(c, x):
    return 64 + 32 * (c // 6) + 5 * (c % 6) if x == 1 else (32 + 5 * c if c < 6 else 5 * (c - 6))


def fetch(links_ref, l_ref, sems, slices):
    return [
        pltpu.make_async_copy(
            links_ref.at[:, :, :, :, tau, :, lb * 128 : lb * 128 + 128],
            l_ref.at[0:4, :, :, :, tau * 4 + lb * 2 : tau * 4 + lb * 2 + 2, :],
            sems.at[tau * 2 + lb],
        )
        for tau in range(slices)
        for lb in range(2)
    ]


def send_body(links_ref, x_ref, z_ref, l_ref, sems):
    copies = fetch(links_ref, l_ref, sems, 5)
    for copy in copies:
        copy.start()
    rows_ref = l_ref.reshape(90 * 24, 128)
    for tau in range(5):
        for copy in copies[2 * tau : 2 * tau + 2]:
            copy.wait()
        for half in range(2):
            at = tau * 2 + half
            x_ref[at] = rows_ref[pl.ds(18 * 24 + tau * 4 + half * 2, 54, stride=24), :].astype(BF16)
            row = tau * 4 + half
            first = rows_ref[pl.ds(row, 36, stride=24), :]
            last = rows_ref[pl.ds(54 * 24 + row, 18, stride=24), :]
            z_ref[at] = jnp.concatenate([first, last], axis=0).astype(BF16)


def loops_body(
    odd_ref, links_ref, xh_ref, zh_ref, o0_ref, o1_ref, l_ref, xs_ref, zs_ref, pq_ref, tile_ref, sems
):
    copies = fetch(links_ref, l_ref, sems, 6)
    for copy in copies:
        copy.start()
    for tau in range(5):
        for half in range(2):
            at = tau * 2 + half
            xs_ref[pl.ds(tau * 4 + half * 2 + 1, 54, stride=24), :] = xh_ref[at].astype(F32)
            zs_ref[pl.ds(tau * 4 + 2 + half, 54, stride=24), :] = zh_ref[at].astype(F32)
    tile_ref[...] = jnp.zeros_like(tile_ref)
    row = lax.broadcasted_iota(jnp.int32, (8, 128), 0)
    odd_x = row % 2 == 1
    high_z = row % 4 >= 2
    upper = lanes((8, 128)) >= LY

    def at_site(d, k):
        part = slice(8 * k, 8 * k + 8)
        return [
            [[l_ref[d, ri, i, j, part, :] for j in range(3)] for i in range(3)] for ri in range(2)
        ]

    def border(d, ri, i, j, k):
        row = (((d * 2 + ri) * 3 + i) * 3 + j) * 24 + 8 * k
        return slice(row, row + 8)

    def ahead(d, step, k):
        part = slice(8 * k, 8 * k + 8)

        def one(ri, i, j):
            if step == 3:
                if k < 2:
                    return l_ref[d, ri, i, j, 8 * k + 4 : 8 * k + 12, :]
                return pltpu.roll(l_ref[d, ri, i, j, 16:24, :], 4, 0)
            own = l_ref[d, ri, i, j, part, :]
            if step == 0:
                return jnp.where(odd_x, xs_ref[border(d - 1, ri, i, j, k), :], pltpu.roll(own, 7, 0))
            if step == 1:
                return shift_y(own, 1)
            edge = zs_ref[border(min(d, 2), ri, i, j, k), :]
            beyond = jnp.where(high_z, edge, pltpu.roll(own, 6, 0))
            return pltpu.roll(jnp.where(upper, own, beyond), LY, 1)

        return [[[one(ri, i, j) for j in range(3)] for i in range(3)] for ri in range(2)]

    def product(a, b, i, j):
        re = a[0][i][0] * b[0][0][j] - a[1][i][0] * b[1][0][j]
        im = a[0][i][0] * b[1][0][j] + a[1][i][0] * b[0][0][j]
        for m in (1, 2):
            re = re + a[0][i][m] * b[0][m][j] - a[1][i][m] * b[1][m][j]
            im = im + a[0][i][m] * b[1][m][j] + a[1][i][m] * b[0][m][j]
        return re, im

    for k in range(3):
        for copy in (copies[:6], copies[6:10], copies[10:])[k]:
            copy.wait()
        for p, (mu, nu) in enumerate(plane_pairs):
            u_mu = at_site(mu, k)
            u_nu = at_site(nu, k)
            nu_ahead = ahead(nu, mu, k)
            mu_ahead = ahead(mu, nu, k)
            re = im = None
            for i in range(3):
                for j in range(3):
                    r1, i1 = product(u_mu, nu_ahead, i, j)
                    r2, i2 = product(u_nu, mu_ahead, i, j)
                    re_term = r1 * r2 + i1 * i2
                    im_term = i1 * r2 - r1 * i2
                    re = re_term if re is None else re + re_term
                    im = im_term if im is None else im + im_term
            pq_ref[2 * p, 8 * k : 8 * k + 8, :] = re
            pq_ref[2 * p + 1, 8 * k : 8 * k + 8, :] = im
    for c in range(12):
        for lb, o_ref in enumerate((o0_ref, o1_ref)):
            for x in range(2):
                row = place(c, x)
                tile_ref[lb, row : row + 5, :] = pq_ref[c, pl.ds(2 * lb + x, 5, stride=4), :]
    odd = odd_ref[0] == 1
    o0_ref[...] = jnp.where(odd, tile_ref[1, 0:128, :], tile_ref[0, 0:128, :]).astype(BF16)
    o1_ref[...] = jnp.where(odd, tile_ref[0, 0:128, :], tile_ref[1, 0:128, :]).astype(BF16)


def layer_body(
    odd_ref, x0_ref, z0_ref, pat_ref, par_ref, second_in, own_in, first_in, w_ref, small_ref, keep_ref, cot_ref,
    coef_ref, g_ref, a_ref, low_ref, rows_ref, left_ref, own_ref, right_ref,
):
    odd = odd_ref[0] == 1
    turned = lax.rem(lax.div(z0_ref[0], 4), 2) == 1
    for i in range(4):

        def pick(ref, part):
            return jnp.where(turned, ref[3 - i, part].astype(F32), ref[i, part].astype(F32))

        own_ref[i, 0:128] = pick(own_in, slice(0, 128))
        left_ref[i, 0:96] = jnp.where(odd, pick(second_in, slice(32, 128)), pick(first_in, slice(32, 128)))
        right_ref[i, 0:64] = jnp.where(odd, pick(first_in, slice(0, 64)), pick(second_in, slice(0, 64)))

    def piece(i, x, c, t):
        if x == 0 and c >= 6:
            return jnp.zeros((4, 128), F32)
        if x < 2:
            ref, row = left_ref, place(c, x) - 32
        elif x < 4:
            ref, row = own_ref, place(c, x - 2)
        else:
            ref, row = right_ref, place(c, 0)
        return ref[i, row + t : row + t + 4, :]

    lane = lanes((8, 128))
    upper = lane >= LY

    def crossed(by):
        y = lane % LY
        return (y >= LY - by) if by > 0 else (y < -by)

    for p in range(6):
        offsets = sorted({y for _, y in TILES[p]})
        for r in range(2):
            c = 2 * p + r
            for t in range(2):
                cols = []
                for i in range(4):
                    pieces = [piece(i, x, c, t) for x in range(5)]
                    cols.append([
                        [jnp.concatenate(pieces[x + 2 * h : x + 2 * h + 2], axis=0) for h in range(2)]
                        for x in range(2)
                    ])
                for x in range(2):
                    for y in offsets:
                        by = y - 2
                        made = []
                        for h in range(2):
                            plain, other = [], []
                            for i in range(4):
                                v = cols[i][x][h]
                                near = v if by == 0 else pltpu.roll(v, (-by) % 128, 1)
                                far = pltpu.roll(v, (LY - by) % 128, 1)
                                if by == 0:
                                    plain.append(near)
                                    other.append(far)
                                else:
                                    plain.append(jnp.where(crossed(by), far, near))
                                    other.append(jnp.where(crossed(by), near, far))
                            made.append([
                                plain[z // 2] if z % 2 == 0 else jnp.where(upper, other[z // 2 + 1], other[z // 2])
                                for z in range(6)
                            ])
                        both = [jnp.concatenate([u, v], axis=0).astype(BF16) for u, v in zip(*made)]
                        for n, (z, y_at) in enumerate(TILES[p]):
                            if y_at == y:
                                for lb in range(2):
                                    col = (t * 4 + x * 2 + lb) * 128
                                    a_ref[c, 16 * n : 16 * n + 16, col : col + 128] = both[z + 2 * lb]

    lane = lanes((1, 256))
    y_pos = lane % LY
    z_pos = z0_ref[0] + lane // LY
    bias_sum = jnp.zeros((64, 256), F32)
    head_sums = [jnp.zeros((64, 256), F32) for _ in range(4)]
    for t in range(2):
        for x in range(2):
            cols = slice((t * 2 + x) * 256, (t * 2 + x) * 256 + 256)
            acc = jnp.zeros((128, 256), F32)
            for c in range(12):
                size = SIZES[c // 2]
                acc = acc + jnp.dot(
                    w_ref[c, :, 0:size], a_ref[c, 0:size, cols], preferred_element_type=F32
                )
            hidden = acc[:64] + acc[64:] + small_ref[:, 4:5]
            act = jnp.tanh(hidden)
            act_grad = jnp.zeros((64, 256), F32)
            for mu in range(4):
                fixed = pat_ref[mu, 0] * (x0_ref[0] + x) + pat_ref[mu, 3] * t + par_ref[mu]
                summed = pat_ref[mu, 1] * y_pos + pat_ref[mu, 2] * z_pos + fixed
                active = ((summed & 1) == 0).astype(F32)
                weight = small_ref[:, mu : mu + 1]
                coef = active * jnp.sum(weight * act, axis=0, keepdims=True)
                coef_ref[mu, t, x : x + 1, :] = coef
                coef_grad = active * cot_ref[mu, t, x : x + 1, :] * (1.0 / math.sqrt(ROWS))
                act_grad = act_grad + weight * coef_grad
                head_sums[mu] = head_sums[mu] + act * coef_grad
            hidden_grad = act_grad * (1.0 - act * act)
            bias_sum = bias_sum + hidden_grad
            low_ref[:, cols] = hidden_grad.astype(BF16)

    spot = lanes((64, 128))
    small = jnp.zeros((64, 128), F32)
    for i, total in enumerate(head_sums + [bias_sum]):
        value = jnp.sum(total, axis=1, keepdims=True)
        rounded = value.astype(BF16).astype(F32)
        small = jnp.where(spot == i, rounded, jnp.where(spot == i + 8, value - rounded, small))

    def put(j, value):
        rows_ref[pl.ds(j, 64, stride=16), :] = value

    ends = [jnp.zeros((64, 128), F32), jnp.zeros((64, 128), F32)]
    for c in range(12):
        start, size = STARTS[c // 2], SIZES[c // 2]
        grad = lax.dot_general(low_ref[...], a_ref[c, 0:size, :], NT, preferred_element_type=F32)
        kept = jnp.dot(grad.astype(BF16), keep_ref[start : start + size, :], preferred_element_type=F32)
        put(c, kept[:, :128])
        end = kept[:, 128:]
        ends[c // 8] = ends[c // 8] + (pltpu.roll(end, 16 * (c % 8), 1) if c % 8 else end)
    put(12, ends[0])
    put(13, ends[1])
    put(14, small)
    put(15, jnp.zeros((64, 128), F32))
    g_ref[...] = rows_ref[...].reshape(64, 16, 128).astype(BF16)


def total_body(me_ref, in_ref, out_ref):
    total = in_ref[...]
    row = me_ref[0] * total.shape[0] + lax.broadcasted_iota(jnp.int32, total.shape, 0)
    lane = lanes(total.shape)
    whole = jnp.where(lane < 8, total + pltpu.roll(total, 120, 1), 0.0)
    rounded = whole.astype(BF16).astype(F32)
    rest = pltpu.roll(whole - rounded, 8, 1)
    total = jnp.where(row % 16 == 14, jnp.where(lane < 8, rounded, rest), total)
    out_ref[...] = jnp.broadcast_to(total.astype(BF16)[None], out_ref.shape)


def expand_body(g_ref, spread_ref, k_ref, b_ref, h_ref, rows_ref):
    rows_ref[...] = g_ref[...].astype(F32).reshape(1024, 128)

    def get(j):
        return rows_ref[pl.ds(j, 64, stride=16), :]

    ends = [get(12), get(13)]
    for c in range(12):
        p, r = c // 2, c % 2
        end = ends[c // 8]
        end = pltpu.roll(end, 128 - 16 * (c % 8), 1) if c % 8 else end
        kept = jnp.concatenate([get(c), end[:, :16]], axis=1).astype(BF16)
        full = jnp.dot(kept, spread_ref[p], preferred_element_type=F32)
        for leaf in range(4):
            k_ref[8 * p + 2 * leaf + r] = full[:, leaf * 128 : leaf * 128 + 81]
    small = get(14)
    small = (small + pltpu.roll(small, 120, 1)).T
    h_ref[...] = small[0:4]
    b_ref[...] = small[4:5]


def call(body, outs, scratch, *args, smem=0, away=(), name):
    def spec(i, away):
        return pl.BlockSpec(memory_space=pl.ANY if i in away else pltpu.VMEM)

    specs = [pl.BlockSpec(memory_space=pltpu.SMEM)] * smem
    return pl.pallas_call(
        body,
        out_shape=outs,
        in_specs=specs + [spec(i, away) for i in range(smem, len(args))],
        out_specs=(pl.BlockSpec(memory_space=pltpu.VMEM),) * len(outs),
        scratch_shapes=scratch,
        compiler_params=PARAMS,
        interpret=INTERPRET,
        name=name,
    )(*args)


def shifted(x, axis, by):
    count = lax.axis_size(axis)
    return lax.ppermute(x, axis, [(i, (i + by) % count) for i in range(count)])


def swapped(x, axis, least):
    count = lax.axis_size(axis)
    pairs = [(i % count, (i + 1) % count) for i in range(least, least + count, 2)]
    return lax.ppermute(x, axis, pairs + [(j, i) for i, j in pairs])


def per_device(gauge_links, pattern, link_parity, conv_weight, conv_bias, head_weight, cotangent):
    shape = jax.ShapeDtypeStruct
    sems = pltpu.SemaphoreType.DMA
    edge = shape((10, 54, 128), BF16)
    links = pltpu.VMEM((5, 2, 3, 3, 24, 128), F32)
    x_edge, z_edge = call(
        send_body, (edge, edge), [links, sems((10,))], gauge_links, away=(0,), name="send"
    )
    next_x = shifted(x_edge, "xy", -1)
    next_z = shifted(z_edge, "gz", -1)
    keep = jnp.asarray(np.concatenate(KEEP), BF16)
    spread = jnp.asarray(SPREAD, BF16)
    weights, small = call(
        weights_body, (shape((12, 128, 256), BF16), shape((64, 8), F32)), [],
        conv_weight.transpose(1, 2, 0), spread, keep, head_weight.T, conv_bias[None], name="weights",
    )
    next_x, next_z, weights, small = lax.optimization_barrier((next_x, next_z, weights, small))
    half = shape((128, 128), BF16)
    odd = (lax.axis_index("xy") % 2).reshape(1)
    z_odd = (lax.axis_index("gz") % 2).reshape(1)
    border = pltpu.VMEM((57 * 24, 128), F32)
    half_one, half_two = call(
        loops_body, (half, half),
        [links, border, border, pltpu.VMEM((14, 24, 128), F32), pltpu.VMEM((2, 136, 128), F32), sems((12,))],
        z_odd, gauge_links, next_x, next_z, smem=1, away=(1,), name="loops",
    )
    block = jnp.stack([swapped(half_one, "gz", 1), half_one, half_two, swapped(half_two, "gz", 0)])
    first = swapped(block, "xy", 1)
    second = swapped(block, "xy", 0)
    x_first = (lax.axis_index("xy") * 2).reshape(1)
    z_first = (lax.axis_index("gz") * 4).reshape(1)
    coefficients, grads = call(
        layer_body, (shape((4, 2, 2, 256), F32), shape((64, 16, 128), BF16)),
        [pltpu.VMEM((12, 256, 1024), BF16), pltpu.VMEM((64, 1024), BF16), pltpu.VMEM((1024, 128), F32)]
        + [pltpu.VMEM((4, n, 128), F32) for n in (104, 136, 72)],
        odd, x_first, z_first, pattern, link_parity, second, block, first, weights, small, keep, cotangent,
        smem=5, name="layer",
    )
    both = ("xy", "gz")
    count = lax.axis_size(both)
    chunks = grads.reshape(count, 1024 // count, 128)
    chunks = lax.all_to_all(chunks, both, 0, 0, tiled=True)
    me = lax.axis_index(both).reshape(1)
    total = jnp.sum(chunks.astype(F32), axis=0)
    chunks = call(total_body, (shape(chunks.shape, BF16),), [], me, total, smem=1, name="total")[0]
    chunks = lax.all_to_all(chunks, both, 0, 0, tiled=True)
    grad_kernel, grad_bias, grad_head = call(
        expand_body, (shape((48, 64, 81), F32), shape((1, 64), F32), shape((4, 64), F32)),
        [pltpu.VMEM((1024, 128), F32)], chunks.reshape(64, 16, 128), spread, name="expand",
    )
    return coefficients, grad_kernel.transpose(2, 0, 1), grad_bias.reshape(64), grad_head.T


def solution(mesh):
    return jax.shard_map(
        per_device,
        mesh=mesh,
        in_specs=(
            P(None, None, None, None, None, "xy", "gz"),
            P(),
            P(),
            P(),
            P(),
            P(),
            P(None, None, "xy", "gz"),
        ),
        out_specs=(P(None, None, "xy", "gz"), P(), P(), P()),
        check_vma=False,
    )
```
